32 devices in a mesh: rep: 4 (over x, core), fsdp: 4 (over z), seq: 2 (over y).
Axes of the slice: x: 2, y: 2, z: 4, core: 2. Of those that a mesh axis runs over, the one named last changes fastest.
Arguments:
- inputs: bfloat16 [2, 16, 1024, 1024], P(None, ('rep', 'fsdp'), 'seq'), may hold values from -6 to 6
- cotangent: bfloat16 [2, 16, 1024, 1024], P(None, ('rep', 'fsdp'), 'seq'), may hold values from -6 to 6
- ln_gain: bfloat16 [6, 1024], P(None, 'fsdp'), may hold values from 0.5 to 1.5
- ln_bias: bfloat16 [6, 1024], P(None, 'fsdp'), may hold values from -1.75 to 1.75
- ffn_in: bfloat16 [2, 1024, 4096], P(None, 'fsdp'), may hold values from -0.1875 to 0.1875
- ffn_in_bias: bfloat16 [2, 4096], P(None, 'fsdp'), may hold values from -3 to 3
- ffn_out: bfloat16 [2, 4096, 1024], P(None, 'fsdp'), may hold values from -0.09375 to 0.09375
- ffn_out_bias: bfloat16 [2, 1024], P(None, 'fsdp'), may hold values from -1.75 to 1.75
- qkv_weight: bfloat16 [1024, 3072], P('fsdp'), may hold values from -0.1875 to 0.1875
- attn_out: bfloat16 [1024, 1024], P('fsdp'), may hold values from -1.5 to 1.5
- attn_bias: bfloat16 [3, 1024], P(None, 'fsdp'), may hold values from -1.75 to 1.75
- dist_embed: bfloat16 [73, 64], P(None, 'fsdp'), may hold values from -6 to 6
- pw_in: bfloat16 [1024, 2048], P('fsdp'), may hold values from -0.1875 to 0.1875
- depthwise: bfloat16 [31, 1024], P(None, 'fsdp'), may hold values from -1 to 1
- pw_out: bfloat16 [1024, 1024], P('fsdp'), may hold values from -0.1875 to 0.1875
Outputs:
- activations: bfloat16 [2, 16, 1024, 1024], P(None, ('rep', 'fsdp'), 'seq')
- input_grad: float32 [2, 16, 1024, 1024], P(None, ('rep', 'fsdp'), 'seq')
- grad_ln_gain: float32 [6, 1024], P(None, 'fsdp')
- grad_ln_bias: float32 [6, 1024], P(None, 'fsdp')
- grad_ffn_in: float32 [2, 1024, 4096], P(None, 'fsdp')
- grad_ffn_in_bias: float32 [2, 4096], P(None, 'fsdp')
- grad_ffn_out: float32 [2, 4096, 1024], P(None, 'fsdp')
- grad_ffn_out_bias: float32 [2, 1024], P(None, 'fsdp')
- grad_qkv_weight: float32 [1024, 3072], P('fsdp')
- grad_attn_out: float32 [1024, 1024], P('fsdp')
- grad_attn_bias: float32 [3, 1024], P(None, 'fsdp')
- grad_dist_embed: float32 [73, 64], P(None, 'fsdp')
- grad_pw_in: float32 [1024, 2048], P('fsdp')
- grad_depthwise: float32 [31, 1024], P(None, 'fsdp')
- grad_pw_out: float32 [1024, 1024], P('fsdp')
The draws below stay inside these ranges and needn't reach their ends.
All inputs are finite; a program needn't handle non-finite values.
Results may differ from the reference program's by a relative error of at most 0.02.
Values may be sent and summed in bfloat16 or wider, within the bound.
No kernel may reach another device: no remote copies, remote signals or barrier semaphores. Data moves between devices by JAX's collectives and lax.ppermute only.
A program may use at most 576 MiB of HBM per device.

```python
import jax
import jax.numpy as jnp
from jax import lax

D = 1024
H = 16
HD = 64
FF = 4096
KERNEL = 31
LEFT = 64
RIGHT = 8
BUCKETS = 73
L = 1024
MB = 2
BATCH = 16


def block_scale(key, shape, split, smallest, high):
    level, own = 1.0, jax.random.fold_in(key, 6)
    for dim, shards_of in split:
        steps = jnp.exp(jax.random.uniform(jax.random.fold_in(own, dim), (shards_of,), jnp.float32, smallest / len(split), high / len(split)))
        level = level * jnp.repeat(steps, shape[dim] // shards_of).reshape([-1 if axis == dim else 1 for axis in range(len(shape))])
    return level


def normal_values(rng, extent, deviation, reach, pieces=(), kind=jnp.bfloat16):
    loudness = block_scale(rng, extent, pieces, -0.22, 0.18) if pieces else 1.0
    array = jax.random.normal(rng, extent, jnp.float32) * deviation * loudness
    return jnp.minimum(jnp.maximum(array, -reach), reach).astype(kind)


def setup_inputs(seed: int = 0) -> dict:
    arg_keys = jax.random.split(jax.random.key(seed), 16)
    return {
        "inputs": normal_values(arg_keys[0], (MB, BATCH, L, D), 1.0, 6.0, ((1, 16), (2, 2))),
        "cotangent": normal_values(arg_keys[1], (MB, BATCH, L, D), 1.0, 6.0, ((1, 16), (2, 2))),
        "ln_gain": jnp.clip(1.0 + 0.1 * jax.random.normal(arg_keys[2], (6, D), jnp.float32), 0.5, 1.5).astype(jnp.bfloat16),
        "ln_bias": normal_values(arg_keys[3], (6, D), 0.3, 1.75, ((1, 4),)),
        "ffn_in": normal_values(arg_keys[4], (2, D, FF), D ** -0.5, 0.1875, ((1, 4),)),
        "ffn_in_bias": normal_values(arg_keys[5], (2, FF), 0.5, 3.0, ((1, 4),)),
        "ffn_out": normal_values(arg_keys[6], (2, FF, D), FF ** -0.5, 0.09375, ((1, 4),)),
        "ffn_out_bias": normal_values(arg_keys[7], (2, D), 0.3, 1.75, ((1, 4),)),
        "qkv_weight": normal_values(arg_keys[8], (D, 3 * D), D ** -0.5, 0.1875, ((0, 4),)),
        "attn_out": normal_values(arg_keys[9], (D, D), (D // 64) ** -0.5, 1.5, ((0, 4),)),
        "attn_bias": normal_values(arg_keys[10], (3, D), 0.3, 1.75, ((1, 4),)),
        "dist_embed": normal_values(arg_keys[11], (BUCKETS, HD), 1.0, 6.0, ((1, 4),)),
        "pw_in": normal_values(arg_keys[12], (D, 2 * D), D ** -0.5, 0.1875, ((0, 4),)),
        "depthwise": normal_values(arg_keys[13], (KERNEL, D), KERNEL ** -0.5, 1.0, ((1, 4),)),
        "pw_out": normal_values(arg_keys[14], (D, D), D ** -0.5, 0.1875, ((0, 4),)),
    }


@jax.custom_vjp
def low(v):
    return lax.optimization_barrier(v.astype(jnp.bfloat16)).astype(jnp.float32)

@jax.custom_vjp
def low_back(v):
    return v

def low_keep(v):
    return (low(v), None)

def low_pass(kept, grad):
    return (grad,)

def back_keep(v):
    return (v, None)

def back_low(kept, grad):
    return (low(grad),)
low.defvjp(low_keep, low_pass)
low_back.defvjp(back_keep, back_low)
EPS = 1e-05
TOP_PRECISION = lax.Precision.HIGHEST

def layer_norm(values, gain, shift):
    mean = lax.optimization_barrier(jnp.mean(values, axis=-1, keepdims=True))
    centred = values - mean
    var = lax.optimization_barrier(jnp.mean(centred * centred, axis=-1, keepdims=True))
    return centred * lax.rsqrt(var + EPS) * gain + shift

def product(left, right):
    return jnp.dot(left, right, precision=TOP_PRECISION)

def feed_forward(values, gain, shift, w_in, b_in, w_out, b_out):
    normed = low(layer_norm(values, gain, shift))
    pre = low_back(product(normed, w_in)) + b_in
    active = low(jax.nn.silu(pre))
    return low_back(product(active, w_out)) + b_out

def attention(values, gain, shift, w_qkv, bias, embed, w_o):
    normed = low(layer_norm(values, gain, shift))
    proj = low_back(product(normed, w_qkv))
    query_rows = low(proj[:, :D] + bias[0]).reshape(L, H, HD)
    key = low(proj[:, D:2 * D]).reshape(L, H, HD)
    value_rows = low(proj[:, 2 * D:] + bias[1]).reshape(L, H, HD)
    rel = low(low_back(jnp.einsum('nhd,bd->hnb', query_rows, embed, precision=TOP_PRECISION)))
    place = jnp.arange(L, dtype=jnp.int32)
    bucket = (jnp.clip(place[None, :] - place[:, None], -LEFT, RIGHT) + LEFT).astype(jnp.int32)
    placed = jnp.take_along_axis(rel, jnp.broadcast_to(bucket[None], (H, L, L)), axis=2)
    direct_path = jnp.einsum('uok,yok->ouy', query_rows, key, precision=TOP_PRECISION)
    scores = low_back((direct_path + placed) * HD ** (-0.5))
    attention_probability = low(jax.nn.softmax(scores, axis=-1))
    mixed_precision = low(low_back(jnp.einsum('oiq,qog->iog', attention_probability, value_rows, precision=TOP_PRECISION)))
    return low_back(product(mixed_precision.reshape(L, D), w_o)) + bias[2]

def convolution(values, gain, shift, w_in, kernel, gain_two, shift_two, w_out):
    normed = low(layer_norm(values, gain, shift))
    pre = low_back(product(normed, w_in))
    gated = low(pre[:, :D] * jax.nn.sigmoid(pre[:, D:]))
    padded = jnp.pad(gated, ((KERNEL - 1, 0), (0, 0)))
    total = kernel[0] * padded[0:L]
    for tap in range(1, KERNEL):
        total = total + kernel[tap] * padded[tap:tap + L]
    mixed_precision = low(jax.nn.silu(layer_norm(total, gain_two, shift_two)))
    return low_back(product(mixed_precision, w_out))

def layer(params, values):
    gains, shifts, f_in, f_in_b, f_out, f_out_b, w_qkv, w_o, a_bias, embed, c_in, kernel, c_out = params
    first = values + 0.5 * feed_forward(values, gains[0], shifts[0], f_in[0], f_in_b[0], f_out[0], f_out_b[0])
    second = first + attention(first, gains[1], shifts[1], w_qkv, a_bias, embed, w_o)
    third = second + convolution(second, gains[2], shifts[2], c_in, kernel, gains[3], shifts[3], c_out)
    fourth = third + 0.5 * feed_forward(third, gains[4], shifts[4], f_in[1], f_in_b[1], f_out[1], f_out_b[1])
    return layer_norm(fourth, gains[5], shifts[5])

def reference(inputs, cotangent, ln_gain, ln_bias, ffn_in, ffn_in_bias, ffn_out, ffn_out_bias, qkv_weight, attn_out, attn_bias, dist_embed, pw_in, depthwise, pw_out):
    params = tuple((w.astype(jnp.float32) for w in (ln_gain, ln_bias, ffn_in, ffn_in_bias, ffn_out, ffn_out_bias, qkv_weight, attn_out, attn_bias, dist_embed, pw_in, depthwise, pw_out)))
    clips_in = inputs.astype(jnp.float32).reshape(MB * BATCH, L, D)
    clips_cot = cotangent.astype(jnp.float32).reshape(MB * BATCH, L, D)

    def step(totals, item):
        values, grad_out = item
        out, pull = jax.vjp(layer, params, values)
        grad_params, grad_values = pull(grad_out)
        totals = jax.tree.map(jnp.add, totals, grad_params)
        return (totals, (out.astype(jnp.bfloat16), grad_values))
    zeros = jax.tree.map(jnp.zeros_like, params)
    totals, (outs, grads) = lax.scan(step, zeros, (clips_in, clips_cot))
    return (outs.reshape(MB, BATCH, L, D), grads.reshape(MB, BATCH, L, D), totals[0], totals[1], totals[2], totals[3], totals[4], totals[5], totals[6], totals[7], totals[8], totals[9], totals[10], totals[11], totals[12])
```

```python
import functools

import jax
import jax.numpy as jnp
from jax import lax
from jax.experimental import pallas as pl
from jax.experimental.pallas import tpu as pltpu
from jax.sharding import PartitionSpec as P

H = 16
HD = 64
KERNEL = 31
LEFT = 64
RIGHT = 8


EPS = 1e-05
LOW = jnp.bfloat16
HIGH = jnp.float32


def from_behind(value, axis, steps):
    count = lax.axis_size(axis)
    first, last = (max(0, -steps), min(count, count - steps))
    return lax.ppermute(value, axis, [(source, source + steps) for source in range(first, last)])


def as_sent(array):
    return jax.tree.map(lambda a: a.astype(jnp.bfloat16) if a.dtype == jnp.float32 else a, array)


def layer_norm(values, gain, shift):
    mean = jnp.mean(values, axis=-1, keepdims=True)
    centred = values - mean
    var = jnp.mean(centred * centred, axis=-1, keepdims=True)
    return centred * lax.rsqrt(var + EPS) * gain + shift


def matmul(left, right):
    return jnp.dot(left, right, preferred_element_type=HIGH)


def left_t(left, right):
    return lax.dot_general(left, right, (((0,), (0,)), ((), ())), preferred_element_type=HIGH)


def right_t(left, right):
    return lax.dot_general(left, right, (((1,), (1,)), ((), ())), preferred_element_type=HIGH)


def fetch(shards):
    return (
        lax.all_gather(shards[0], "fsdp", axis=1, tiled=True),
        lax.all_gather(shards[1], "fsdp", axis=1, tiled=True),
        lax.all_gather(shards[2], "fsdp", axis=1, tiled=True),
        lax.all_gather(shards[3], "fsdp", axis=1, tiled=True),
        lax.all_gather(shards[4], "fsdp", axis=1, tiled=True),
        lax.all_gather(shards[5], "fsdp", axis=1, tiled=True),
        lax.all_gather(shards[6], "fsdp", axis=0, tiled=True),
        lax.all_gather(shards[7], "fsdp", axis=0, tiled=True),
        lax.all_gather(shards[8], "fsdp", axis=1, tiled=True),
        lax.all_gather(shards[9], "fsdp", axis=1, tiled=True),
        lax.all_gather(shards[10], "fsdp", axis=0, tiled=True),
        lax.all_gather(shards[11], "fsdp", axis=1, tiled=True),
        lax.all_gather(shards[12], "fsdp", axis=0, tiled=True),
    )


def unpack(whole):
    gains, shifts, f_in, f_in_b, f_out, f_out_b, w_qkv, w_o, a_bias, embed, c_in, kernel, c_out = (
        whole
    )
    return (
        gains.astype(HIGH),
        shifts.astype(HIGH),
        f_in,
        f_in_b.astype(HIGH),
        f_out,
        f_out_b.astype(HIGH),
        w_qkv,
        w_o,
        a_bias.astype(HIGH),
        embed,
        c_in,
        kernel.astype(HIGH),
        c_out,
    )


def ffn_forward(values, gain, shift, w_in, b_in, w_out, b_out):
    normed, norm_pull = jax.vjp(layer_norm, values, gain, shift)
    normed_low = normed.astype(LOW)
    linear = matmul(normed_low, w_in)
    active, act_pull = jax.vjp(lambda lin, bias: jax.nn.silu(lin + bias), linear, b_in)
    active_low = active.astype(LOW)
    out = matmul(active_low, w_out) + b_out
    return (out, (norm_pull, normed_low, act_pull, active_low))


def ffn_backward(grad, kept, w_in, w_out):
    norm_pull, normed_low, act_pull, active_low = kept
    grad_b_out = jnp.sum(grad, axis=0)
    grad_low = grad.astype(LOW)
    grad_w_out = left_t(active_low, grad_low)
    grad_active = right_t(grad_low, w_out)
    grad_lin, grad_b_in = act_pull(grad_active)
    lin_low = grad_lin.astype(LOW)
    grad_w_in = left_t(normed_low, lin_low)
    grad_normed = right_t(lin_low, w_in)
    grad_values, grad_gain, grad_shift = norm_pull(grad_normed)
    return (grad_values, (grad_gain, grad_shift, grad_w_in, grad_b_in, grad_w_out, grad_b_out))


def scores_of(query4, key4, embed, onehot):
    direct_path = jnp.einsum("cnhd,clhd->chnl", query4, key4, preferred_element_type=HIGH)
    rel_low = jnp.einsum("cnhd,bd->chnb", query4, embed, preferred_element_type=HIGH).astype(LOW)
    placed = jnp.einsum("chnb,nbl->chnl", rel_low, onehot, preferred_element_type=HIGH)
    return (direct_path + placed) * HD ** (-0.5)


def attn_forward(values, gain, shift, w_qkv, bias, embed, w_o, onehot):
    clips, rows, width = values.shape
    normed, norm_pull = jax.vjp(layer_norm, values, gain, shift)
    normed_low = normed.astype(LOW).reshape(clips * rows, width)
    proj = matmul(normed_low, w_qkv).reshape(clips, rows, 3 * width)
    query_rows = (proj[..., :width] + bias[0]).astype(LOW)
    key = proj[..., width : 2 * width].astype(LOW)
    value_rows = (proj[..., 2 * width :] + bias[1]).astype(LOW)
    keys, values_all = (
        lax.all_gather(key, "seq", axis=1, tiled=True),
        lax.all_gather(value_rows, "seq", axis=1, tiled=True),
    )
    span = keys.shape[1]
    query4 = query_rows.reshape(clips, rows, H, HD)
    key4 = keys.reshape(clips, span, H, HD)
    value4 = values_all.reshape(clips, span, H, HD)
    scores = scores_of(query4, key4, embed, onehot)
    total_log = jax.nn.logsumexp(scores, axis=-1)
    prob_low = jnp.exp(scores - total_log[..., None]).astype(LOW)
    mixed_precision = jnp.einsum("chnl,clhd->cnhd", prob_low, value4, preferred_element_type=HIGH)
    mixed_low = mixed_precision.astype(LOW).reshape(clips * rows, width)
    out = matmul(mixed_low, w_o) + bias[2]
    return (out, (norm_pull, normed_low, query4, key4, value4, total_log, mixed_low))


def attn_backward(grad, kept, w_qkv, w_o, embed, onehot):
    norm_pull, normed_low, query4, key4, value4, total_log, mixed_low = kept
    clips, rows = (query4.shape[0], query4.shape[1])
    span = key4.shape[1]
    width = H * HD
    scale = HD ** (-0.5)
    grad_b_o = jnp.sum(grad, axis=0)
    grad_low = grad.astype(LOW)
    grad_w_o = left_t(mixed_low, grad_low)
    grad_mixed = right_t(grad_low, w_o).astype(LOW).reshape(clips, rows, H, HD)
    scores = scores_of(query4, key4, embed, onehot)
    attention_probability = jnp.exp(scores - total_log[..., None])
    prob_low = attention_probability.astype(LOW)
    grad_prob = jnp.einsum("cnhd,clhd->chnl", grad_mixed, value4, preferred_element_type=HIGH)
    grad_value = jnp.einsum("chnl,cnhd->clhd", prob_low, grad_mixed, preferred_element_type=HIGH)
    grad_scores = (
        attention_probability
        * (grad_prob - jnp.sum(attention_probability * grad_prob, axis=-1, keepdims=True))
    ).astype(LOW)
    grad_rel = (
        jnp.einsum("chnl,nbl->chnb", grad_scores, onehot, preferred_element_type=HIGH) * scale
    ).astype(LOW)
    grad_query = scale * jnp.einsum(
        "chnl,clhd->cnhd", grad_scores, key4, preferred_element_type=HIGH
    )
    grad_query = grad_query + jnp.einsum(
        "chnb,bd->cnhd", grad_rel, embed, preferred_element_type=HIGH
    )
    grad_embed = jnp.einsum("chnb,cnhd->bd", grad_rel, query4, preferred_element_type=HIGH)
    grad_key = scale * jnp.einsum(
        "chnl,cnhd->clhd", grad_scores, query4, preferred_element_type=HIGH
    )
    mine_key, mine_value = (
        lax.psum_scatter(
            grad_key.reshape(clips, span, width).astype(jnp.bfloat16),
            "seq",
            scatter_dimension=1,
            tiled=True,
        ).astype(jnp.float32),
        lax.psum_scatter(
            grad_value.reshape(clips, span, width).astype(jnp.bfloat16),
            "seq",
            scatter_dimension=1,
            tiled=True,
        ).astype(jnp.float32),
    )
    grad_query = grad_query.reshape(clips, rows, width)
    grad_b_q = jnp.sum(grad_query, axis=(0, 1))
    grad_b_v = jnp.sum(mine_value, axis=(0, 1))
    grad_proj = (
        jnp.concatenate([grad_query, mine_key, mine_value], axis=-1)
        .astype(LOW)
        .reshape(clips * rows, 3 * width)
    )
    grad_w_qkv = left_t(normed_low, grad_proj)
    grad_normed = right_t(grad_proj, w_qkv).reshape(clips, rows, width)
    grad_values, grad_gain, grad_shift = norm_pull(grad_normed)
    grad_bias = jnp.stack([grad_b_q, grad_b_v, grad_b_o])
    return (
        grad_values.reshape(clips * rows, width),
        (grad_gain, grad_shift, grad_w_qkv, grad_bias, grad_embed, grad_w_o),
    )


def depthwise_block(extended, kernel, gain, shift):
    taps = kernel.shape[0]
    span = extended.shape[1] - taps + 1
    total = kernel[0] * extended[:, 0:span, :]
    for tap in range(1, taps):
        total = total + kernel[tap] * extended[:, tap : tap + span, :]
    return jax.nn.silu(layer_norm(total, gain, shift))


def conv_forward(values, gain, shift, w_in, kernel, gain_two, shift_two, w_out):
    clips, rows, width = values.shape
    normed, norm_pull = jax.vjp(layer_norm, values, gain, shift)
    normed_low = normed.astype(LOW).reshape(clips * rows, width)
    pre = matmul(normed_low, w_in).reshape(clips, rows, 2 * width)
    gated, gate_pull = jax.vjp(
        lambda both: both[..., :width] * jax.nn.sigmoid(both[..., width:]), pre
    )
    gated_low = gated.astype(LOW)
    rim = from_behind(gated_low[:, rows - (KERNEL - 1) :, :], "seq", 1)
    extended = jnp.concatenate([rim, gated_low], axis=1).astype(HIGH)
    mixed_precision, mix_pull = jax.vjp(depthwise_block, extended, kernel, gain_two, shift_two)
    mixed_low = mixed_precision.astype(LOW).reshape(clips * rows, width)
    out = matmul(mixed_low, w_out)
    return (out, (norm_pull, normed_low, gate_pull, mix_pull, mixed_low))


def conv_backward(grad, kept, w_in, w_out, clips, rows):
    norm_pull, normed_low, gate_pull, mix_pull, mixed_low = kept
    width = grad.shape[1]
    grad_low = grad.astype(LOW)
    grad_w_out = left_t(mixed_low, grad_low)
    grad_mixed = right_t(grad_low, w_out).reshape(clips, rows, width)
    grad_ext, grad_kernel, grad_gain_two, grad_shift_two = mix_pull(grad_mixed)
    returned = from_behind(grad_ext[:, : KERNEL - 1, :].astype(jnp.bfloat16), "seq", -1).astype(
        jnp.float32
    )
    grad_gated = grad_ext[:, KERNEL - 1 :, :] + jnp.pad(
        returned, ((0, 0), (rows - (KERNEL - 1), 0), (0, 0))
    )
    (grad_pre,) = gate_pull(grad_gated)
    pre_low = grad_pre.astype(LOW).reshape(clips * rows, 2 * width)
    grad_w_in = left_t(normed_low, pre_low)
    grad_normed = right_t(pre_low, w_in).reshape(clips, rows, width)
    grad_values, grad_gain, grad_shift = norm_pull(grad_normed)
    return (
        grad_values.reshape(clips * rows, width),
        (grad_gain, grad_shift, grad_w_in, grad_kernel, grad_gain_two, grad_shift_two, grad_w_out),
    )


def general_body(
    inputs,
    cotangent,
    ln_gain,
    ln_bias,
    ffn_in,
    ffn_in_bias,
    ffn_out,
    ffn_out_bias,
    qkv_weight,
    attn_out,
    attn_bias,
    dist_embed,
    pw_in,
    depthwise,
    pw_out,
):
    shards = (
        ln_gain,
        ln_bias,
        ffn_in,
        ffn_in_bias,
        ffn_out,
        ffn_out_bias,
        qkv_weight,
        attn_out,
        attn_bias,
        dist_embed,
        pw_in,
        depthwise,
        pw_out,
    )
    micro, clips, rows, width = inputs.shape
    span = rows * lax.axis_size("seq")
    positions = lax.axis_index("seq") * rows + jnp.arange(rows, dtype=jnp.int32)
    bucket = (
        jnp.clip(jnp.arange(span, dtype=jnp.int32)[None, :] - positions[:, None], -LEFT, RIGHT)
        + LEFT
    )
    onehot = (
        bucket[:, None, :] == jnp.arange(LEFT + RIGHT + 1, dtype=jnp.int32)[None, :, None]
    ).astype(LOW)
    outputs = []
    input_grads = []
    totals = None
    for step in range(micro):
        whole = fetch(shards)
        (
            gains,
            shifts,
            f_in,
            f_in_b,
            f_out,
            f_out_b,
            w_qkv,
            w_o,
            a_bias,
            embed,
            c_in,
            kernel,
            c_out,
        ) = unpack(whole)
        start_rows = inputs[step].astype(HIGH).reshape(clips * rows, width)
        branch_one, keep_one = ffn_forward(
            start_rows, gains[0], shifts[0], f_in[0], f_in_b[0], f_out[0], f_out_b[0]
        )
        first = start_rows + 0.5 * branch_one
        branch_two, keep_two = attn_forward(
            first.reshape(clips, rows, width),
            gains[1],
            shifts[1],
            w_qkv,
            a_bias,
            embed,
            w_o,
            onehot,
        )
        second = first + branch_two
        branch_three, keep_three = conv_forward(
            second.reshape(clips, rows, width),
            gains[2],
            shifts[2],
            c_in,
            kernel,
            gains[3],
            shifts[3],
            c_out,
        )
        third = second + branch_three
        branch_four, keep_four = ffn_forward(
            third, gains[4], shifts[4], f_in[1], f_in_b[1], f_out[1], f_out_b[1]
        )
        fourth = third + 0.5 * branch_four
        final, final_pull = jax.vjp(layer_norm, fourth, gains[5], shifts[5])
        outputs.append(final.astype(LOW).reshape(clips, rows, width))
        again = (
            lax.all_gather(shards[0], "fsdp", axis=1, tiled=True),
            lax.all_gather(shards[1], "fsdp", axis=1, tiled=True),
            lax.all_gather(shards[2], "fsdp", axis=1, tiled=True),
            lax.all_gather(shards[3], "fsdp", axis=1, tiled=True),
            lax.all_gather(shards[4], "fsdp", axis=1, tiled=True),
            lax.all_gather(shards[5], "fsdp", axis=1, tiled=True),
            lax.all_gather(shards[6], "fsdp", axis=0, tiled=True),
            lax.all_gather(shards[7], "fsdp", axis=0, tiled=True),
            lax.all_gather(shards[8], "fsdp", axis=1, tiled=True),
            lax.all_gather(shards[9], "fsdp", axis=1, tiled=True),
            lax.all_gather(shards[10], "fsdp", axis=0, tiled=True),
            lax.all_gather(shards[11], "fsdp", axis=1, tiled=True),
            lax.all_gather(shards[12], "fsdp", axis=0, tiled=True),
        )
        (
            gains,
            shifts,
            f_in,
            f_in_b,
            f_out,
            f_out_b,
            w_qkv,
            w_o,
            a_bias,
            embed,
            c_in,
            kernel,
            c_out,
        ) = unpack(again)
        grad_fourth, gain_five, shift_five = final_pull(
            cotangent[step].astype(HIGH).reshape(clips * rows, width)
        )
        grad_inner, four_grads = ffn_backward(0.5 * grad_fourth, keep_four, f_in[1], f_out[1])
        grad_third = grad_fourth + grad_inner
        grad_inner, three_grads = conv_backward(grad_third, keep_three, c_in, c_out, clips, rows)
        grad_second = grad_third + grad_inner
        grad_inner, two_grads = attn_backward(grad_second, keep_two, w_qkv, w_o, embed, onehot)
        grad_first = grad_second + grad_inner
        grad_inner, one_grads = ffn_backward(0.5 * grad_first, keep_one, f_in[0], f_out[0])
        input_grads.append((grad_first + grad_inner).reshape(clips, rows, width))
        grads = (
            jnp.stack(
                [
                    one_grads[0],
                    two_grads[0],
                    three_grads[0],
                    three_grads[4],
                    four_grads[0],
                    gain_five,
                ]
            ),
            jnp.stack(
                [
                    one_grads[1],
                    two_grads[1],
                    three_grads[1],
                    three_grads[5],
                    four_grads[1],
                    shift_five,
                ]
            ),
            jnp.stack([one_grads[2], four_grads[2]]),
            jnp.stack([one_grads[3], four_grads[3]]),
            jnp.stack([one_grads[4], four_grads[4]]),
            jnp.stack([one_grads[5], four_grads[5]]),
            two_grads[2],
            two_grads[5],
            two_grads[3],
            two_grads[4],
            three_grads[2],
            three_grads[3],
            three_grads[6],
        )
        totals = grads if totals is None else jax.tree.map(jnp.add, totals, grads)
    totals = (
        lax.psum_scatter(
            totals[0].astype(jnp.bfloat16), "fsdp", scatter_dimension=1, tiled=True
        ).astype(jnp.float32),
        lax.psum_scatter(
            totals[1].astype(jnp.bfloat16), "fsdp", scatter_dimension=1, tiled=True
        ).astype(jnp.float32),
        lax.psum_scatter(
            totals[2].astype(jnp.bfloat16), "fsdp", scatter_dimension=1, tiled=True
        ).astype(jnp.float32),
        lax.psum_scatter(
            totals[3].astype(jnp.bfloat16), "fsdp", scatter_dimension=1, tiled=True
        ).astype(jnp.float32),
        lax.psum_scatter(
            totals[4].astype(jnp.bfloat16), "fsdp", scatter_dimension=1, tiled=True
        ).astype(jnp.float32),
        lax.psum_scatter(
            totals[5].astype(jnp.bfloat16), "fsdp", scatter_dimension=1, tiled=True
        ).astype(jnp.float32),
        lax.psum_scatter(
            totals[6].astype(jnp.bfloat16), "fsdp", scatter_dimension=0, tiled=True
        ).astype(jnp.float32),
        lax.psum_scatter(
            totals[7].astype(jnp.bfloat16), "fsdp", scatter_dimension=0, tiled=True
        ).astype(jnp.float32),
        lax.psum_scatter(
            totals[8].astype(jnp.bfloat16), "fsdp", scatter_dimension=1, tiled=True
        ).astype(jnp.float32),
        lax.psum_scatter(
            totals[9].astype(jnp.bfloat16), "fsdp", scatter_dimension=1, tiled=True
        ).astype(jnp.float32),
        lax.psum_scatter(
            totals[10].astype(jnp.bfloat16), "fsdp", scatter_dimension=0, tiled=True
        ).astype(jnp.float32),
        lax.psum_scatter(
            totals[11].astype(jnp.bfloat16), "fsdp", scatter_dimension=1, tiled=True
        ).astype(jnp.float32),
        lax.psum_scatter(
            totals[12].astype(jnp.bfloat16), "fsdp", scatter_dimension=0, tiled=True
        ).astype(jnp.float32),
    )
    summed = jax.tree.map(
        lambda part: part.astype(jnp.float32), lax.psum(as_sent(totals), ("rep", "seq"))
    )
    return (
        jnp.stack(outputs),
        jnp.stack(input_grads),
        summed[0],
        summed[1],
        summed[2],
        summed[3],
        summed[4],
        summed[5],
        summed[6],
        summed[7],
        summed[8],
        summed[9],
        summed[10],
        summed[11],
        summed[12],
    )


SUB = 128
PAD = 128
FWD_ROWS = 512
BWD_ROWS = 1024


def dot(a, b):
    return lax.dot_general(a, b, (((1,), (0,)), ((), ())), preferred_element_type=HIGH)


def dot_nt(a, b):
    return lax.dot_general(a, b, (((1,), (1,)), ((), ())), preferred_element_type=HIGH)


def biased_scores(qs, table, kcat, s_ref, first, span):
    count = qs.shape[0]
    rel = dot_nt(qs, table).astype(LOW).astype(HIGH)
    lane = lax.broadcasted_iota(jnp.int32, (count, 128), 1)
    block = first + lax.broadcasted_iota(jnp.int32, (count, 128), 0) // SUB
    far = jnp.where(lane < block - 1, rel[:, 384:512], jnp.where(lane > block + 1, rel[:, 128:256], 0.0))
    s_ref[:, PAD : PAD + span] = dot_nt(jnp.concatenate([qs, far.astype(LOW)], axis=1), kcat)
    for sub in range(count // SUB):
        rows = slice(sub * SUB, (sub + 1) * SUB)
        band = pltpu.roll(rel[rows], LEFT, 1, stride=1, stride_axis=0)
        at = pl.multiple_of((first + sub) * SUB, 128)
        s_ref[rows, pl.ds(at, 384)] += band[:, :384]


def blocks_onehot(span):
    row = lax.broadcasted_iota(jnp.int32, (span, 128), 0)
    lane = lax.broadcasted_iota(jnp.int32, (span, 128), 1)
    return (row // SUB == lane).astype(HIGH).astype(LOW)


def attn_fwd_kernel(q_ref, k_ref, v_ref, table_ref, o_ref, lse_ref, kcat, vcat, s_ref):
    span = k_ref.shape[0]
    kcat[:, :128] = k_ref[...]
    kcat[:, 128:] = blocks_onehot(span)
    vcat[:, :128] = v_ref[...]
    vcat[:, 128:] = jnp.ones((span, 128), LOW)
    lane = lax.broadcasted_iota(jnp.int32, (FWD_ROWS, 128), 1)

    def body(qb, carry):
        rows = pl.ds(pl.multiple_of(qb * FWD_ROWS, FWD_ROWS), FWD_ROWS)
        q = q_ref[rows, :].astype(HIGH) * (HD**-0.5)
        outs, logs = [], []
        for h in range(2):
            mine = (lane < HD) if h == 0 else (lane >= HD)
            qs = jnp.where(mine, q, 0.0).astype(LOW)
            sr = s_ref.at[h]
            biased_scores(qs, table_ref[...], kcat[...], sr, qb * (FWD_ROWS // SUB), span)
        for h in range(2):
            s = s_ref[h, :, PAD : PAD + span]
            top = jnp.max(s, axis=-1, keepdims=True)
            p = jnp.exp(s - top).astype(LOW)
            mixed = dot(p, vcat[...])
            total = mixed[:, 128:]
            outs.append(mixed[:, :128] / total)
            logs.append(top + jnp.log(total))
        o_ref[rows, :] = jnp.where(lane < HD, outs[0], outs[1]).astype(o_ref.dtype)
        lse_ref[rows, :] = jnp.where(lane < HD, logs[0], logs[1])
        return carry

    lax.fori_loop(0, q_ref.shape[0] // FWD_ROWS, body, 0)


def attn_forward_call(proj, table, width):
    rows = proj.shape[0]
    pairs = width // 128
    col = lambda off: pl.BlockSpec((rows, 128), lambda h: (0, off * pairs + h))
    return pl.pallas_call(
        attn_fwd_kernel,
        grid=(pairs,),
        in_specs=[col(0), col(1), col(2), pl.BlockSpec((512, 128), lambda h: (0, 0))],
        out_specs=[pl.BlockSpec((rows, 128), lambda h: (0, h))] * 2,
        out_shape=[jax.ShapeDtypeStruct((rows, width), LOW), jax.ShapeDtypeStruct((rows, width), HIGH)],
        scratch_shapes=[
            pltpu.VMEM((rows, 256), LOW),
            pltpu.VMEM((rows, 256), LOW),
            pltpu.VMEM((2, FWD_ROWS, rows + 2 * PAD), HIGH),
        ],
        compiler_params=pltpu.CompilerParams(vmem_limit_bytes=40 * 1024 * 1024),
        cost_estimate=pl.CostEstimate(
            flops=16 * rows * rows * width, bytes_accessed=12 * rows * width, transcendentals=rows * rows * 16
        ),
    )(proj, proj, proj, table)


def attn_bwd_kernel(q_ref, k_ref, v_ref, o_ref, lse_ref, do_ref, table_ref, embed_ref,
                    g_ref, dembed_ref, bias_ref, kcat, qt, dot_t, dkt, dvt, s_ref):
    span = k_ref.shape[0]
    count = BWD_ROWS
    kcat[:, :128] = k_ref[...]
    kcat[:, 128:] = blocks_onehot(span)
    qt[...] = (q_ref[...].astype(HIGH) * (HD**-0.5)).T.astype(LOW)
    dot_t[...] = do_ref[...].astype(HIGH).T.astype(LOW)
    dkt[...] = jnp.zeros_like(dkt)
    dvt[...] = jnp.zeros_like(dvt)
    lane = lax.broadcasted_iota(jnp.int32, (count, 128), 1)
    block_of = lax.broadcasted_iota(jnp.int32, (count, 128), 0) // SUB
    column = lax.broadcasted_iota(jnp.int32, (SUB, 384), 1)
    last = q_ref.shape[0] // SUB - 1
    turn = lax.broadcasted_iota(jnp.int32, (SUB, SUB), 0) + lax.broadcasted_iota(jnp.int32, (SUB, SUB), 1)
    flip = (turn == SUB - 1).astype(HIGH).astype(LOW)
    lane_sub = lax.broadcasted_iota(jnp.int32, (SUB, 128), 1)
    edge = LEFT + RIGHT

    def body(qb, carry):
        dembed, dbias = carry
        first = qb * (count // SUB)
        rows = pl.ds(pl.multiple_of(qb * count, count), count)
        q = q_ref[rows, :].astype(HIGH) * (HD**-0.5)
        grad = do_ref[rows, :].astype(HIGH)
        lse2 = lse_ref[rows, :]
        weighted = grad * o_ref[rows, :].astype(HIGH)
        block = first + block_of
        dqs, news = [], []
        for h in range(2):
            mine = (lane < HD) if h == 0 else (lane >= HD)
            qs = jnp.where(mine, q, 0.0).astype(LOW)
            biased_scores(qs, table_ref[...], kcat[...], s_ref.at[h], first, span)
        for h in range(2):
            mine = (lane < HD) if h == 0 else (lane >= HD)
            part = slice(h * HD, (h + 1) * HD)
            sr = s_ref.at[h]
            lse = lse2[:, h * HD : h * HD + 1]
            p = jnp.exp(sr[:, PAD : PAD + span] - lse)
            delta = jnp.sum(jnp.where(mine, weighted, 0.0), axis=-1, keepdims=True)
            gs = jnp.where(mine, grad, 0.0).astype(LOW)
            ds = p * (dot_nt(gs, v_ref[...]) - delta)
            sr[:, PAD : PAD + span] = ds
            ds_low = ds.astype(LOW)
            dq = dot(ds_low, kcat[...])
            dvt[part, :] += dot(dot_t[part, rows], p.astype(LOW))
            dkt[part, :] += dot(qt[part, rows], ds_low)
            tables = []
            for sub in range(count // SUB):
                band = sr[sub * SUB : (sub + 1) * SUB, pl.ds(pl.multiple_of((first + sub) * SUB, 128), 384)]
                if sub == 0:
                    band = jnp.where((column < 128) & (first == 0), 0.0, band)
                if sub == count // SUB - 1:
                    band = jnp.where((column >= 256) & (first + sub == last), 0.0, band)
                turned = dot(flip, band.astype(LOW))
                turned = jnp.concatenate([turned, jnp.zeros((SUB, 128), HIGH)], axis=1)
                drel = pltpu.roll(turned, 512 - LEFT - SUB + 1, 1, stride=1, stride_axis=0)
                near, middle = drel[:, :128], drel[:, 256:384]
                left = jnp.sum(drel[:, 384:512] + jnp.where(lane_sub >= 64, middle, 0.0), axis=-1, keepdims=True)
                right = jnp.sum(
                    drel[:, 128:256] + jnp.where(lane_sub < 64, middle, 0.0) + jnp.where(lane_sub >= edge, near, 0.0),
                    axis=-1,
                    keepdims=True,
                )
                left_top, right_top = left.astype(LOW).astype(HIGH), right.astype(LOW).astype(HIGH)
                packed = jnp.where(lane_sub < edge, near, 0.0)
                for at, value in ((80, left_top), (81, left - left_top), (82, right_top), (83, right - right_top)):
                    packed = jnp.where(lane_sub == at, value, packed)
                tables.append(dot(flip, packed.astype(LOW)))
            table = jnp.concatenate(tables, axis=0)
            sums = dq[:, 128:]
            left = jnp.sum(jnp.where(lane < block - 1, sums, 0.0) + jnp.where((lane == 80) | (lane == 81), table, 0.0), axis=-1, keepdims=True)
            right = jnp.sum(jnp.where(lane > block + 1, sums, 0.0) + jnp.where((lane == 82) | (lane == 83), table, 0.0), axis=-1, keepdims=True)
            drl = jnp.where(lane < edge, table, 0.0) + jnp.where(lane == 0, left, 0.0) + jnp.where(lane == edge, right, 0.0)
            drl = drl.astype(LOW)
            dqs.append((dq[:, :128] + dot(drl, embed_ref[...])) * (HD**-0.5))
            news.append(dembed[part] + dot(qt[part, rows], drl))
        dq = jnp.where(lane < HD, dqs[0], dqs[1])
        g_ref[0, rows, :] = dq.astype(LOW)
        return (jnp.concatenate(news, axis=0), dbias + jnp.sum(dq, axis=0, keepdims=True))

    start = (jnp.zeros((128, 128), HIGH), jnp.zeros((1, 128), HIGH))
    dembed, dbias = lax.fori_loop(0, q_ref.shape[0] // count, body, start)
    dembed_ref[...] = dembed
    g_ref[1, :, :] = dkt[...].T.astype(LOW)
    dv = dvt[...].T
    g_ref[2, :, :] = dv.astype(LOW)
    row8 = lax.broadcasted_iota(jnp.int32, (8, 128), 0)
    bias_ref[...] = jnp.where(row8 == 0, dbias, jnp.where(row8 == 1, jnp.sum(dv, axis=0, keepdims=True), 0.0))


def attn_backward_call(proj, mixed, lse, grad_mixed, table, embed2, width):
    rows = proj.shape[0]
    pairs = width // 128
    col = lambda off: pl.BlockSpec((rows, 128), lambda h: (0, off * pairs + h))
    return pl.pallas_call(
        attn_bwd_kernel,
        grid=(pairs,),
        in_specs=[
            col(0), col(1), col(2), col(0), col(0), col(0),
            pl.BlockSpec((512, 128), lambda h: (0, 0)),
            pl.BlockSpec((128, 128), lambda h: (0, 0)),
        ],
        out_specs=[
            pl.BlockSpec((3, rows, 128), lambda h: (0, 0, h)),
            pl.BlockSpec((128, 128), lambda h: (0, h)),
            pl.BlockSpec((8, 128), lambda h: (0, h)),
        ],
        out_shape=[
            jax.ShapeDtypeStruct((3, rows, width), LOW),
            jax.ShapeDtypeStruct((128, width), HIGH),
            jax.ShapeDtypeStruct((8, width), HIGH),
        ],
        scratch_shapes=[
            pltpu.VMEM((rows, 256), LOW),
            pltpu.VMEM((128, rows), LOW),
            pltpu.VMEM((128, rows), LOW),
            pltpu.VMEM((128, rows), HIGH),
            pltpu.VMEM((128, rows), HIGH),
            pltpu.VMEM((2, BWD_ROWS, rows + 2 * PAD), HIGH),
        ],
        compiler_params=pltpu.CompilerParams(vmem_limit_bytes=48 * 1024 * 1024),
        cost_estimate=pl.CostEstimate(
            flops=40 * rows * rows * width, bytes_accessed=24 * rows * width, transcendentals=rows * rows * 16
        ),
    )(proj, proj, proj, mixed, lse, grad_mixed, table, embed2)


def bias_tables(embed):
    last = LEFT + RIGHT
    tail = jnp.broadcast_to(embed[last:], (320 - last - 1, HD))
    head = jnp.broadcast_to(embed[:1], (192, HD))
    table = jnp.concatenate([embed, tail, head], axis=0)
    pair = jnp.concatenate([table, table], axis=1)
    return pair, pair[:128]


CONV_ROWS = 64
EDGE = 32


def conv_fwd_kernel(u_ref, w_ref, m_ref, padded):
    rows = u_ref.shape[0]
    padded[:EDGE, :] = jnp.zeros((EDGE, 128), HIGH)
    padded[EDGE:, :] = u_ref[...].astype(HIGH)

    def chunk(i, carry):
        start = pl.multiple_of(i * CONV_ROWS, CONV_ROWS)
        total = jnp.zeros((CONV_ROWS, 128), HIGH)
        for tap in range(KERNEL):
            total += w_ref[tap : tap + 1, :] * padded[pl.ds(start + (EDGE - KERNEL + 1 + tap), CONV_ROWS), :]
        m_ref[pl.ds(start, CONV_ROWS), :] = total
        return carry

    lax.fori_loop(0, rows // CONV_ROWS, chunk, 0)


def conv_fwd_call(u, kernel):
    rows, width = u.shape
    return pl.pallas_call(
        conv_fwd_kernel,
        grid=(width // 128,),
        in_specs=[pl.BlockSpec((rows, 128), lambda c: (0, c)), pl.BlockSpec((KERNEL, 128), lambda c: (0, c))],
        out_specs=pl.BlockSpec((rows, 128), lambda c: (0, c)),
        out_shape=jax.ShapeDtypeStruct((rows, width), HIGH),
        scratch_shapes=[pltpu.VMEM((rows + EDGE, 128), HIGH)],
        cost_estimate=pl.CostEstimate(flops=62 * rows * width, bytes_accessed=6 * rows * width, transcendentals=0),
    )(u, kernel)


def conv_bwd_kernel(dm_ref, u_ref, pre_a_ref, pre_b_ref, w_ref, g_ref, dw_ref, padded, acc):
    rows = u_ref.shape[0]
    padded[:rows, :] = dm_ref[...]
    padded[rows:, :] = jnp.zeros((EDGE, 128), HIGH)
    acc[...] = jnp.zeros_like(acc)

    def chunk(i, carry):
        start = pl.multiple_of(i * CONV_ROWS, CONV_ROWS)
        at = pl.ds(start, CONV_ROWS)
        u = u_ref[at, :].astype(HIGH)
        total = jnp.zeros((CONV_ROWS, 128), HIGH)
        for tap in range(KERNEL):
            later = padded[pl.ds(start + (KERNEL - 1 - tap), CONV_ROWS), :]
            total += w_ref[tap : tap + 1, :] * later
            acc[tap] += jnp.sum((u * later).reshape(CONV_ROWS // 8, 8, 128), axis=0)
        gate = jax.nn.sigmoid(pre_b_ref[at, :].astype(HIGH))
        through = total * gate
        g_ref[0, at, :] = through.astype(LOW)
        g_ref[1, at, :] = (through * pre_a_ref[at, :].astype(HIGH) * (1.0 - gate)).astype(LOW)
        return carry

    lax.fori_loop(0, rows // CONV_ROWS, chunk, 0)
    dw_ref[...] = jnp.sum(acc[...], axis=1)


def conv_bwd_call(dm, u, pre, kernel):
    rows, width = u.shape
    cols = width // 128
    block = pl.BlockSpec((rows, 128), lambda c: (0, c))
    taps = pl.BlockSpec((KERNEL, 128), lambda c: (0, c))
    return pl.pallas_call(
        conv_bwd_kernel,
        grid=(cols,),
        in_specs=[block, block, block, pl.BlockSpec((rows, 128), lambda c: (0, cols + c)), taps],
        out_specs=[pl.BlockSpec((2, rows, 128), lambda c: (0, 0, c)), taps],
        out_shape=[jax.ShapeDtypeStruct((2, rows, width), LOW), jax.ShapeDtypeStruct((KERNEL, width), HIGH)],
        scratch_shapes=[pltpu.VMEM((rows + EDGE, 128), HIGH), pltpu.VMEM((KERNEL, 8, 128), HIGH)],
        cost_estimate=pl.CostEstimate(flops=124 * rows * width, bytes_accessed=14 * rows * width, transcendentals=rows * width),
    )(dm, u, pre, pre, kernel)


REPLICAS = ("rep", "seq")
X_FLIP, CORE_FLIP = 2, 1


def replica_index():
    return lax.axis_index("rep") * lax.axis_size("seq") + lax.axis_index("seq")


def hop(value, axis, flip):
    return lax.ppermute(value, axis, [(i, i ^ flip) for i in range(lax.axis_size(axis))])


def ring(value, axis, steps):
    count = lax.axis_size(axis)
    return lax.ppermute(value, axis, [(i, (i + steps) % count) for i in range(count)])


def place():
    rep = lax.axis_index("rep")
    return jnp.stack([rep // 2, rep % 2, lax.axis_index("seq"), lax.axis_index("fsdp")]).astype(jnp.int32)


def spread(first, second):
    first_x, second_y = hop(first, "rep", X_FLIP), hop(second, "seq", 1)
    first, second = jnp.stack([first, first_x]), jnp.stack([second, second_y])
    first_y, second_x = hop(first, "seq", 1), hop(second, "rep", X_FLIP)
    near = [first, first_y, second, second_x]
    return near + [hop(value, "rep", CORE_FLIP) for value in near]


def spread_blocks(x, core, y):
    for other in range(2):
        for half, moved, array in ((0, 0, 0), (0, 1, 1), (1, 0, 2), (1, 1, 3)):
            for entry in range(2):
                if half == 0:
                    flip_x, flip_y = entry, moved
                else:
                    flip_x, flip_y = moved, entry
                yield other * 4 + array, entry, half, x ^ flip_x, core ^ other, y ^ flip_y


def assemble_kernel(planes, has_own, at_ref, *refs):
    shard_ref = refs[0] if has_own else None
    parts = refs[has_own : has_own + 8]
    out_ref, sems = refs[has_own + 8 :]
    x, core, y, z = (at_ref[i] for i in range(4))
    half_rows = parts[0].shape[-2]
    rows = 16 * half_rows
    copies = []
    if has_own:
        copies.append((shard_ref, out_ref.at[pl.ds(pl.multiple_of(z * rows, rows), rows), :]))
    for array, entry, half, bx, bc, by in spread_blocks(x, core, y):
        for plane in range(planes):
            base = lax.rem(z + (planes - plane), planes + 1) * rows if has_own else 0
            row = base + (((bx * 2 + bc) * 2 + by) * 2 + half) * half_rows
            copies.append((parts[array].at[entry, plane], out_ref.at[pl.ds(pl.multiple_of(row, half_rows), half_rows), :]))
    started = [pltpu.make_async_copy(source, target, sems.at[i]) for i, (source, target) in enumerate(copies)]
    for copy in started:
        copy.start()
    for copy in started:
        copy.wait()


def assemble(at, shard, parts):
    planes, half_rows, columns = parts[0].shape[1:]
    has_own = 0 if shard is None else 1
    rows = 16 * half_rows * (planes + 1 if has_own else 1)
    own = [shard] if has_own else []
    return pl.pallas_call(
        functools.partial(assemble_kernel, planes, has_own),
        in_specs=[pl.BlockSpec(memory_space=pltpu.SMEM)] + [pl.BlockSpec(memory_space=pl.ANY)] * (8 + has_own),
        out_specs=pl.BlockSpec(memory_space=pltpu.VMEM),
        out_shape=jax.ShapeDtypeStruct((rows, columns), LOW),
        scratch_shapes=[pltpu.SemaphoreType.DMA((16 * planes + has_own,))],
        compiler_params=pltpu.CompilerParams(vmem_limit_bytes=12 * 1024 * 1024),
        cost_estimate=pl.CostEstimate(flops=0, bytes_accessed=4 * rows * columns, transcendentals=0),
    )(at, *own, *parts)


def gather_by_hops(at, shard):
    pieces = lax.axis_size("rep") * lax.axis_size("seq")
    count = shard.shape[0] // pieces
    mine = lax.dynamic_slice_in_dim(shard, replica_index() * count, count, 0)
    got = [ring(mine, "fsdp", steps) for steps in range(1, lax.axis_size("fsdp"))]
    half = count // 2
    first, second = jnp.stack([g[:half] for g in got]), jnp.stack([g[half:] for g in got])
    return assemble(at, shard, spread(first, second))


def plus(a, b):
    return (a.astype(HIGH) + b.astype(HIGH)).astype(LOW)


def pick(value, index, axis):
    return lax.dynamic_index_in_dim(value, index, axis, keepdims=False)


def reduce_by_hops(at, grad):
    x, core, y, z = (at[i] for i in range(4))
    groups = lax.axis_size("fsdp")
    rows, columns = grad.shape
    parts = grad.reshape(groups, 2, 2, 2, 2, rows // (16 * groups), columns)
    total = plus(pick(parts, core, 2), hop(pick(parts, 1 - core, 2), "rep", CORE_FLIP))
    first, second = total[:, :, :, 0], total[:, :, :, 1]
    first = plus(pick(first, x, 1), hop(pick(first, 1 - x, 1), "rep", X_FLIP))
    second = plus(pick(second, y, 2), hop(pick(second, 1 - y, 2), "seq", 1))
    first = plus(pick(first, y, 1), hop(pick(first, 1 - y, 1), "seq", 1))
    second = plus(pick(second, x, 1), hop(pick(second, 1 - x, 1), "rep", X_FLIP))
    both = jnp.stack([first, second], axis=1)
    total = pick(both, z, 0).astype(HIGH)
    for steps in range(1, groups):
        total = total + ring(pick(both, (z + steps) % groups, 0), "fsdp", steps).astype(HIGH)
    total = total.astype(LOW)[:, None]
    return assemble(at, None, spread(total[0], total[1]))


NORM_ROWS = 256


def normed_of(values, gain, shift):
    mean = jnp.mean(values, axis=-1, keepdims=True)
    centred = values - mean
    rstd = lax.rsqrt(jnp.mean(centred * centred, axis=-1, keepdims=True) + EPS)
    unit = centred * rstd
    return unit, rstd, unit * gain + shift


def norm_fwd_kernel(active, x_ref, gain_ref, shift_ref, out_ref):
    _, _, out = normed_of(x_ref[...].astype(HIGH), gain_ref[...], shift_ref[...])
    out_ref[...] = (jax.nn.silu(out) if active else out).astype(LOW)


def norm_fwd(values, gain, shift, active=False):
    rows, width = values.shape
    block = pl.BlockSpec((NORM_ROWS, width), lambda i: (i, 0))
    line = pl.BlockSpec((1, width), lambda i: (0, 0))
    return pl.pallas_call(
        functools.partial(norm_fwd_kernel, active),
        grid=(rows // NORM_ROWS,),
        in_specs=[block, line, line],
        out_specs=block,
        out_shape=jax.ShapeDtypeStruct((rows, width), LOW),
        cost_estimate=pl.CostEstimate(flops=10 * rows * width, bytes_accessed=6 * rows * width, transcendentals=0),
    )(values, gain[None], shift[None])


def norm_bwd_kernel(active, has_rest, scale, x_ref, grad_ref, gain_ref, shift_ref, *refs):
    rest_ref = refs[0] if has_rest else None
    out_ref, low_ref, sums_ref = refs[has_rest:]
    unit, rstd, out = normed_of(x_ref[...].astype(HIGH), gain_ref[...], shift_ref[...])
    grad = grad_ref[...].astype(HIGH)
    if active:
        gate = jax.nn.sigmoid(out)
        grad = grad * (gate * (1.0 + out * (1.0 - gate)))
    inner = grad * gain_ref[...]
    back = (inner - jnp.mean(inner, axis=-1, keepdims=True) - unit * jnp.mean(inner * unit, axis=-1, keepdims=True)) * rstd
    if has_rest:
        back = back + rest_ref[...]
    out_ref[...] = back
    scaled = back * scale
    low_ref[...] = scaled.astype(LOW)

    @pl.when(pl.program_id(0) == 0)
    def _():
        sums_ref[...] = jnp.zeros_like(sums_ref)

    sums_ref[0:1, :] += jnp.sum(grad * unit, axis=0, keepdims=True)
    sums_ref[1:2, :] += jnp.sum(grad, axis=0, keepdims=True)
    sums_ref[2:3, :] += jnp.sum(scaled, axis=0, keepdims=True)


def norm_bwd(values, grad, gain, shift, rest=None, scale=1.0, active=False):
    rows, width = values.shape
    block = pl.BlockSpec((NORM_ROWS, width), lambda i: (i, 0))
    line = pl.BlockSpec((1, width), lambda i: (0, 0))
    extra = [] if rest is None else [rest]
    return pl.pallas_call(
        functools.partial(norm_bwd_kernel, active, len(extra), scale),
        grid=(rows // NORM_ROWS,),
        in_specs=[block, block, line, line] + [block] * len(extra),
        out_specs=[block, block, pl.BlockSpec((8, width), lambda i: (0, 0))],
        out_shape=[
            jax.ShapeDtypeStruct((rows, width), HIGH),
            jax.ShapeDtypeStruct((rows, width), LOW),
            jax.ShapeDtypeStruct((8, width), HIGH),
        ],
        compiler_params=pltpu.CompilerParams(vmem_limit_bytes=32 * 1024 * 1024),
        cost_estimate=pl.CostEstimate(flops=30 * rows * width, bytes_accessed=18 * rows * width, transcendentals=0),
    )(values, grad, gain[None], shift[None], *extra)


def weight_grads_kernel(many, g_ref, last_ref, a_ref, b_ref, out_ref):
    step = pl.program_id(0)

    @pl.when(step < many)
    def _():
        out_ref[...] = left_t(g_ref[...], a_ref[...]).astype(LOW)

    @pl.when(step == many)
    def _():
        out_ref[...] = left_t(last_ref[...], b_ref[...]).astype(LOW)


def weight_grads(grads, last, first_in, last_in):
    many, rows, width = grads.shape
    full = pl.BlockSpec((rows, width), lambda i: (0, 0))
    return pl.pallas_call(
        functools.partial(weight_grads_kernel, many),
        grid=(many + 1,),
        in_specs=[pl.BlockSpec((None, rows, width), lambda i: (jnp.minimum(i, many - 1), 0, 0)), full, full, full],
        out_specs=pl.BlockSpec((width, width), lambda i: (i, 0)),
        out_shape=jax.ShapeDtypeStruct(((many + 1) * width, width), LOW),
        compiler_params=pltpu.CompilerParams(vmem_limit_bytes=40 * 1024 * 1024),
        cost_estimate=pl.CostEstimate(
            flops=2 * (many + 1) * rows * width * width, bytes_accessed=4 * (many + 2) * rows * width, transcendentals=0
        ),
    )(grads, last, first_in, last_in)


def gather_weight(shard):
    pieces = lax.axis_size("rep") * lax.axis_size("seq")
    count = shard.shape[0] // pieces
    piece = lax.dynamic_slice_in_dim(shard, replica_index() * count, count, 0)
    return lax.all_gather(piece, ("fsdp",) + REPLICAS, axis=0, tiled=True)


def reduce_replicas(grad_t):
    return lax.psum_scatter(grad_t, REPLICAS, scatter_dimension=0, tiled=True)


def reduce_groups(part):
    groups = lax.axis_size("fsdp")
    columns, rows = part.shape
    part = jnp.swapaxes(part.reshape(columns, groups, rows // groups), 0, 1)
    part = lax.psum_scatter(part, "fsdp", scatter_dimension=0, tiled=False)
    return lax.all_gather(part, REPLICAS, axis=0, tiled=True)


def reduce_weight(grad_t):
    return reduce_groups(reduce_replicas(grad_t))


def as_grad(grad_t):
    return grad_t.astype(HIGH).T


def swap_in(value):
    count = value.shape[0]
    rows = value.shape[1]
    me = lax.axis_index("seq")
    whole = jnp.zeros((count * rows,) + value.shape[2:], value.dtype)
    own = lax.dynamic_index_in_dim(value, me, 0, keepdims=False)
    whole = lax.dynamic_update_slice_in_dim(whole, own, me * rows, 0)
    for steps in range(1, count):
        sent = lax.dynamic_index_in_dim(value, (me + steps) % count, 0, keepdims=False)
        got = ring(sent, "seq", steps)
        whole = lax.dynamic_update_slice_in_dim(whole, got, ((me - steps) % count) * rows, 0)
    return whole


def swap_out(whole, count, kind, low=None):
    low = whole if low is None else low
    rows = whole.shape[0] // count
    me = lax.axis_index("seq")
    value = jnp.zeros((count, rows) + whole.shape[1:], kind)
    own = lax.dynamic_slice_in_dim(whole, me * rows, rows, 0)
    value = lax.dynamic_update_index_in_dim(value, own.astype(kind), me, 0)
    for steps in range(1, count):
        sent = lax.dynamic_slice_in_dim(low, ((me + steps) % count) * rows, rows, 0)
        got = ring(sent, "seq", steps)
        value = lax.dynamic_update_index_in_dim(value, got.astype(kind), (me - steps) % count, 0)
    return value


def pack_small(arrays, shard):
    gains, shifts, in_bias, out_bias, a_bias, embed, kernel = arrays
    flat = [x.reshape(-1) for x in (gains, shifts, in_bias, out_bias, a_bias, kernel, embed)]
    total = jnp.concatenate(flat)
    return jnp.pad(total, (0, -total.shape[0] % (16 * shard))).reshape(-1, shard)


def unpack_small(packed, shard):
    groups = packed.shape[0]
    wide = lambda lo, hi: jnp.swapaxes(packed[:, lo:hi], 0, 1).reshape(hi - lo, groups * shard)
    taken = 12
    gains, shifts = wide(0, 6), wide(6, 12)
    per = 4
    in_bias = jnp.swapaxes(packed[:, taken : taken + 2 * per].reshape(groups, 2, per * shard), 0, 1).reshape(2, -1)
    taken += 2 * per
    out_bias = wide(taken, taken + 2)
    a_bias = wide(taken + 2, taken + 5)
    kernel = wide(taken + 5, taken + 5 + KERNEL)
    taken += 5 + KERNEL
    buckets = LEFT + RIGHT + 1
    embed = packed[:, taken:].reshape(groups, -1)[:, : buckets * (HD // groups)].reshape(groups, buckets, HD // groups)
    return gains, shifts, in_bias, out_bias, a_bias, jnp.swapaxes(embed, 0, 1).reshape(buckets, HD), kernel


def split_small(whole, groups):
    gains, shifts, in_bias, out_bias, a_bias, embed, kernel = whole
    shard = gains.shape[1] // groups
    cut = lambda x: jnp.swapaxes(x.reshape(x.shape[0], groups, -1), 0, 1).reshape(groups, -1)
    flat = jnp.concatenate([cut(x) for x in (gains, shifts, in_bias, out_bias, a_bias, kernel, embed)], axis=1)
    flat = jnp.pad(flat, ((0, 0), (0, -flat.shape[1] % (16 * shard))))
    return flat.reshape(groups, -1, shard)


def unsplit_small(rows, shapes):
    flat = rows.reshape(-1)
    out, taken = [], 0
    for shape in shapes:
        size = shape[0] * shape[1]
        out.append(flat[taken : taken + size].reshape(shape))
        taken += size
    return out


def gather_small(value):
    groups, z = lax.axis_size("fsdp"), lax.axis_index("fsdp")
    parts = [value] + [ring(value, "fsdp", steps) for steps in range(1, groups)]
    turned = jnp.stack(parts[::-1] * 2)
    return lax.dynamic_slice_in_dim(turned, groups - 1 - z, groups, 0)


def reduce_small(value):
    groups, z = lax.axis_size("fsdp"), lax.axis_index("fsdp")
    for axis, flip in (("rep", CORE_FLIP), ("rep", X_FLIP), ("seq", 1)):
        value = value + hop(value, axis, flip)
    total = pick(value, z, 0)
    for steps in range(1, groups):
        total = total + ring(pick(value, (z + steps) % groups, 0), "fsdp", steps)
    return total


def fast_body(inputs, cotangent, ln_gain, ln_bias, ffn_in, ffn_in_bias, ffn_out, ffn_out_bias, qkv_weight, attn_out, attn_bias, dist_embed, pw_in, depthwise, pw_out):
    micro, clips, rows, width = inputs.shape
    shard = ln_gain.shape[1]
    groups = lax.axis_size("fsdp")
    at = place()
    small = pack_small((ln_gain, ln_bias, ffn_in_bias, ffn_out_bias, attn_bias, dist_embed, depthwise), shard)
    small = gather_small(small)
    start = swap_in(inputs.reshape(micro, rows, width))
    f_in0 = gather_by_hops(at, ffn_in[0])
    f_out0 = gather_by_hops(at, ffn_out[0])
    w_mid = gather_weight(jnp.concatenate([qkv_weight, attn_out, pw_in, pw_out], axis=1))
    w_qkv, w_o, c_in, c_out = jnp.split(w_mid, [3 * width, 4 * width, 6 * width], axis=1)
    f_in1 = gather_by_hops(at, ffn_in[1])
    f_out1 = gather_weight(ffn_out[1])

    gains, shifts, f_in_b, f_out_b, a_bias, embed, kernel = unpack_small(small, shard)
    table, embed2 = bias_tables(embed)
    gains, shifts, f_in_b, f_out_b, a_bias, kernel = (x.astype(HIGH) for x in (gains, shifts, f_in_b, f_out_b, a_bias, kernel))

    def ffn_fwd(values, i, w_in, w_out, which):
        normed = norm_fwd(values, gains[which], shifts[which])
        linear = matmul(normed, w_in) + f_in_b[i]
        active, linear = lax.optimization_barrier((jax.nn.silu(linear).astype(LOW), linear.astype(LOW)))
        out = values.astype(HIGH) + 0.5 * (matmul(active, w_out) + f_out_b[i])
        return out, (values, normed, linear, active)

    def silu_bwd(grad, linear):
        gate = jax.nn.sigmoid(linear)
        return grad * (gate * (1.0 + linear * (1.0 - gate)))

    def ffn_bwd(grad, grad_low, kept, which, w_in, w_out, scale, flipped):
        values, normed, linear, active = kept
        product = left_t if not flipped else lambda a, g: left_t(g, a)
        d_w_out = product(active, grad_low).astype(LOW)
        d_lin = silu_bwd(right_t(grad_low, w_out), linear.astype(HIGH))
        d_b_in = jnp.sum(d_lin, axis=0)
        lin_low, d_w_out = lax.optimization_barrier((d_lin.astype(LOW), d_w_out))
        d_w_in = product(normed, lin_low).astype(LOW)
        lin_low, d_w_in = lax.optimization_barrier((lin_low, d_w_in))
        back = norm_bwd(values, right_t(lin_low, w_in), gains[which], shifts[which], grad, scale)
        return back, d_w_in, d_b_in, d_w_out

    first, keep_one = ffn_fwd(start, 0, f_in0, f_out0, 0)
    n_two = norm_fwd(first, gains[1], shifts[1])
    proj_bias = jnp.concatenate([a_bias[0], jnp.zeros_like(a_bias[0]), a_bias[1]])
    proj = (matmul(n_two, w_qkv) + proj_bias).astype(LOW)
    mixed, lse = attn_forward_call(proj, table, width)
    mixed, cotangent = lax.optimization_barrier((mixed, cotangent))
    cot = swap_in(cotangent.reshape(micro, rows, width))
    second = first + matmul(mixed, w_o) + a_bias[2]
    n_three = norm_fwd(second, gains[2], shifts[2])
    pre = matmul(n_three, c_in)
    gated, pre = lax.optimization_barrier(((pre[:, :width] * jax.nn.sigmoid(pre[:, width:])).astype(LOW), pre.astype(LOW)))
    conv = conv_fwd_call(gated, kernel)
    z = norm_fwd(conv, gains[3], shifts[3], True)
    third = second + matmul(z, c_out)
    fourth, keep_four = ffn_fwd(third, 1, f_in1, f_out1, 4)
    final = norm_fwd(fourth, gains[5], shifts[5])
    out_final = swap_out(final, micro, LOW)

    grad_fourth, grad_low, sums_five = norm_bwd(fourth, cot, gains[5], shifts[5], None, 0.5)
    (grad_third, grad_low, sums_four), d_in1, d_in_b1, d_out1 = ffn_bwd(grad_fourth, grad_low, keep_four, 4, f_in1, f_out1, 1.0, True)
    r_out1, r_in1 = reduce_weight(d_out1), reduce_weight(d_in1)

    conv_low = grad_low
    grad_conv, _, sums_three = norm_bwd(conv, right_t(grad_low, c_out), gains[3], shifts[3], None, 1.0, True)
    g_pre, d_kernel = conv_bwd_call(grad_conv, gated, pre, kernel)
    d_conv = weight_grads(g_pre, conv_low, n_three, z)
    d_conv, g_pre = lax.optimization_barrier((d_conv, g_pre))
    r_conv = reduce_weight(d_conv)
    g_pre = jnp.concatenate([g_pre[0], g_pre[1]], axis=1)
    grad_second, grad_low, sums_two = norm_bwd(second, right_t(g_pre, c_in), gains[2], shifts[2], grad_third)

    attn_low = grad_low
    grad_mixed = right_t(grad_low, w_o).astype(LOW)
    g_proj, d_embed, d_bias = attn_backward_call(proj, mixed, lse, grad_mixed, table, embed2, width)
    d_embed = jnp.sum(d_embed.reshape(2, HD, width // 128, 128), axis=(0, 2)).T[: LEFT + RIGHT + 1]
    d_attn = weight_grads(g_proj, attn_low, n_two, mixed)
    d_attn, g_proj = lax.optimization_barrier((d_attn, g_proj))
    r_attn = reduce_weight(d_attn)
    g_proj = jnp.concatenate([g_proj[0], g_proj[1], g_proj[2]], axis=1)
    grad_first, grad_low, sums_one = norm_bwd(first, right_t(g_proj, w_qkv), gains[1], shifts[1], grad_second, 0.5)

    (grad_start, start_low, sums_zero), d_in0, d_in_b0, d_out0 = ffn_bwd(grad_first, grad_low, keep_one, 0, f_in0, f_out0, 1.0, False)
    r_out0, r_in0 = reduce_by_hops(at, d_out0), reduce_by_hops(at, d_in0)
    grad_start = swap_out(grad_start, micro, HIGH, start_low)

    sums = [sums_zero, sums_one, sums_two, sums_three, sums_four, sums_five]
    small = split_small(
        (
            jnp.stack([x[0] for x in sums]),
            jnp.stack([x[1] for x in sums]),
            jnp.stack([d_in_b0, d_in_b1]),
            jnp.stack([sums_one[2], sums_five[2]]),
            jnp.stack([d_bias[0], d_bias[1], sums_two[2]]),
            d_embed,
            d_kernel,
        ),
        groups,
    )
    small = reduce_small(small)
    shapes = [(6, shard), (6, shard), (2, 4 * shard), (2, shard), (3, shard), (KERNEL, shard), (LEFT + RIGHT + 1, HD // groups)]
    s_gain, s_shift, s_in_b, s_out_b, s_a, s_kernel, s_embed = unsplit_small(small, shapes)
    g_qkv, g_o = r_attn[: 3 * width], r_attn[3 * width :]
    g_c_in, g_c_out = r_conv[: 2 * width], r_conv[2 * width :]
    return (
        out_final.reshape(micro, clips, rows, width),
        grad_start.reshape(micro, clips, rows, width),
        s_gain,
        s_shift,
        jnp.stack([r_in0.astype(HIGH), as_grad(r_in1)]),
        s_in_b,
        jnp.stack([r_out0.astype(HIGH), as_grad(r_out1)]),
        s_out_b,
        as_grad(g_qkv),
        as_grad(g_o),
        s_a,
        s_embed,
        as_grad(g_c_in),
        s_kernel,
        as_grad(g_c_out),
    )


def body(inputs, *rest):
    micro, clips, _, width = inputs.shape
    if (lax.axis_size("seq"), lax.axis_size("rep"), micro, clips) == (2, 4, 2, 1):
        return fast_body(inputs, *rest)
    return general_body(inputs, *rest)


def solution(mesh):
    return jax.shard_map(
        body,
        mesh=mesh,
        in_specs=(
            P(None, ("rep", "fsdp"), "seq", None),
            P(None, ("rep", "fsdp"), "seq", None),
            P(None, "fsdp"),
            P(None, "fsdp"),
            P(None, "fsdp", None),
            P(None, "fsdp"),
            P(None, "fsdp", None),
            P(None, "fsdp"),
            P("fsdp", None),
            P("fsdp", None),
            P(None, "fsdp"),
            P(None, "fsdp"),
            P("fsdp", None),
            P(None, "fsdp"),
            P("fsdp", None),
        ),
        out_specs=(
            P(None, ("rep", "fsdp"), "seq", None),
            P(None, ("rep", "fsdp"), "seq", None),
            P(None, "fsdp"),
            P(None, "fsdp"),
            P(None, "fsdp", None),
            P(None, "fsdp"),
            P(None, "fsdp", None),
            P(None, "fsdp"),
            P("fsdp", None),
            P("fsdp", None),
            P(None, "fsdp"),
            P(None, "fsdp"),
            P("fsdp", None),
            P(None, "fsdp"),
            P("fsdp", None),
        ),
        check_vma=False,
    )
```

```python
import functools

import jax
import jax.numpy as jnp
from jax import lax
from jax.experimental import pallas as pl
from jax.experimental.pallas import tpu as pltpu
from jax.sharding import PartitionSpec as P

H = 16
HD = 64
KERNEL = 31
LEFT = 64
RIGHT = 8


EPS = 1e-05
LOW = jnp.bfloat16
HIGH = jnp.float32


def from_behind(value, axis, steps):
    count = lax.axis_size(axis)
    first, last = (max(0, -steps), min(count, count - steps))
    return lax.ppermute(value, axis, [(source, source + steps) for source in range(first, last)])


def as_sent(array):
    return jax.tree.map(lambda a: a.astype(jnp.bfloat16) if a.dtype == jnp.float32 else a, array)


def layer_norm(values, gain, shift):
    mean = jnp.mean(values, axis=-1, keepdims=True)
    centred = values - mean
    var = jnp.mean(centred * centred, axis=-1, keepdims=True)
    return centred * lax.rsqrt(var + EPS) * gain + shift


def matmul(left, right):
    return jnp.dot(left, right, preferred_element_type=HIGH)


def left_t(left, right):
    return lax.dot_general(left, right, (((0,), (0,)), ((), ())), preferred_element_type=HIGH)


def right_t(left, right):
    return lax.dot_general(left, right, (((1,), (1,)), ((), ())), preferred_element_type=HIGH)


def fetch(shards):
    return (
        lax.all_gather(shards[0], "fsdp", axis=1, tiled=True),
        lax.all_gather(shards[1], "fsdp", axis=1, tiled=True),
        lax.all_gather(shards[2], "fsdp", axis=1, tiled=True),
        lax.all_gather(shards[3], "fsdp", axis=1, tiled=True),
        lax.all_gather(shards[4], "fsdp", axis=1, tiled=True),
        lax.all_gather(shards[5], "fsdp", axis=1, tiled=True),
        lax.all_gather(shards[6], "fsdp", axis=0, tiled=True),
        lax.all_gather(shards[7], "fsdp", axis=0, tiled=True),
        lax.all_gather(shards[8], "fsdp", axis=1, tiled=True),
        lax.all_gather(shards[9], "fsdp", axis=1, tiled=True),
        lax.all_gather(shards[10], "fsdp", axis=0, tiled=True),
        lax.all_gather(shards[11], "fsdp", axis=1, tiled=True),
        lax.all_gather(shards[12], "fsdp", axis=0, tiled=True),
    )


def unpack(whole):
    gains, shifts, f_in, f_in_b, f_out, f_out_b, w_qkv, w_o, a_bias, embed, c_in, kernel, c_out = (
        whole
    )
    return (
        gains.astype(HIGH),
        shifts.astype(HIGH),
        f_in,
        f_in_b.astype(HIGH),
        f_out,
        f_out_b.astype(HIGH),
        w_qkv,
        w_o,
        a_bias.astype(HIGH),
        embed,
        c_in,
        kernel.astype(HIGH),
        c_out,
    )


def ffn_forward(values, gain, shift, w_in, b_in, w_out, b_out):
    normed, norm_pull = jax.vjp(layer_norm, values, gain, shift)
    normed_low = normed.astype(LOW)
    linear = matmul(normed_low, w_in)
    active, act_pull = jax.vjp(lambda lin, bias: jax.nn.silu(lin + bias), linear, b_in)
    active_low = active.astype(LOW)
    out = matmul(active_low, w_out) + b_out
    return (out, (norm_pull, normed_low, act_pull, active_low))


def ffn_backward(grad, kept, w_in, w_out):
    norm_pull, normed_low, act_pull, active_low = kept
    grad_b_out = jnp.sum(grad, axis=0)
    grad_low = grad.astype(LOW)
    grad_w_out = left_t(active_low, grad_low)
    grad_active = right_t(grad_low, w_out)
    grad_lin, grad_b_in = act_pull(grad_active)
    lin_low = grad_lin.astype(LOW)
    grad_w_in = left_t(normed_low, lin_low)
    grad_normed = right_t(lin_low, w_in)
    grad_values, grad_gain, grad_shift = norm_pull(grad_normed)
    return (grad_values, (grad_gain, grad_shift, grad_w_in, grad_b_in, grad_w_out, grad_b_out))


def scores_of(query4, key4, embed, onehot):
    direct_path = jnp.einsum("cnhd,clhd->chnl", query4, key4, preferred_element_type=HIGH)
    rel_low = jnp.einsum("cnhd,bd->chnb", query4, embed, preferred_element_type=HIGH).astype(LOW)
    placed = jnp.einsum("chnb,nbl->chnl", rel_low, onehot, preferred_element_type=HIGH)
    return (direct_path + placed) * HD ** (-0.5)


def attn_forward(values, gain, shift, w_qkv, bias, embed, w_o, onehot):
    clips, rows, width = values.shape
    normed, norm_pull = jax.vjp(layer_norm, values, gain, shift)
    normed_low = normed.astype(LOW).reshape(clips * rows, width)
    proj = matmul(normed_low, w_qkv).reshape(clips, rows, 3 * width)
    query_rows = (proj[..., :width] + bias[0]).astype(LOW)
    key = proj[..., width : 2 * width].astype(LOW)
    value_rows = (proj[..., 2 * width :] + bias[1]).astype(LOW)
    keys, values_all = (
        lax.all_gather(key, "seq", axis=1, tiled=True),
        lax.all_gather(value_rows, "seq", axis=1, tiled=True),
    )
    span = keys.shape[1]
    query4 = query_rows.reshape(clips, rows, H, HD)
    key4 = keys.reshape(clips, span, H, HD)
    value4 = values_all.reshape(clips, span, H, HD)
    scores = scores_of(query4, key4, embed, onehot)
    total_log = jax.nn.logsumexp(scores, axis=-1)
    prob_low = jnp.exp(scores - total_log[..., None]).astype(LOW)
    mixed_precision = jnp.einsum("chnl,clhd->cnhd", prob_low, value4, preferred_element_type=HIGH)
    mixed_low = mixed_precision.astype(LOW).reshape(clips * rows, width)
    out = matmul(mixed_low, w_o) + bias[2]
    return (out, (norm_pull, normed_low, query4, key4, value4, total_log, mixed_low))


def attn_backward(grad, kept, w_qkv, w_o, embed, onehot):
    norm_pull, normed_low, query4, key4, value4, total_log, mixed_low = kept
    clips, rows = (query4.shape[0], query4.shape[1])
    span = key4.shape[1]
    width = H * HD
    scale = HD ** (-0.5)
    grad_b_o = jnp.sum(grad, axis=0)
    grad_low = grad.astype(LOW)
    grad_w_o = left_t(mixed_low, grad_low)
    grad_mixed = right_t(grad_low, w_o).astype(LOW).reshape(clips, rows, H, HD)
    scores = scores_of(query4, key4, embed, onehot)
    attention_probability = jnp.exp(scores - total_log[..., None])
    prob_low = attention_probability.astype(LOW)
    grad_prob = jnp.einsum("cnhd,clhd->chnl", grad_mixed, value4, preferred_element_type=HIGH)
    grad_value = jnp.einsum("chnl,cnhd->clhd", prob_low, grad_mixed, preferred_element_type=HIGH)
    grad_scores = (
        attention_probability
        * (grad_prob - jnp.sum(attention_probability * grad_prob, axis=-1, keepdims=True))
    ).astype(LOW)
    grad_rel = (
        jnp.einsum("chnl,nbl->chnb", grad_scores, onehot, preferred_element_type=HIGH) * scale
    ).astype(LOW)
    grad_query = scale * jnp.einsum(
        "chnl,clhd->cnhd", grad_scores, key4, preferred_element_type=HIGH
    )
    grad_query = grad_query + jnp.einsum(
        "chnb,bd->cnhd", grad_rel, embed, preferred_element_type=HIGH
    )
    grad_embed = jnp.einsum("chnb,cnhd->bd", grad_rel, query4, preferred_element_type=HIGH)
    grad_key = scale * jnp.einsum(
        "chnl,cnhd->clhd", grad_scores, query4, preferred_element_type=HIGH
    )
    mine_key, mine_value = (
        lax.psum_scatter(
            grad_key.reshape(clips, span, width).astype(jnp.bfloat16),
            "seq",
            scatter_dimension=1,
            tiled=True,
        ).astype(jnp.float32),
        lax.psum_scatter(
            grad_value.reshape(clips, span, width).astype(jnp.bfloat16),
            "seq",
            scatter_dimension=1,
            tiled=True,
        ).astype(jnp.float32),
    )
    grad_query = grad_query.reshape(clips, rows, width)
    grad_b_q = jnp.sum(grad_query, axis=(0, 1))
    grad_b_v = jnp.sum(mine_value, axis=(0, 1))
    grad_proj = (
        jnp.concatenate([grad_query, mine_key, mine_value], axis=-1)
        .astype(LOW)
        .reshape(clips * rows, 3 * width)
    )
    grad_w_qkv = left_t(normed_low, grad_proj)
    grad_normed = right_t(grad_proj, w_qkv).reshape(clips, rows, width)
    grad_values, grad_gain, grad_shift = norm_pull(grad_normed)
    grad_bias = jnp.stack([grad_b_q, grad_b_v, grad_b_o])
    return (
        grad_values.reshape(clips * rows, width),
        (grad_gain, grad_shift, grad_w_qkv, grad_bias, grad_embed, grad_w_o),
    )


def depthwise_block(extended, kernel, gain, shift):
    taps = kernel.shape[0]
    span = extended.shape[1] - taps + 1
    total = kernel[0] * extended[:, 0:span, :]
    for tap in range(1, taps):
        total = total + kernel[tap] * extended[:, tap : tap + span, :]
    return jax.nn.silu(layer_norm(total, gain, shift))


def conv_forward(values, gain, shift, w_in, kernel, gain_two, shift_two, w_out):
    clips, rows, width = values.shape
    normed, norm_pull = jax.vjp(layer_norm, values, gain, shift)
    normed_low = normed.astype(LOW).reshape(clips * rows, width)
    pre = matmul(normed_low, w_in).reshape(clips, rows, 2 * width)
    gated, gate_pull = jax.vjp(
        lambda both: both[..., :width] * jax.nn.sigmoid(both[..., width:]), pre
    )
    gated_low = gated.astype(LOW)
    rim = from_behind(gated_low[:, rows - (KERNEL - 1) :, :], "seq", 1)
    extended = jnp.concatenate([rim, gated_low], axis=1).astype(HIGH)
    mixed_precision, mix_pull = jax.vjp(depthwise_block, extended, kernel, gain_two, shift_two)
    mixed_low = mixed_precision.astype(LOW).reshape(clips * rows, width)
    out = matmul(mixed_low, w_out)
    return (out, (norm_pull, normed_low, gate_pull, mix_pull, mixed_low))


def conv_backward(grad, kept, w_in, w_out, clips, rows):
    norm_pull, normed_low, gate_pull, mix_pull, mixed_low = kept
    width = grad.shape[1]
    grad_low = grad.astype(LOW)
    grad_w_out = left_t(mixed_low, grad_low)
    grad_mixed = right_t(grad_low, w_out).reshape(clips, rows, width)
    grad_ext, grad_kernel, grad_gain_two, grad_shift_two = mix_pull(grad_mixed)
    returned = from_behind(grad_ext[:, : KERNEL - 1, :].astype(jnp.bfloat16), "seq", -1).astype(
        jnp.float32
    )
    grad_gated = grad_ext[:, KERNEL - 1 :, :] + jnp.pad(
        returned, ((0, 0), (rows - (KERNEL - 1), 0), (0, 0))
    )
    (grad_pre,) = gate_pull(grad_gated)
    pre_low = grad_pre.astype(LOW).reshape(clips * rows, 2 * width)
    grad_w_in = left_t(normed_low, pre_low)
    grad_normed = right_t(pre_low, w_in).reshape(clips, rows, width)
    grad_values, grad_gain, grad_shift = norm_pull(grad_normed)
    return (
        grad_values.reshape(clips * rows, width),
        (grad_gain, grad_shift, grad_w_in, grad_kernel, grad_gain_two, grad_shift_two, grad_w_out),
    )


def general_body(
    inputs,
    cotangent,
    ln_gain,
    ln_bias,
    ffn_in,
    ffn_in_bias,
    ffn_out,
    ffn_out_bias,
    qkv_weight,
    attn_out,
    attn_bias,
    dist_embed,
    pw_in,
    depthwise,
    pw_out,
):
    shards = (
        ln_gain,
        ln_bias,
        ffn_in,
        ffn_in_bias,
        ffn_out,
        ffn_out_bias,
        qkv_weight,
        attn_out,
        attn_bias,
        dist_embed,
        pw_in,
        depthwise,
        pw_out,
    )
    micro, clips, rows, width = inputs.shape
    span = rows * lax.axis_size("seq")
    positions = lax.axis_index("seq") * rows + jnp.arange(rows, dtype=jnp.int32)
    bucket = (
        jnp.clip(jnp.arange(span, dtype=jnp.int32)[None, :] - positions[:, None], -LEFT, RIGHT)
        + LEFT
    )
    onehot = (
        bucket[:, None, :] == jnp.arange(LEFT + RIGHT + 1, dtype=jnp.int32)[None, :, None]
    ).astype(LOW)
    outputs = []
    input_grads = []
    totals = None
    for step in range(micro):
        whole = fetch(shards)
        (
            gains,
            shifts,
            f_in,
            f_in_b,
            f_out,
            f_out_b,
            w_qkv,
            w_o,
            a_bias,
            embed,
            c_in,
            kernel,
            c_out,
        ) = unpack(whole)
        start_rows = inputs[step].astype(HIGH).reshape(clips * rows, width)
        branch_one, keep_one = ffn_forward(
            start_rows, gains[0], shifts[0], f_in[0], f_in_b[0], f_out[0], f_out_b[0]
        )
        first = start_rows + 0.5 * branch_one
        branch_two, keep_two = attn_forward(
            first.reshape(clips, rows, width),
            gains[1],
            shifts[1],
            w_qkv,
            a_bias,
            embed,
            w_o,
            onehot,
        )
        second = first + branch_two
        branch_three, keep_three = conv_forward(
            second.reshape(clips, rows, width),
            gains[2],
            shifts[2],
            c_in,
            kernel,
            gains[3],
            shifts[3],
            c_out,
        )
        third = second + branch_three
        branch_four, keep_four = ffn_forward(
            third, gains[4], shifts[4], f_in[1], f_in_b[1], f_out[1], f_out_b[1]
        )
        fourth = third + 0.5 * branch_four
        final, final_pull = jax.vjp(layer_norm, fourth, gains[5], shifts[5])
        outputs.append(final.astype(LOW).reshape(clips, rows, width))
        again = (
            lax.all_gather(shards[0], "fsdp", axis=1, tiled=True),
            lax.all_gather(shards[1], "fsdp", axis=1, tiled=True),
            lax.all_gather(shards[2], "fsdp", axis=1, tiled=True),
            lax.all_gather(shards[3], "fsdp", axis=1, tiled=True),
            lax.all_gather(shards[4], "fsdp", axis=1, tiled=True),
            lax.all_gather(shards[5], "fsdp", axis=1, tiled=True),
            lax.all_gather(shards[6], "fsdp", axis=0, tiled=True),
            lax.all_gather(shards[7], "fsdp", axis=0, tiled=True),
            lax.all_gather(shards[8], "fsdp", axis=1, tiled=True),
            lax.all_gather(shards[9], "fsdp", axis=1, tiled=True),
            lax.all_gather(shards[10], "fsdp", axis=0, tiled=True),
            lax.all_gather(shards[11], "fsdp", axis=1, tiled=True),
            lax.all_gather(shards[12], "fsdp", axis=0, tiled=True),
        )
        (
            gains,
            shifts,
            f_in,
            f_in_b,
            f_out,
            f_out_b,
            w_qkv,
            w_o,
            a_bias,
            embed,
            c_in,
            kernel,
            c_out,
        ) = unpack(again)
        grad_fourth, gain_five, shift_five = final_pull(
            cotangent[step].astype(HIGH).reshape(clips * rows, width)
        )
        grad_inner, four_grads = ffn_backward(0.5 * grad_fourth, keep_four, f_in[1], f_out[1])
        grad_third = grad_fourth + grad_inner
        grad_inner, three_grads = conv_backward(grad_third, keep_three, c_in, c_out, clips, rows)
        grad_second = grad_third + grad_inner
        grad_inner, two_grads = attn_backward(grad_second, keep_two, w_qkv, w_o, embed, onehot)
        grad_first = grad_second + grad_inner
        grad_inner, one_grads = ffn_backward(0.5 * grad_first, keep_one, f_in[0], f_out[0])
        input_grads.append((grad_first + grad_inner).reshape(clips, rows, width))
        grads = (
            jnp.stack(
                [
                    one_grads[0],
                    two_grads[0],
                    three_grads[0],
                    three_grads[4],
                    four_grads[0],
                    gain_five,
                ]
            ),
            jnp.stack(
                [
                    one_grads[1],
                    two_grads[1],
                    three_grads[1],
                    three_grads[5],
                    four_grads[1],
                    shift_five,
                ]
            ),
            jnp.stack([one_grads[2], four_grads[2]]),
            jnp.stack([one_grads[3], four_grads[3]]),
            jnp.stack([one_grads[4], four_grads[4]]),
            jnp.stack([one_grads[5], four_grads[5]]),
            two_grads[2],
            two_grads[5],
            two_grads[3],
            two_grads[4],
            three_grads[2],
            three_grads[3],
            three_grads[6],
        )
        totals = grads if totals is None else jax.tree.map(jnp.add, totals, grads)
    totals = (
        lax.psum_scatter(
            totals[0].astype(jnp.bfloat16), "fsdp", scatter_dimension=1, tiled=True
        ).astype(jnp.float32),
        lax.psum_scatter(
            totals[1].astype(jnp.bfloat16), "fsdp", scatter_dimension=1, tiled=True
        ).astype(jnp.float32),
        lax.psum_scatter(
            totals[2].astype(jnp.bfloat16), "fsdp", scatter_dimension=1, tiled=True
        ).astype(jnp.float32),
        lax.psum_scatter(
            totals[3].astype(jnp.bfloat16), "fsdp", scatter_dimension=1, tiled=True
        ).astype(jnp.float32),
        lax.psum_scatter(
            totals[4].astype(jnp.bfloat16), "fsdp", scatter_dimension=1, tiled=True
        ).astype(jnp.float32),
        lax.psum_scatter(
            totals[5].astype(jnp.bfloat16), "fsdp", scatter_dimension=1, tiled=True
        ).astype(jnp.float32),
        lax.psum_scatter(
            totals[6].astype(jnp.bfloat16), "fsdp", scatter_dimension=0, tiled=True
        ).astype(jnp.float32),
        lax.psum_scatter(
            totals[7].astype(jnp.bfloat16), "fsdp", scatter_dimension=0, tiled=True
        ).astype(jnp.float32),
        lax.psum_scatter(
            totals[8].astype(jnp.bfloat16), "fsdp", scatter_dimension=1, tiled=True
        ).astype(jnp.float32),
        lax.psum_scatter(
            totals[9].astype(jnp.bfloat16), "fsdp", scatter_dimension=1, tiled=True
        ).astype(jnp.float32),
        lax.psum_scatter(
            totals[10].astype(jnp.bfloat16), "fsdp", scatter_dimension=0, tiled=True
        ).astype(jnp.float32),
        lax.psum_scatter(
            totals[11].astype(jnp.bfloat16), "fsdp", scatter_dimension=1, tiled=True
        ).astype(jnp.float32),
        lax.psum_scatter(
            totals[12].astype(jnp.bfloat16), "fsdp", scatter_dimension=0, tiled=True
        ).astype(jnp.float32),
    )
    summed = jax.tree.map(
        lambda part: part.astype(jnp.float32), lax.psum(as_sent(totals), ("rep", "seq"))
    )
    return (
        jnp.stack(outputs),
        jnp.stack(input_grads),
        summed[0],
        summed[1],
        summed[2],
        summed[3],
        summed[4],
        summed[5],
        summed[6],
        summed[7],
        summed[8],
        summed[9],
        summed[10],
        summed[11],
        summed[12],
    )


SUB = 128
PAD = 128
FWD_ROWS = 512
BWD_ROWS = 1024


def dot(a, b):
    return lax.dot_general(a, b, (((1,), (0,)), ((), ())), preferred_element_type=HIGH)


def dot_nt(a, b):
    return lax.dot_general(a, b, (((1,), (1,)), ((), ())), preferred_element_type=HIGH)


def biased_scores(qs, table, kcat, s_ref, first, span):
    count = qs.shape[0]
    rel = dot_nt(qs, table).astype(LOW).astype(HIGH)
    lane = lax.broadcasted_iota(jnp.int32, (count, 128), 1)
    block = first + lax.broadcasted_iota(jnp.int32, (count, 128), 0) // SUB
    far = jnp.where(lane < block - 1, rel[:, 384:512], jnp.where(lane > block + 1, rel[:, 128:256], 0.0))
    s_ref[:, PAD : PAD + span] = dot_nt(jnp.concatenate([qs, far.astype(LOW)], axis=1), kcat)
    for sub in range(count // SUB):
        rows = slice(sub * SUB, (sub + 1) * SUB)
        band = pltpu.roll(rel[rows], LEFT, 1, stride=1, stride_axis=0)
        at = pl.multiple_of((first + sub) * SUB, 128)
        s_ref[rows, pl.ds(at, 384)] += band[:, :384]


def blocks_onehot(span):
    row = lax.broadcasted_iota(jnp.int32, (span, 128), 0)
    lane = lax.broadcasted_iota(jnp.int32, (span, 128), 1)
    return (row // SUB == lane).astype(HIGH).astype(LOW)


def attn_fwd_kernel(q_ref, k_ref, v_ref, table_ref, o_ref, lse_ref, kcat, vcat, s_ref):
    span = k_ref.shape[0]
    kcat[:, :128] = k_ref[...]
    kcat[:, 128:] = blocks_onehot(span)
    vcat[:, :128] = v_ref[...]
    vcat[:, 128:] = jnp.ones((span, 128), LOW)
    lane = lax.broadcasted_iota(jnp.int32, (FWD_ROWS, 128), 1)

    def body(qb, carry):
        rows = pl.ds(pl.multiple_of(qb * FWD_ROWS, FWD_ROWS), FWD_ROWS)
        q = q_ref[rows, :].astype(HIGH) * (HD**-0.5)
        outs, logs = [], []
        for h in range(2):
            mine = (lane < HD) if h == 0 else (lane >= HD)
            qs = jnp.where(mine, q, 0.0).astype(LOW)
            sr = s_ref.at[h]
            biased_scores(qs, table_ref[...], kcat[...], sr, qb * (FWD_ROWS // SUB), span)
        for h in range(2):
            s = s_ref[h, :, PAD : PAD + span]
            top = jnp.max(s, axis=-1, keepdims=True)
            p = jnp.exp(s - top).astype(LOW)
            mixed = dot(p, vcat[...])
            total = mixed[:, 128:]
            outs.append(mixed[:, :128] / total)
            logs.append(top + jnp.log(total))
        o_ref[rows, :] = jnp.where(lane < HD, outs[0], outs[1]).astype(o_ref.dtype)
        lse_ref[rows, :] = jnp.where(lane < HD, logs[0], logs[1])
        return carry

    lax.fori_loop(0, q_ref.shape[0] // FWD_ROWS, body, 0)


def attn_forward_call(proj, table, width):
    rows = proj.shape[0]
    pairs = width // 128
    col = lambda off: pl.BlockSpec((rows, 128), lambda h: (0, off * pairs + h))
    return pl.pallas_call(
        attn_fwd_kernel,
        grid=(pairs,),
        in_specs=[col(0), col(1), col(2), pl.BlockSpec((512, 128), lambda h: (0, 0))],
        out_specs=[pl.BlockSpec((rows, 128), lambda h: (0, h))] * 2,
        out_shape=[jax.ShapeDtypeStruct((rows, width), LOW), jax.ShapeDtypeStruct((rows, width), HIGH)],
        scratch_shapes=[
            pltpu.VMEM((rows, 256), LOW),
            pltpu.VMEM((rows, 256), LOW),
            pltpu.VMEM((2, FWD_ROWS, rows + 2 * PAD), HIGH),
        ],
        compiler_params=pltpu.CompilerParams(vmem_limit_bytes=40 * 1024 * 1024),
        cost_estimate=pl.CostEstimate(
            flops=16 * rows * rows * width, bytes_accessed=12 * rows * width, transcendentals=rows * rows * 16
        ),
    )(proj, proj, proj, table)


def attn_bwd_kernel(q_ref, k_ref, v_ref, o_ref, lse_ref, do_ref, table_ref, embed_ref,
                    g_ref, dembed_ref, bias_ref, kcat, qt, dot_t, dkt, dvt, s_ref):
    span = k_ref.shape[0]
    count = BWD_ROWS
    kcat[:, :128] = k_ref[...]
    kcat[:, 128:] = blocks_onehot(span)
    qt[...] = (q_ref[...].astype(HIGH) * (HD**-0.5)).T.astype(LOW)
    dot_t[...] = do_ref[...].astype(HIGH).T.astype(LOW)
    dkt[...] = jnp.zeros_like(dkt)
    dvt[...] = jnp.zeros_like(dvt)
    lane = lax.broadcasted_iota(jnp.int32, (count, 128), 1)
    block_of = lax.broadcasted_iota(jnp.int32, (count, 128), 0) // SUB
    column = lax.broadcasted_iota(jnp.int32, (SUB, 384), 1)
    last = q_ref.shape[0] // SUB - 1
    turn = lax.broadcasted_iota(jnp.int32, (SUB, SUB), 0) + lax.broadcasted_iota(jnp.int32, (SUB, SUB), 1)
    flip = (turn == SUB - 1).astype(HIGH).astype(LOW)
    lane_sub = lax.broadcasted_iota(jnp.int32, (SUB, 128), 1)
    edge = LEFT + RIGHT

    def body(qb, carry):
        dembed, dbias = carry
        first = qb * (count // SUB)
        rows = pl.ds(pl.multiple_of(qb * count, count), count)
        q = q_ref[rows, :].astype(HIGH) * (HD**-0.5)
        grad = do_ref[rows, :].astype(HIGH)
        lse2 = lse_ref[rows, :]
        weighted = grad * o_ref[rows, :].astype(HIGH)
        block = first + block_of
        dqs, news = [], []
        for h in range(2):
            mine = (lane < HD) if h == 0 else (lane >= HD)
            qs = jnp.where(mine, q, 0.0).astype(LOW)
            biased_scores(qs, table_ref[...], kcat[...], s_ref.at[h], first, span)
        for h in range(2):
            mine = (lane < HD) if h == 0 else (lane >= HD)
            part = slice(h * HD, (h + 1) * HD)
            sr = s_ref.at[h]
            lse = lse2[:, h * HD : h * HD + 1]
            p = jnp.exp(sr[:, PAD : PAD + span] - lse)
            delta = jnp.sum(jnp.where(mine, weighted, 0.0), axis=-1, keepdims=True)
            gs = jnp.where(mine, grad, 0.0).astype(LOW)
            ds = p * (dot_nt(gs, v_ref[...]) - delta)
            sr[:, PAD : PAD + span] = ds
            ds_low = ds.astype(LOW)
            dq = dot(ds_low, kcat[...])
            dvt[part, :] += dot(dot_t[part, rows], p.astype(LOW))
            dkt[part, :] += dot(qt[part, rows], ds_low)
            tables = []
            for sub in range(count // SUB):
                band = sr[sub * SUB : (sub + 1) * SUB, pl.ds(pl.multiple_of((first + sub) * SUB, 128), 384)]
                if sub == 0:
                    band = jnp.where((column < 128) & (first == 0), 0.0, band)
                if sub == count // SUB - 1:
                    band = jnp.where((column >= 256) & (first + sub == last), 0.0, band)
                turned = dot(flip, band.astype(LOW))
                turned = jnp.concatenate([turned, jnp.zeros((SUB, 128), HIGH)], axis=1)
                drel = pltpu.roll(turned, 512 - LEFT - SUB + 1, 1, stride=1, stride_axis=0)
                near, middle = drel[:, :128], drel[:, 256:384]
                left = jnp.sum(drel[:, 384:512] + jnp.where(lane_sub >= 64, middle, 0.0), axis=-1, keepdims=True)
                right = jnp.sum(
                    drel[:, 128:256] + jnp.where(lane_sub < 64, middle, 0.0) + jnp.where(lane_sub >= edge, near, 0.0),
                    axis=-1,
                    keepdims=True,
                )
                left_top, right_top = left.astype(LOW).astype(HIGH), right.astype(LOW).astype(HIGH)
                packed = jnp.where(lane_sub < edge, near, 0.0)
                for at, value in ((80, left_top), (81, left - left_top), (82, right_top), (83, right - right_top)):
                    packed = jnp.where(lane_sub == at, value, packed)
                tables.append(dot(flip, packed.astype(LOW)))
            table = jnp.concatenate(tables, axis=0)
            sums = dq[:, 128:]
            left = jnp.sum(jnp.where(lane < block - 1, sums, 0.0) + jnp.where((lane == 80) | (lane == 81), table, 0.0), axis=-1, keepdims=True)
            right = jnp.sum(jnp.where(lane > block + 1, sums, 0.0) + jnp.where((lane == 82) | (lane == 83), table, 0.0), axis=-1, keepdims=True)
            drl = jnp.where(lane < edge, table, 0.0) + jnp.where(lane == 0, left, 0.0) + jnp.where(lane == edge, right, 0.0)
            drl = drl.astype(LOW)
            dqs.append((dq[:, :128] + dot(drl, embed_ref[...])) * (HD**-0.5))
            news.append(dembed[part] + dot(qt[part, rows], drl))
        dq = jnp.where(lane < HD, dqs[0], dqs[1])
        g_ref[0, rows, :] = dq.astype(LOW)
        return (jnp.concatenate(news, axis=0), dbias + jnp.sum(dq, axis=0, keepdims=True))

    start = (jnp.zeros((128, 128), HIGH), jnp.zeros((1, 128), HIGH))
    dembed, dbias = lax.fori_loop(0, q_ref.shape[0] // count, body, start)
    dembed_ref[...] = dembed
    g_ref[1, :, :] = dkt[...].T.astype(LOW)
    dv = dvt[...].T
    g_ref[2, :, :] = dv.astype(LOW)
    row8 = lax.broadcasted_iota(jnp.int32, (8, 128), 0)
    bias_ref[...] = jnp.where(row8 == 0, dbias, jnp.where(row8 == 1, jnp.sum(dv, axis=0, keepdims=True), 0.0))


def attn_backward_call(proj, mixed, lse, grad_mixed, table, embed2, width):
    rows = proj.shape[0]
    pairs = width // 128
    col = lambda off: pl.BlockSpec((rows, 128), lambda h: (0, off * pairs + h))
    return pl.pallas_call(
        attn_bwd_kernel,
        grid=(pairs,),
        in_specs=[
            col(0), col(1), col(2), col(0), col(0), col(0),
            pl.BlockSpec((512, 128), lambda h: (0, 0)),
            pl.BlockSpec((128, 128), lambda h: (0, 0)),
        ],
        out_specs=[
            pl.BlockSpec((3, rows, 128), lambda h: (0, 0, h)),
            pl.BlockSpec((128, 128), lambda h: (0, h)),
            pl.BlockSpec((8, 128), lambda h: (0, h)),
        ],
        out_shape=[
            jax.ShapeDtypeStruct((3, rows, width), LOW),
            jax.ShapeDtypeStruct((128, width), HIGH),
            jax.ShapeDtypeStruct((8, width), HIGH),
        ],
        scratch_shapes=[
            pltpu.VMEM((rows, 256), LOW),
            pltpu.VMEM((128, rows), LOW),
            pltpu.VMEM((128, rows), LOW),
            pltpu.VMEM((128, rows), HIGH),
            pltpu.VMEM((128, rows), HIGH),
            pltpu.VMEM((2, BWD_ROWS, rows + 2 * PAD), HIGH),
        ],
        compiler_params=pltpu.CompilerParams(vmem_limit_bytes=48 * 1024 * 1024),
        cost_estimate=pl.CostEstimate(
            flops=40 * rows * rows * width, bytes_accessed=24 * rows * width, transcendentals=rows * rows * 16
        ),
    )(proj, proj, proj, mixed, lse, grad_mixed, table, embed2)


def bias_tables(embed):
    last = LEFT + RIGHT
    tail = jnp.broadcast_to(embed[last:], (320 - last - 1, HD))
    head = jnp.broadcast_to(embed[:1], (192, HD))
    table = jnp.concatenate([embed, tail, head], axis=0)
    pair = jnp.concatenate([table, table], axis=1)
    return pair, pair[:128]


CONV_ROWS = 64
EDGE = 32


def conv_fwd_kernel(u_ref, w_ref, m_ref, padded):
    rows = u_ref.shape[0]
    padded[:EDGE, :] = jnp.zeros((EDGE, 128), HIGH)
    padded[EDGE:, :] = u_ref[...].astype(HIGH)

    def chunk(i, carry):
        start = pl.multiple_of(i * CONV_ROWS, CONV_ROWS)
        total = jnp.zeros((CONV_ROWS, 128), HIGH)
        for tap in range(KERNEL):
            total += w_ref[tap : tap + 1, :] * padded[pl.ds(start + (EDGE - KERNEL + 1 + tap), CONV_ROWS), :]
        m_ref[pl.ds(start, CONV_ROWS), :] = total
        return carry

    lax.fori_loop(0, rows // CONV_ROWS, chunk, 0)


def conv_fwd_call(u, kernel):
    rows, width = u.shape
    return pl.pallas_call(
        conv_fwd_kernel,
        grid=(width // 128,),
        in_specs=[pl.BlockSpec((rows, 128), lambda c: (0, c)), pl.BlockSpec((KERNEL, 128), lambda c: (0, c))],
        out_specs=pl.BlockSpec((rows, 128), lambda c: (0, c)),
        out_shape=jax.ShapeDtypeStruct((rows, width), HIGH),
        scratch_shapes=[pltpu.VMEM((rows + EDGE, 128), HIGH)],
        cost_estimate=pl.CostEstimate(flops=62 * rows * width, bytes_accessed=6 * rows * width, transcendentals=0),
    )(u, kernel)


def conv_bwd_kernel(dm_ref, u_ref, pre_a_ref, pre_b_ref, w_ref, g_ref, dw_ref, padded, acc):
    rows = u_ref.shape[0]
    padded[:rows, :] = dm_ref[...]
    padded[rows:, :] = jnp.zeros((EDGE, 128), HIGH)
    acc[...] = jnp.zeros_like(acc)

    def chunk(i, carry):
        start = pl.multiple_of(i * CONV_ROWS, CONV_ROWS)
        at = pl.ds(start, CONV_ROWS)
        u = u_ref[at, :].astype(HIGH)
        total = jnp.zeros((CONV_ROWS, 128), HIGH)
        for tap in range(KERNEL):
            later = padded[pl.ds(start + (KERNEL - 1 - tap), CONV_ROWS), :]
            total += w_ref[tap : tap + 1, :] * later
            acc[tap] += jnp.sum((u * later).reshape(CONV_ROWS // 8, 8, 128), axis=0)
        gate = jax.nn.sigmoid(pre_b_ref[at, :].astype(HIGH))
        through = total * gate
        g_ref[0, at, :] = through.astype(LOW)
        g_ref[1, at, :] = (through * pre_a_ref[at, :].astype(HIGH) * (1.0 - gate)).astype(LOW)
        return carry

    lax.fori_loop(0, rows // CONV_ROWS, chunk, 0)
    dw_ref[...] = jnp.sum(acc[...], axis=1)


def conv_bwd_call(dm, u, pre, kernel):
    rows, width = u.shape
    cols = width // 128
    block = pl.BlockSpec((rows, 128), lambda c: (0, c))
    taps = pl.BlockSpec((KERNEL, 128), lambda c: (0, c))
    return pl.pallas_call(
        conv_bwd_kernel,
        grid=(cols,),
        in_specs=[block, block, block, pl.BlockSpec((rows, 128), lambda c: (0, cols + c)), taps],
        out_specs=[pl.BlockSpec((2, rows, 128), lambda c: (0, 0, c)), taps],
        out_shape=[jax.ShapeDtypeStruct((2, rows, width), LOW), jax.ShapeDtypeStruct((KERNEL, width), HIGH)],
        scratch_shapes=[pltpu.VMEM((rows + EDGE, 128), HIGH), pltpu.VMEM((KERNEL, 8, 128), HIGH)],
        cost_estimate=pl.CostEstimate(flops=124 * rows * width, bytes_accessed=14 * rows * width, transcendentals=rows * width),
    )(dm, u, pre, pre, kernel)


REPLICAS = ("rep", "seq")
X_FLIP, CORE_FLIP = 2, 1


def replica_index():
    return lax.axis_index("rep") * lax.axis_size("seq") + lax.axis_index("seq")


def hop(value, axis, flip):
    return lax.ppermute(value, axis, [(i, i ^ flip) for i in range(lax.axis_size(axis))])


def ring(value, axis, steps):
    count = lax.axis_size(axis)
    return lax.ppermute(value, axis, [(i, (i + steps) % count) for i in range(count)])


def place():
    rep = lax.axis_index("rep")
    return jnp.stack([rep // 2, rep % 2, lax.axis_index("seq"), lax.axis_index("fsdp")]).astype(jnp.int32)


def spread_blocks(x, core, y):
    for other in range(2):
        for half, moved, array in ((0, 0, 0), (0, 1, 1), (1, 0, 2), (1, 1, 3)):
            for entry in range(2):
                if half == 0:
                    flip_x, flip_y = entry, moved
                else:
                    flip_x, flip_y = moved, entry
                yield other * 4 + array, entry, half, x ^ flip_x, core ^ other, y ^ flip_y


def assemble_kernel(planes, at_ref, shard_ref, *refs):
    parts = refs[:8]
    out_ref, sems = refs[8:]
    x, core, y, z = (at_ref[i] for i in range(4))
    half_rows = parts[0].shape[-2]
    rows = 16 * half_rows
    copies = [(shard_ref, out_ref.at[pl.ds(pl.multiple_of(z * rows, rows), rows), :])]
    for array, entry, half, bx, bc, by in spread_blocks(x, core, y):
        for plane in range(planes):
            base = lax.rem(z + (planes - plane), planes + 1) * rows
            row = base + (((bx * 2 + bc) * 2 + by) * 2 + half) * half_rows
            copies.append((parts[array].at[entry, plane], out_ref.at[pl.ds(pl.multiple_of(row, half_rows), half_rows), :]))
    started = [pltpu.make_async_copy(source, target, sems.at[i]) for i, (source, target) in enumerate(copies)]
    for copy in started:
        copy.start()
    for copy in started:
        copy.wait()


def assemble(at, shard, parts):
    planes, half_rows, columns = parts[0].shape[1:]
    rows = 16 * half_rows * (planes + 1)
    return pl.pallas_call(
        functools.partial(assemble_kernel, planes),
        in_specs=[pl.BlockSpec(memory_space=pltpu.SMEM)] + [pl.BlockSpec(memory_space=pl.ANY)] * 9,
        out_specs=pl.BlockSpec(memory_space=pltpu.VMEM),
        out_shape=jax.ShapeDtypeStruct((rows, columns), LOW),
        scratch_shapes=[pltpu.SemaphoreType.DMA((16 * planes + 1,))],
        compiler_params=pltpu.CompilerParams(vmem_limit_bytes=12 * 1024 * 1024),
        cost_estimate=pl.CostEstimate(flops=0, bytes_accessed=4 * rows * columns, transcendentals=0),
    )(at, shard, *parts)


def own_piece(shard):
    count = shard.shape[0] // (lax.axis_size("rep") * lax.axis_size("seq"))
    return lax.dynamic_slice_in_dim(shard, replica_index() * count, count, 0)


def from_planes(piece):
    got = [ring(piece, "fsdp", steps) for steps in range(1, lax.axis_size("fsdp"))]
    half = piece.shape[0] // 2
    return jnp.stack([g[:half] for g in got]), jnp.stack([g[half:] for g in got])


def around(halves):
    first, second = halves
    first_x, second_y = hop(first, "rep", X_FLIP), hop(second, "seq", 1)
    first, second = jnp.stack([first, first_x]), jnp.stack([second, second_y])
    first_y, second_x = hop(first, "seq", 1), hop(second, "rep", X_FLIP)
    return [first, first_y, second, second_x]


def both_cores(near):
    return near + [hop(value, "rep", CORE_FLIP) for value in near]


def plus(a, b):
    return (a.astype(HIGH) + b.astype(HIGH)).astype(LOW)


def pick(value, index, axis):
    return lax.dynamic_index_in_dim(value, index, axis, keepdims=False)


X, Y, CORE = 4, 1, 2


def across(value, flip):
    pieces = lax.axis_size("rep") * lax.axis_size("seq")
    return lax.ppermute(value, REPLICAS, [(i, i ^ flip) for i in range(pieces)])


def reduce_cores(at, grad):
    groups = lax.axis_size("fsdp")
    rows, columns = grad.shape
    parts = grad.reshape(groups, 2, 2, 2, rows // (8 * groups), columns)
    return plus(pick(parts, at[1], 2), across(pick(parts, 1 - at[1], 2), CORE))


def reduce_first(at, total):
    x, y = at[0], at[2]
    half = total.shape[3] // 2
    first, second = total[:, :, :, :half], total[:, :, :, half:]
    first = plus(pick(first, x, 1), across(pick(first, 1 - x, 1), X))
    second = plus(pick(second, y, 2), across(pick(second, 1 - y, 2), Y))
    return first, second


def reduce_second(at, halves):
    x, y = at[0], at[2]
    first, second = halves
    first = plus(pick(first, y, 1), across(pick(first, 1 - y, 1), Y))
    second = plus(pick(second, x, 1), across(pick(second, 1 - x, 1), X))
    return jnp.concatenate([first, second], axis=1)


def reduce_along(at, part):
    groups, z = lax.axis_size("fsdp"), at[3]
    total = pick(part, z, 0).astype(HIGH)
    for steps in range(1, groups):
        total = total + ring(pick(part, (z + steps) % groups, 0), "fsdp", steps).astype(HIGH)
    return total.astype(LOW)


def spread_plane(part):
    return jnp.stack([part] + [across(part, flip) for flip in (X, Y, X + Y)])


def finish_kernel(at_ref, near_ref, far_ref, whole_ref, out_ref):
    step = pl.program_id(0)

    @pl.when(step < 4)
    def _():
        out_ref[...] = near_ref[...].astype(HIGH)

    @pl.when(step >= 4)
    def _():
        out_ref[...] = far_ref[...].astype(HIGH)


def finish_place(step, at):
    x, core, y = at[0], at[1], at[2]
    entry = step % 4
    return ((x ^ (entry % 2)) * 2 + (core ^ (step // 4))) * 2 + (y ^ (entry // 2))


def finish_first(at, near, far, whole):
    _, rows, columns = near.shape
    return pl.pallas_call(
        finish_kernel,
        grid_spec=pltpu.PrefetchScalarGridSpec(
            num_scalar_prefetch=1,
            grid=(8,),
            in_specs=[
                pl.BlockSpec((1, rows, columns), lambda i, at: (jnp.minimum(i, 3), 0, 0)),
                pl.BlockSpec((1, rows, columns), lambda i, at: (jnp.maximum(i - 4, 0), 0, 0)),
                pl.BlockSpec(memory_space=pl.ANY),
            ],
            out_specs=pl.BlockSpec((1, rows, columns), lambda i, at: (0, finish_place(i, at), 0)),
        ),
        out_shape=jax.ShapeDtypeStruct(whole.shape, HIGH),
        input_output_aliases={3: 0},
        cost_estimate=pl.CostEstimate(flops=0, bytes_accessed=48 * rows * columns, transcendentals=0),
    )(at, near, far, whole)


def turn_early_kernel(count, part_ref, out_ref, in_ref, conv_ref):
    shard, columns = part_ref.shape[2], out_ref.shape[2]
    for block in range(count):
        rows = slice(block * columns, (block + 1) * columns)
        out_ref[0, block * shard : (block + 1) * shard, :] = part_ref[0, rows, :].astype(HIGH).T
    edge = count * columns
    middle = edge + in_ref.shape[2]
    in_ref[0] = part_ref[0, edge:middle, :].astype(HIGH).T
    conv_ref[...] = part_ref[0, middle:, :].astype(HIGH).T


def turn_early(part, width, hidden):
    replicas, total, shard = part.shape
    count = hidden // width
    inner = total - (width + hidden) // replicas
    return pl.pallas_call(
        functools.partial(turn_early_kernel, count),
        grid=(replicas,),
        in_specs=[pl.BlockSpec((1, total, shard), lambda r: (r, 0, 0))],
        out_specs=[
            pl.BlockSpec((1, count * shard, width // replicas), lambda r: (1, 0, r)),
            pl.BlockSpec((1, shard, hidden // replicas), lambda r: (1, 0, r)),
            pl.BlockSpec((shard, 3 * width // replicas), lambda r: (0, r)),
        ],
        out_shape=[
            jax.ShapeDtypeStruct((2, count * shard, width), HIGH),
            jax.ShapeDtypeStruct((2, shard, hidden), HIGH),
            jax.ShapeDtypeStruct((shard, 3 * width), HIGH),
        ],
        cost_estimate=pl.CostEstimate(flops=0, bytes_accessed=6 * replicas * total * shard, transcendentals=0),
    )(part)


def turn_attn_kernel(edge, part_ref, qkv_ref, o_ref):
    turned = part_ref[0].astype(HIGH).T

    @pl.when(pl.program_id(0) < edge)
    def _():
        qkv_ref[...] = turned

    @pl.when(pl.program_id(0) >= edge)
    def _():
        o_ref[...] = turned


def turn_attn(part, width):
    replicas, total, shard = part.shape
    edge = 3 * width // total
    return pl.pallas_call(
        functools.partial(turn_attn_kernel, edge),
        grid=(replicas,),
        in_specs=[pl.BlockSpec((1, total, shard), lambda r: (r, 0, 0))],
        out_specs=[
            pl.BlockSpec((shard, total), lambda r: (0, jnp.minimum(r, edge - 1))),
            pl.BlockSpec((shard, total), lambda r: (0, jnp.maximum(r - edge, 0))),
        ],
        out_shape=[jax.ShapeDtypeStruct((shard, 3 * width), HIGH), jax.ShapeDtypeStruct((shard, width), HIGH)],
        cost_estimate=pl.CostEstimate(flops=0, bytes_accessed=6 * replicas * total * shard, transcendentals=0),
    )(part)


NORM_ROWS = 256


def normed_of(values, gain, shift):
    mean = jnp.mean(values, axis=-1, keepdims=True)
    centred = values - mean
    rstd = lax.rsqrt(jnp.mean(centred * centred, axis=-1, keepdims=True) + EPS)
    unit = centred * rstd
    return unit, rstd, unit * gain + shift


def norm_fwd_kernel(active, x_ref, gain_ref, shift_ref, out_ref):
    _, _, out = normed_of(x_ref[...].astype(HIGH), gain_ref[...], shift_ref[...])
    out_ref[...] = (jax.nn.silu(out) if active else out).astype(LOW)


def norm_fwd(values, gain, shift, active=False):
    rows, width = values.shape
    block = pl.BlockSpec((NORM_ROWS, width), lambda i: (i, 0))
    line = pl.BlockSpec((1, width), lambda i: (0, 0))
    return pl.pallas_call(
        functools.partial(norm_fwd_kernel, active),
        grid=(rows // NORM_ROWS,),
        in_specs=[block, line, line],
        out_specs=block,
        out_shape=jax.ShapeDtypeStruct((rows, width), LOW),
        cost_estimate=pl.CostEstimate(flops=10 * rows * width, bytes_accessed=6 * rows * width, transcendentals=0),
    )(values, gain[None], shift[None])


def norm_bwd_kernel(active, has_rest, scale, x_ref, grad_ref, gain_ref, shift_ref, *refs):
    rest_ref = refs[0] if has_rest else None
    out_ref, low_ref, sums_ref = refs[has_rest:]
    unit, rstd, out = normed_of(x_ref[...].astype(HIGH), gain_ref[...], shift_ref[...])
    grad = grad_ref[...].astype(HIGH)
    if active:
        gate = jax.nn.sigmoid(out)
        grad = grad * (gate * (1.0 + out * (1.0 - gate)))
    inner = grad * gain_ref[...]
    back = (inner - jnp.mean(inner, axis=-1, keepdims=True) - unit * jnp.mean(inner * unit, axis=-1, keepdims=True)) * rstd
    if has_rest:
        back = back + rest_ref[...]
    out_ref[...] = back
    scaled = back * scale
    low_ref[...] = scaled.astype(LOW)

    @pl.when(pl.program_id(0) == 0)
    def _():
        sums_ref[...] = jnp.zeros_like(sums_ref)

    sums_ref[0:1, :] += jnp.sum(grad * unit, axis=0, keepdims=True)
    sums_ref[1:2, :] += jnp.sum(grad, axis=0, keepdims=True)
    sums_ref[2:3, :] += jnp.sum(scaled, axis=0, keepdims=True)


def norm_bwd(values, grad, gain, shift, rest=None, scale=1.0, active=False):
    rows, width = values.shape
    block = pl.BlockSpec((NORM_ROWS, width), lambda i: (i, 0))
    line = pl.BlockSpec((1, width), lambda i: (0, 0))
    extra = [] if rest is None else [rest]
    return pl.pallas_call(
        functools.partial(norm_bwd_kernel, active, len(extra), scale),
        grid=(rows // NORM_ROWS,),
        in_specs=[block, block, line, line] + [block] * len(extra),
        out_specs=[block, block, pl.BlockSpec((8, width), lambda i: (0, 0))],
        out_shape=[
            jax.ShapeDtypeStruct((rows, width), HIGH),
            jax.ShapeDtypeStruct((rows, width), LOW),
            jax.ShapeDtypeStruct((8, width), HIGH),
        ],
        compiler_params=pltpu.CompilerParams(vmem_limit_bytes=32 * 1024 * 1024),
        cost_estimate=pl.CostEstimate(flops=30 * rows * width, bytes_accessed=18 * rows * width, transcendentals=0),
    )(values, grad, gain[None], shift[None], *extra)


def weight_grads_kernel(many, flipped, g_ref, last_ref, a_ref, b_ref, out_ref):
    step = pl.program_id(0)

    def product(grad, value):
        return (left_t(grad, value) if flipped else left_t(value, grad)).astype(LOW)

    @pl.when(step < many)
    def _():
        out_ref[...] = product(g_ref[...], a_ref[...])

    @pl.when(step == many)
    def _():
        out_ref[...] = product(last_ref[...], b_ref[...])


def weight_grads(grads, last, first_in, last_in, flipped):
    many, rows, width = grads.shape
    full = pl.BlockSpec((rows, width), lambda i: (0, 0))
    shape = ((many + 1) * width, width) if flipped else (width, (many + 1) * width)
    return pl.pallas_call(
        functools.partial(weight_grads_kernel, many, flipped),
        grid=(many + 1,),
        in_specs=[pl.BlockSpec((None, rows, width), lambda i: (jnp.minimum(i, many - 1), 0, 0)), full, full, full],
        out_specs=pl.BlockSpec((width, width), (lambda i: (i, 0)) if flipped else (lambda i: (0, i))),
        out_shape=jax.ShapeDtypeStruct(shape, LOW),
        compiler_params=pltpu.CompilerParams(vmem_limit_bytes=40 * 1024 * 1024),
        cost_estimate=pl.CostEstimate(
            flops=2 * (many + 1) * rows * width * width, bytes_accessed=4 * (many + 2) * rows * width, transcendentals=0
        ),
    )(grads, last, first_in, last_in)


def gather_weight(shard):
    pieces = lax.axis_size("rep") * lax.axis_size("seq")
    count = shard.shape[0] // pieces
    piece = lax.dynamic_slice_in_dim(shard, replica_index() * count, count, 0)
    return lax.all_gather(piece, ("fsdp",) + REPLICAS, axis=0, tiled=True)


def reduce_replicas(grad_t):
    return lax.psum_scatter(grad_t, REPLICAS, scatter_dimension=0, tiled=True)


def by_groups(part):
    groups = lax.axis_size("fsdp")
    columns, rows = part.shape
    return jnp.swapaxes(part.reshape(columns, groups, rows // groups), 0, 1)


def reduce_groups(part):
    return lax.psum_scatter(part, "fsdp", scatter_dimension=0, tiled=False)


def to_replicas(part):
    return lax.all_gather(part, REPLICAS, axis=0, tiled=False)


def swap_in(value):
    count = value.shape[0]
    rows = value.shape[1]
    me = lax.axis_index("seq")
    whole = jnp.zeros((count * rows,) + value.shape[2:], value.dtype)
    own = lax.dynamic_index_in_dim(value, me, 0, keepdims=False)
    whole = lax.dynamic_update_slice_in_dim(whole, own, me * rows, 0)
    for steps in range(1, count):
        sent = lax.dynamic_index_in_dim(value, (me + steps) % count, 0, keepdims=False)
        got = ring(sent, "seq", steps)
        whole = lax.dynamic_update_slice_in_dim(whole, got, ((me - steps) % count) * rows, 0)
    return whole


def swap_out(whole, count, kind, low=None):
    low = whole if low is None else low
    rows = whole.shape[0] // count
    me = lax.axis_index("seq")
    value = jnp.zeros((count, rows) + whole.shape[1:], kind)
    own = lax.dynamic_slice_in_dim(whole, me * rows, rows, 0)
    value = lax.dynamic_update_index_in_dim(value, own.astype(kind), me, 0)
    for steps in range(1, count):
        sent = lax.dynamic_slice_in_dim(low, ((me + steps) % count) * rows, rows, 0)
        got = ring(sent, "seq", steps)
        value = lax.dynamic_update_index_in_dim(value, got.astype(kind), (me - steps) % count, 0)
    return value


def pack_small(arrays, shard):
    gains, shifts, in_bias, out_bias, a_bias, embed, kernel = arrays
    flat = [x.reshape(-1) for x in (gains, shifts, in_bias, out_bias, a_bias, kernel, embed)]
    total = jnp.concatenate(flat)
    return jnp.pad(total, (0, -total.shape[0] % (16 * shard))).reshape(-1, shard)


def unpack_small(packed, shard):
    groups = packed.shape[0]
    wide = lambda lo, hi: jnp.swapaxes(packed[:, lo:hi], 0, 1).reshape(hi - lo, groups * shard)
    taken = 12
    gains, shifts = wide(0, 6), wide(6, 12)
    per = 4
    in_bias = jnp.swapaxes(packed[:, taken : taken + 2 * per].reshape(groups, 2, per * shard), 0, 1).reshape(2, -1)
    taken += 2 * per
    out_bias = wide(taken, taken + 2)
    a_bias = wide(taken + 2, taken + 5)
    kernel = wide(taken + 5, taken + 5 + KERNEL)
    taken += 5 + KERNEL
    buckets = LEFT + RIGHT + 1
    embed = packed[:, taken:].reshape(groups, -1)[:, : buckets * (HD // groups)].reshape(groups, buckets, HD // groups)
    return gains, shifts, in_bias, out_bias, a_bias, jnp.swapaxes(embed, 0, 1).reshape(buckets, HD), kernel


def split_small(whole, groups):
    gains, shifts, in_bias, out_bias, a_bias, embed, kernel = whole
    shard = gains.shape[1] // groups
    cut = lambda x: jnp.swapaxes(x.reshape(x.shape[0], groups, -1), 0, 1).reshape(groups, -1)
    flat = jnp.concatenate([cut(x) for x in (gains, shifts, in_bias, out_bias, a_bias, kernel, embed)], axis=1)
    flat = jnp.pad(flat, ((0, 0), (0, -flat.shape[1] % (16 * shard))))
    return flat.reshape(groups, -1, shard)


def unsplit_small(rows, shapes):
    flat = rows.reshape(-1)
    out, taken = [], 0
    for shape in shapes:
        size = shape[0] * shape[1]
        out.append(flat[taken : taken + size].reshape(shape))
        taken += size
    return out


def gather_small(value):
    groups, z = lax.axis_size("fsdp"), lax.axis_index("fsdp")
    parts = [value] + [ring(value, "fsdp", steps) for steps in range(1, groups)]
    turned = jnp.stack(parts[::-1] * 2)
    return lax.dynamic_slice_in_dim(turned, groups - 1 - z, groups, 0)


def reduce_planes(value):
    groups, z = lax.axis_size("fsdp"), lax.axis_index("fsdp")
    total = pick(value, z, 0)
    for steps in range(1, groups):
        total = total + ring(pick(value, (z + steps) % groups, 0), "fsdp", steps)
    return total


def sum_replicas(value):
    pieces = lax.axis_size("rep") * lax.axis_size("seq")
    terms = [value] + [across(value, flip) for flip in range(1, pieces)]
    while len(terms) > 1:
        terms = [a + b for a, b in zip(terms[::2], terms[1::2])]
    return terms[0]


def fast_body(inputs, cotangent, ln_gain, ln_bias, ffn_in, ffn_in_bias, ffn_out, ffn_out_bias, qkv_weight, attn_out, attn_bias, dist_embed, pw_in, depthwise, pw_out):
    micro, clips, rows, width = inputs.shape
    shard = ln_gain.shape[1]
    groups = lax.axis_size("fsdp")
    at = place()
    pieces = lax.axis_size("rep") * lax.axis_size("seq")
    small = pack_small((ln_gain, ln_bias, ffn_in_bias, ffn_out_bias, attn_bias, dist_embed, depthwise), shard)
    small = gather_small(small)
    start = swap_in(inputs.reshape(micro, rows, width))
    tie = lax.optimization_barrier
    piece, halves_in = tie((own_piece(ffn_out[0]), from_planes(own_piece(ffn_in[0]))))
    halves_out = from_planes(piece)
    near_in, halves_out, start, small = tie((around(halves_in), halves_out, start, small))
    f_in0 = assemble(at, ffn_in[0], both_cores(near_in))
    near_out = around(halves_out)
    w_attn = gather_weight(jnp.concatenate([qkv_weight, attn_out], axis=1))
    w_qkv, w_o = w_attn[:, : 3 * width], w_attn[:, 3 * width :]
    rest = gather_weight(jnp.concatenate([pw_in, pw_out, ffn_in[1]], axis=1))
    c_in, c_out, f_in1 = jnp.split(rest, [2 * width, 3 * width], axis=1)
    f_out1 = gather_weight(ffn_out[1])

    gains, shifts, f_in_b, f_out_b, a_bias, embed, kernel = unpack_small(small, shard)
    table, embed2 = bias_tables(embed)
    gains, shifts, f_in_b, f_out_b, a_bias, kernel = (x.astype(HIGH) for x in (gains, shifts, f_in_b, f_out_b, a_bias, kernel))

    def ffn_fwd(values, i, w_in, which, w_out):
        normed = norm_fwd(values, gains[which], shifts[which])
        linear = matmul(normed, w_in) + f_in_b[i]
        active, linear = tie((jax.nn.silu(linear).astype(LOW), linear.astype(LOW)))
        active, w_out = w_out(active)
        out = values.astype(HIGH) + 0.5 * (matmul(active, w_out) + f_out_b[i])
        return out, (values, normed, linear, active), w_out

    def late_weight(active):
        active_low, near = tie((active, near_out))
        return active_low, assemble(at, ffn_out[0], both_cores(near))

    def silu_bwd(grad, linear):
        gate = jax.nn.sigmoid(linear)
        return grad * (gate * (1.0 + linear * (1.0 - gate)))

    first, keep_one, f_out0 = ffn_fwd(start, 0, f_in0, 0, late_weight)
    n_two = norm_fwd(first, gains[1], shifts[1])
    proj_bias = jnp.concatenate([a_bias[0], jnp.zeros_like(a_bias[0]), a_bias[1]])
    proj = (matmul(n_two, w_qkv) + proj_bias).astype(LOW)
    mixed, lse = attn_forward_call(proj, table, width)
    second = first + matmul(mixed, w_o) + a_bias[2]
    n_three = norm_fwd(second, gains[2], shifts[2])
    pre = matmul(n_three, c_in)
    gated, pre = lax.optimization_barrier(((pre[:, :width] * jax.nn.sigmoid(pre[:, width:])).astype(LOW), pre.astype(LOW)))
    conv, cotangent = tie((conv_fwd_call(gated, kernel), cotangent))
    cot = swap_in(cotangent.reshape(micro, rows, width))
    z = norm_fwd(conv, gains[3], shifts[3], True)
    third = second + matmul(z, c_out)
    fourth, keep_four, _ = ffn_fwd(third, 1, f_in1, 4, lambda active: (active, f_out1))
    final = norm_fwd(fourth, gains[5], shifts[5])
    out_final = swap_out(final, micro, LOW)

    grad_fourth, grad_low, sums_five = norm_bwd(fourth, cot, gains[5], shifts[5], None, 0.5)
    tie = lax.optimization_barrier
    values, normed, linear, active = keep_four
    d_out1 = left_t(grad_low, active).astype(LOW)
    d_out1, grad_low = tie((d_out1, grad_low))
    p_out1 = reduce_replicas(d_out1)
    d_lin = silu_bwd(right_t(grad_low, f_out1), linear.astype(HIGH))
    d_in_b1 = jnp.sum(d_lin, axis=0)
    lin_low = tie(d_lin.astype(LOW))
    d_in1 = left_t(lin_low, normed).astype(LOW)
    lin_low, d_in1 = tie((lin_low, d_in1))
    p_in1 = reduce_replicas(d_in1)
    grad_third, grad_low, sums_four = norm_bwd(values, right_t(lin_low, f_in1), gains[4], shifts[4], grad_fourth)

    conv_low = grad_low
    grad_conv, _, sums_three = norm_bwd(conv, right_t(grad_low, c_out), gains[3], shifts[3], None, 1.0, True)
    g_pre, d_kernel = conv_bwd_call(grad_conv, gated, pre, kernel)
    d_conv = weight_grads(g_pre, conv_low, n_three, z, True)
    d_conv, g_pre, p_out1 = tie((d_conv, g_pre, p_out1))
    p_conv = reduce_replicas(d_conv)
    g_pre = jnp.concatenate([g_pre[0], g_pre[1]], axis=1)
    grad_second, grad_low, sums_two = norm_bwd(second, right_t(g_pre, c_in), gains[2], shifts[2], grad_third)

    attn_low = grad_low
    grad_mixed = right_t(grad_low, w_o).astype(LOW)
    g_proj, d_embed, d_bias = attn_backward_call(proj, mixed, lse, grad_mixed, table, embed2, width)
    d_embed = jnp.sum(d_embed.reshape(2, HD, width // 128, 128), axis=(0, 2)).T[: LEFT + RIGHT + 1]
    g_proj, p_out1, p_in1, p_conv = tie((g_proj, p_out1, p_in1, p_conv))
    strips = p_out1.reshape(p_out1.shape[0], groups, -1, width // groups).transpose(1, 2, 0, 3)
    early = jnp.concatenate([strips.reshape(groups, -1, width // groups), by_groups(p_in1), by_groups(p_conv)], axis=1)
    g_proj, early = tie((g_proj, early))
    early = reduce_groups(early)
    d_attn = weight_grads(g_proj, attn_low, n_two, mixed, True)
    d_attn, g_proj = tie((d_attn, g_proj))
    p_attn = reduce_replicas(d_attn)
    g_proj = jnp.concatenate([g_proj[0], g_proj[1], g_proj[2]], axis=1)
    grad_normed = right_t(g_proj, w_qkv)
    grad_first, grad_low, sums_one = norm_bwd(first, grad_normed, gains[1], shifts[1], grad_second, 0.5)

    values, normed, linear, active = keep_one
    d_out0 = left_t(active, grad_low).astype(LOW)
    d_out0, grad_low = tie((d_out0, grad_low))
    t_out0 = reduce_cores(at, d_out0)
    d_lin = silu_bwd(right_t(grad_low, f_out0), linear.astype(HIGH))
    d_in_b0 = jnp.sum(d_lin, axis=0)
    lin_low, t_out0, early, out_final = tie((d_lin.astype(LOW), t_out0, early, out_final))
    early = to_replicas(early)
    t_out0 = reduce_first(at, t_out0)
    d_in0 = left_t(normed, lin_low).astype(LOW)
    d_in0, lin_low, t_out0 = tie((d_in0, lin_low, t_out0))
    t_out0 = reduce_second(at, t_out0)
    t_in0 = reduce_cores(at, d_in0)
    grad_normed = right_t(lin_low, f_in0)
    grad_normed, t_out0, t_in0, p_attn = tie((grad_normed, t_out0, t_in0, p_attn))
    attn = to_replicas(reduce_groups(by_groups(p_attn)))
    t_out0 = reduce_along(at, t_out0)
    t_in0 = reduce_first(at, t_in0)
    grad_start, start_low, sums_zero = norm_bwd(values, grad_normed, gains[0], shifts[0], grad_first)
    start_low, t_out0, t_in0 = tie((start_low, t_out0, t_in0))

    sums = [sums_zero, sums_one, sums_two, sums_three, sums_four, sums_five]
    small = split_small(
        (
            jnp.stack([x[0] for x in sums]),
            jnp.stack([x[1] for x in sums]),
            jnp.stack([d_in_b0, d_in_b1]),
            jnp.stack([sums_one[2], sums_five[2]]),
            jnp.stack([d_bias[0], d_bias[1], sums_two[2]]),
            d_embed,
            d_kernel,
        ),
        groups,
    )
    near = spread_plane(t_out0)
    t_in0 = reduce_second(at, t_in0)
    small = reduce_planes(small)
    near, t_in0, start_low, small = tie((near, t_in0, start_low, small))
    t_in0 = reduce_along(at, t_in0)
    far = across(near, CORE)
    small = sum_replicas(small)
    grad_start = swap_out(grad_start, micro, HIGH, start_low)
    far, t_in0, small = tie((far, t_in0, small))
    near_in = spread_plane(t_in0)
    grad_out, grad_in, g_conv = turn_early(early, width, lin_low.shape[1])
    grad_out = finish_first(at, near, far, grad_out)
    near_in, grad_out = tie((near_in, grad_out))
    grad_in = finish_first(at, near_in, across(near_in, CORE), grad_in)
    g_qkv, g_o = turn_attn(attn, width)
    shapes = [(6, shard), (6, shard), (2, 4 * shard), (2, shard), (3, shard), (KERNEL, shard), (LEFT + RIGHT + 1, HD // groups)]
    s_gain, s_shift, s_in_b, s_out_b, s_a, s_kernel, s_embed = unsplit_small(small, shapes)
    return (
        out_final.reshape(micro, clips, rows, width),
        grad_start.reshape(micro, clips, rows, width),
        s_gain,
        s_shift,
        grad_in,
        s_in_b,
        grad_out,
        s_out_b,
        g_qkv,
        g_o,
        s_a,
        s_embed,
        g_conv[:, : 2 * width],
        s_kernel,
        g_conv[:, 2 * width :],
    )


def body(inputs, *rest):
    micro, clips, _, width = inputs.shape
    if (lax.axis_size("seq"), lax.axis_size("rep"), micro, clips) == (2, 4, 2, 1):
        return fast_body(inputs, *rest)
    return general_body(inputs, *rest)


def solution(mesh):
    return jax.shard_map(
        body,
        mesh=mesh,
        in_specs=(
            P(None, ("rep", "fsdp"), "seq", None),
            P(None, ("rep", "fsdp"), "seq", None),
            P(None, "fsdp"),
            P(None, "fsdp"),
            P(None, "fsdp", None),
            P(None, "fsdp"),
            P(None, "fsdp", None),
            P(None, "fsdp"),
            P("fsdp", None),
            P("fsdp", None),
            P(None, "fsdp"),
            P(None, "fsdp"),
            P("fsdp", None),
            P(None, "fsdp"),
            P("fsdp", None),
        ),
        out_specs=(
            P(None, ("rep", "fsdp"), "seq", None),
            P(None, ("rep", "fsdp"), "seq", None),
            P(None, "fsdp"),
            P(None, "fsdp"),
            P(None, "fsdp", None),
            P(None, "fsdp"),
            P(None, "fsdp", None),
            P(None, "fsdp"),
            P("fsdp", None),
            P("fsdp", None),
            P(None, "fsdp"),
            P(None, "fsdp"),
            P("fsdp", None),
            P(None, "fsdp"),
            P("fsdp", None),
        ),
        check_vma=False,
    )
```

```python
import functools

import jax
import jax.numpy as jnp
from jax import lax
from jax.experimental import pallas as pl
from jax.experimental.pallas import tpu as pltpu
from jax.sharding import PartitionSpec as P

H = 16
HD = 64
KERNEL = 31
LEFT = 64
RIGHT = 8


EPS = 1e-05
LOW = jnp.bfloat16
HIGH = jnp.float32


def from_behind(value, axis, steps):
    count = lax.axis_size(axis)
    first, last = (max(0, -steps), min(count, count - steps))
    return lax.ppermute(value, axis, [(source, source + steps) for source in range(first, last)])


def as_sent(array):
    return jax.tree.map(lambda a: a.astype(jnp.bfloat16) if a.dtype == jnp.float32 else a, array)


def layer_norm(values, gain, shift):
    mean = jnp.mean(values, axis=-1, keepdims=True)
    centred = values - mean
    var = jnp.mean(centred * centred, axis=-1, keepdims=True)
    return centred * lax.rsqrt(var + EPS) * gain + shift


def matmul(left, right):
    return jnp.dot(left, right, preferred_element_type=HIGH)


def left_t(left, right):
    return lax.dot_general(left, right, (((0,), (0,)), ((), ())), preferred_element_type=HIGH)


def right_t(left, right):
    return lax.dot_general(left, right, (((1,), (1,)), ((), ())), preferred_element_type=HIGH)


def fetch(shards):
    return (
        lax.all_gather(shards[0], "fsdp", axis=1, tiled=True),
        lax.all_gather(shards[1], "fsdp", axis=1, tiled=True),
        lax.all_gather(shards[2], "fsdp", axis=1, tiled=True),
        lax.all_gather(shards[3], "fsdp", axis=1, tiled=True),
        lax.all_gather(shards[4], "fsdp", axis=1, tiled=True),
        lax.all_gather(shards[5], "fsdp", axis=1, tiled=True),
        lax.all_gather(shards[6], "fsdp", axis=0, tiled=True),
        lax.all_gather(shards[7], "fsdp", axis=0, tiled=True),
        lax.all_gather(shards[8], "fsdp", axis=1, tiled=True),
        lax.all_gather(shards[9], "fsdp", axis=1, tiled=True),
        lax.all_gather(shards[10], "fsdp", axis=0, tiled=True),
        lax.all_gather(shards[11], "fsdp", axis=1, tiled=True),
        lax.all_gather(shards[12], "fsdp", axis=0, tiled=True),
    )


def unpack(whole):
    gains, shifts, f_in, f_in_b, f_out, f_out_b, w_qkv, w_o, a_bias, embed, c_in, kernel, c_out = (
        whole
    )
    return (
        gains.astype(HIGH),
        shifts.astype(HIGH),
        f_in,
        f_in_b.astype(HIGH),
        f_out,
        f_out_b.astype(HIGH),
        w_qkv,
        w_o,
        a_bias.astype(HIGH),
        embed,
        c_in,
        kernel.astype(HIGH),
        c_out,
    )


def ffn_forward(values, gain, shift, w_in, b_in, w_out, b_out):
    normed, norm_pull = jax.vjp(layer_norm, values, gain, shift)
    normed_low = normed.astype(LOW)
    linear = matmul(normed_low, w_in)
    active, act_pull = jax.vjp(lambda lin, bias: jax.nn.silu(lin + bias), linear, b_in)
    active_low = active.astype(LOW)
    out = matmul(active_low, w_out) + b_out
    return (out, (norm_pull, normed_low, act_pull, active_low))


def ffn_backward(grad, kept, w_in, w_out):
    norm_pull, normed_low, act_pull, active_low = kept
    grad_b_out = jnp.sum(grad, axis=0)
    grad_low = grad.astype(LOW)
    grad_w_out = left_t(active_low, grad_low)
    grad_active = right_t(grad_low, w_out)
    grad_lin, grad_b_in = act_pull(grad_active)
    lin_low = grad_lin.astype(LOW)
    grad_w_in = left_t(normed_low, lin_low)
    grad_normed = right_t(lin_low, w_in)
    grad_values, grad_gain, grad_shift = norm_pull(grad_normed)
    return (grad_values, (grad_gain, grad_shift, grad_w_in, grad_b_in, grad_w_out, grad_b_out))


def scores_of(query4, key4, embed, onehot):
    direct_path = jnp.einsum("cnhd,clhd->chnl", query4, key4, preferred_element_type=HIGH)
    rel_low = jnp.einsum("cnhd,bd->chnb", query4, embed, preferred_element_type=HIGH).astype(LOW)
    placed = jnp.einsum("chnb,nbl->chnl", rel_low, onehot, preferred_element_type=HIGH)
    return (direct_path + placed) * HD ** (-0.5)


def attn_forward(values, gain, shift, w_qkv, bias, embed, w_o, onehot):
    clips, rows, width = values.shape
    normed, norm_pull = jax.vjp(layer_norm, values, gain, shift)
    normed_low = normed.astype(LOW).reshape(clips * rows, width)
    proj = matmul(normed_low, w_qkv).reshape(clips, rows, 3 * width)
    query_rows = (proj[..., :width] + bias[0]).astype(LOW)
    key = proj[..., width : 2 * width].astype(LOW)
    value_rows = (proj[..., 2 * width :] + bias[1]).astype(LOW)
    keys, values_all = (
        lax.all_gather(key, "seq", axis=1, tiled=True),
        lax.all_gather(value_rows, "seq", axis=1, tiled=True),
    )
    span = keys.shape[1]
    query4 = query_rows.reshape(clips, rows, H, HD)
    key4 = keys.reshape(clips, span, H, HD)
    value4 = values_all.reshape(clips, span, H, HD)
    scores = scores_of(query4, key4, embed, onehot)
    total_log = jax.nn.logsumexp(scores, axis=-1)
    prob_low = jnp.exp(scores - total_log[..., None]).astype(LOW)
    mixed_precision = jnp.einsum("chnl,clhd->cnhd", prob_low, value4, preferred_element_type=HIGH)
    mixed_low = mixed_precision.astype(LOW).reshape(clips * rows, width)
    out = matmul(mixed_low, w_o) + bias[2]
    return (out, (norm_pull, normed_low, query4, key4, value4, total_log, mixed_low))


def attn_backward(grad, kept, w_qkv, w_o, embed, onehot):
    norm_pull, normed_low, query4, key4, value4, total_log, mixed_low = kept
    clips, rows = (query4.shape[0], query4.shape[1])
    span = key4.shape[1]
    width = H * HD
    scale = HD ** (-0.5)
    grad_b_o = jnp.sum(grad, axis=0)
    grad_low = grad.astype(LOW)
    grad_w_o = left_t(mixed_low, grad_low)
    grad_mixed = right_t(grad_low, w_o).astype(LOW).reshape(clips, rows, H, HD)
    scores = scores_of(query4, key4, embed, onehot)
    attention_probability = jnp.exp(scores - total_log[..., None])
    prob_low = attention_probability.astype(LOW)
    grad_prob = jnp.einsum("cnhd,clhd->chnl", grad_mixed, value4, preferred_element_type=HIGH)
    grad_value = jnp.einsum("chnl,cnhd->clhd", prob_low, grad_mixed, preferred_element_type=HIGH)
    grad_scores = (
        attention_probability
        * (grad_prob - jnp.sum(attention_probability * grad_prob, axis=-1, keepdims=True))
    ).astype(LOW)
    grad_rel = (
        jnp.einsum("chnl,nbl->chnb", grad_scores, onehot, preferred_element_type=HIGH) * scale
    ).astype(LOW)
    grad_query = scale * jnp.einsum(
        "chnl,clhd->cnhd", grad_scores, key4, preferred_element_type=HIGH
    )
    grad_query = grad_query + jnp.einsum(
        "chnb,bd->cnhd", grad_rel, embed, preferred_element_type=HIGH
    )
    grad_embed = jnp.einsum("chnb,cnhd->bd", grad_rel, query4, preferred_element_type=HIGH)
    grad_key = scale * jnp.einsum(
        "chnl,cnhd->clhd", grad_scores, query4, preferred_element_type=HIGH
    )
    mine_key, mine_value = (
        lax.psum_scatter(
            grad_key.reshape(clips, span, width).astype(jnp.bfloat16),
            "seq",
            scatter_dimension=1,
            tiled=True,
        ).astype(jnp.float32),
        lax.psum_scatter(
            grad_value.reshape(clips, span, width).astype(jnp.bfloat16),
            "seq",
            scatter_dimension=1,
            tiled=True,
        ).astype(jnp.float32),
    )
    grad_query = grad_query.reshape(clips, rows, width)
    grad_b_q = jnp.sum(grad_query, axis=(0, 1))
    grad_b_v = jnp.sum(mine_value, axis=(0, 1))
    grad_proj = (
        jnp.concatenate([grad_query, mine_key, mine_value], axis=-1)
        .astype(LOW)
        .reshape(clips * rows, 3 * width)
    )
    grad_w_qkv = left_t(normed_low, grad_proj)
    grad_normed = right_t(grad_proj, w_qkv).reshape(clips, rows, width)
    grad_values, grad_gain, grad_shift = norm_pull(grad_normed)
    grad_bias = jnp.stack([grad_b_q, grad_b_v, grad_b_o])
    return (
        grad_values.reshape(clips * rows, width),
        (grad_gain, grad_shift, grad_w_qkv, grad_bias, grad_embed, grad_w_o),
    )


def depthwise_block(extended, kernel, gain, shift):
    taps = kernel.shape[0]
    span = extended.shape[1] - taps + 1
    total = kernel[0] * extended[:, 0:span, :]
    for tap in range(1, taps):
        total = total + kernel[tap] * extended[:, tap : tap + span, :]
    return jax.nn.silu(layer_norm(total, gain, shift))


def conv_forward(values, gain, shift, w_in, kernel, gain_two, shift_two, w_out):
    clips, rows, width = values.shape
    normed, norm_pull = jax.vjp(layer_norm, values, gain, shift)
    normed_low = normed.astype(LOW).reshape(clips * rows, width)
    pre = matmul(normed_low, w_in).reshape(clips, rows, 2 * width)
    gated, gate_pull = jax.vjp(
        lambda both: both[..., :width] * jax.nn.sigmoid(both[..., width:]), pre
    )
    gated_low = gated.astype(LOW)
    rim = from_behind(gated_low[:, rows - (KERNEL - 1) :, :], "seq", 1)
    extended = jnp.concatenate([rim, gated_low], axis=1).astype(HIGH)
    mixed_precision, mix_pull = jax.vjp(depthwise_block, extended, kernel, gain_two, shift_two)
    mixed_low = mixed_precision.astype(LOW).reshape(clips * rows, width)
    out = matmul(mixed_low, w_out)
    return (out, (norm_pull, normed_low, gate_pull, mix_pull, mixed_low))


def conv_backward(grad, kept, w_in, w_out, clips, rows):
    norm_pull, normed_low, gate_pull, mix_pull, mixed_low = kept
    width = grad.shape[1]
    grad_low = grad.astype(LOW)
    grad_w_out = left_t(mixed_low, grad_low)
    grad_mixed = right_t(grad_low, w_out).reshape(clips, rows, width)
    grad_ext, grad_kernel, grad_gain_two, grad_shift_two = mix_pull(grad_mixed)
    returned = from_behind(grad_ext[:, : KERNEL - 1, :].astype(jnp.bfloat16), "seq", -1).astype(
        jnp.float32
    )
    grad_gated = grad_ext[:, KERNEL - 1 :, :] + jnp.pad(
        returned, ((0, 0), (rows - (KERNEL - 1), 0), (0, 0))
    )
    (grad_pre,) = gate_pull(grad_gated)
    pre_low = grad_pre.astype(LOW).reshape(clips * rows, 2 * width)
    grad_w_in = left_t(normed_low, pre_low)
    grad_normed = right_t(pre_low, w_in).reshape(clips, rows, width)
    grad_values, grad_gain, grad_shift = norm_pull(grad_normed)
    return (
        grad_values.reshape(clips * rows, width),
        (grad_gain, grad_shift, grad_w_in, grad_kernel, grad_gain_two, grad_shift_two, grad_w_out),
    )


def general_body(
    inputs,
    cotangent,
    ln_gain,
    ln_bias,
    ffn_in,
    ffn_in_bias,
    ffn_out,
    ffn_out_bias,
    qkv_weight,
    attn_out,
    attn_bias,
    dist_embed,
    pw_in,
    depthwise,
    pw_out,
):
    shards = (
        ln_gain,
        ln_bias,
        ffn_in,
        ffn_in_bias,
        ffn_out,
        ffn_out_bias,
        qkv_weight,
        attn_out,
        attn_bias,
        dist_embed,
        pw_in,
        depthwise,
        pw_out,
    )
    micro, clips, rows, width = inputs.shape
    span = rows * lax.axis_size("seq")
    positions = lax.axis_index("seq") * rows + jnp.arange(rows, dtype=jnp.int32)
    bucket = (
        jnp.clip(jnp.arange(span, dtype=jnp.int32)[None, :] - positions[:, None], -LEFT, RIGHT)
        + LEFT
    )
    onehot = (
        bucket[:, None, :] == jnp.arange(LEFT + RIGHT + 1, dtype=jnp.int32)[None, :, None]
    ).astype(LOW)
    outputs = []
    input_grads = []
    totals = None
    for step in range(micro):
        whole = fetch(shards)
        (
            gains,
            shifts,
            f_in,
            f_in_b,
            f_out,
            f_out_b,
            w_qkv,
            w_o,
            a_bias,
            embed,
            c_in,
            kernel,
            c_out,
        ) = unpack(whole)
        start_rows = inputs[step].astype(HIGH).reshape(clips * rows, width)
        branch_one, keep_one = ffn_forward(
            start_rows, gains[0], shifts[0], f_in[0], f_in_b[0], f_out[0], f_out_b[0]
        )
        first = start_rows + 0.5 * branch_one
        branch_two, keep_two = attn_forward(
            first.reshape(clips, rows, width),
            gains[1],
            shifts[1],
            w_qkv,
            a_bias,
            embed,
            w_o,
            onehot,
        )
        second = first + branch_two
        branch_three, keep_three = conv_forward(
            second.reshape(clips, rows, width),
            gains[2],
            shifts[2],
            c_in,
            kernel,
            gains[3],
            shifts[3],
            c_out,
        )
        third = second + branch_three
        branch_four, keep_four = ffn_forward(
            third, gains[4], shifts[4], f_in[1], f_in_b[1], f_out[1], f_out_b[1]
        )
        fourth = third + 0.5 * branch_four
        final, final_pull = jax.vjp(layer_norm, fourth, gains[5], shifts[5])
        outputs.append(final.astype(LOW).reshape(clips, rows, width))
        again = (
            lax.all_gather(shards[0], "fsdp", axis=1, tiled=True),
            lax.all_gather(shards[1], "fsdp", axis=1, tiled=True),
            lax.all_gather(shards[2], "fsdp", axis=1, tiled=True),
            lax.all_gather(shards[3], "fsdp", axis=1, tiled=True),
            lax.all_gather(shards[4], "fsdp", axis=1, tiled=True),
            lax.all_gather(shards[5], "fsdp", axis=1, tiled=True),
            lax.all_gather(shards[6], "fsdp", axis=0, tiled=True),
            lax.all_gather(shards[7], "fsdp", axis=0, tiled=True),
            lax.all_gather(shards[8], "fsdp", axis=1, tiled=True),
            lax.all_gather(shards[9], "fsdp", axis=1, tiled=True),
            lax.all_gather(shards[10], "fsdp", axis=0, tiled=True),
            lax.all_gather(shards[11], "fsdp", axis=1, tiled=True),
            lax.all_gather(shards[12], "fsdp", axis=0, tiled=True),
        )
        (
            gains,
            shifts,
            f_in,
            f_in_b,
            f_out,
            f_out_b,
            w_qkv,
            w_o,
            a_bias,
            embed,
            c_in,
            kernel,
            c_out,
        ) = unpack(again)
        grad_fourth, gain_five, shift_five = final_pull(
            cotangent[step].astype(HIGH).reshape(clips * rows, width)
        )
        grad_inner, four_grads = ffn_backward(0.5 * grad_fourth, keep_four, f_in[1], f_out[1])
        grad_third = grad_fourth + grad_inner
        grad_inner, three_grads = conv_backward(grad_third, keep_three, c_in, c_out, clips, rows)
        grad_second = grad_third + grad_inner
        grad_inner, two_grads = attn_backward(grad_second, keep_two, w_qkv, w_o, embed, onehot)
        grad_first = grad_second + grad_inner
        grad_inner, one_grads = ffn_backward(0.5 * grad_first, keep_one, f_in[0], f_out[0])
        input_grads.append((grad_first + grad_inner).reshape(clips, rows, width))
        grads = (
            jnp.stack(
                [
                    one_grads[0],
                    two_grads[0],
                    three_grads[0],
                    three_grads[4],
                    four_grads[0],
                    gain_five,
                ]
            ),
            jnp.stack(
                [
                    one_grads[1],
                    two_grads[1],
                    three_grads[1],
                    three_grads[5],
                    four_grads[1],
                    shift_five,
                ]
            ),
            jnp.stack([one_grads[2], four_grads[2]]),
            jnp.stack([one_grads[3], four_grads[3]]),
            jnp.stack([one_grads[4], four_grads[4]]),
            jnp.stack([one_grads[5], four_grads[5]]),
            two_grads[2],
            two_grads[5],
            two_grads[3],
            two_grads[4],
            three_grads[2],
            three_grads[3],
            three_grads[6],
        )
        totals = grads if totals is None else jax.tree.map(jnp.add, totals, grads)
    totals = (
        lax.psum_scatter(
            totals[0].astype(jnp.bfloat16), "fsdp", scatter_dimension=1, tiled=True
        ).astype(jnp.float32),
        lax.psum_scatter(
            totals[1].astype(jnp.bfloat16), "fsdp", scatter_dimension=1, tiled=True
        ).astype(jnp.float32),
        lax.psum_scatter(
            totals[2].astype(jnp.bfloat16), "fsdp", scatter_dimension=1, tiled=True
        ).astype(jnp.float32),
        lax.psum_scatter(
            totals[3].astype(jnp.bfloat16), "fsdp", scatter_dimension=1, tiled=True
        ).astype(jnp.float32),
        lax.psum_scatter(
            totals[4].astype(jnp.bfloat16), "fsdp", scatter_dimension=1, tiled=True
        ).astype(jnp.float32),
        lax.psum_scatter(
            totals[5].astype(jnp.bfloat16), "fsdp", scatter_dimension=1, tiled=True
        ).astype(jnp.float32),
        lax.psum_scatter(
            totals[6].astype(jnp.bfloat16), "fsdp", scatter_dimension=0, tiled=True
        ).astype(jnp.float32),
        lax.psum_scatter(
            totals[7].astype(jnp.bfloat16), "fsdp", scatter_dimension=0, tiled=True
        ).astype(jnp.float32),
        lax.psum_scatter(
            totals[8].astype(jnp.bfloat16), "fsdp", scatter_dimension=1, tiled=True
        ).astype(jnp.float32),
        lax.psum_scatter(
            totals[9].astype(jnp.bfloat16), "fsdp", scatter_dimension=1, tiled=True
        ).astype(jnp.float32),
        lax.psum_scatter(
            totals[10].astype(jnp.bfloat16), "fsdp", scatter_dimension=0, tiled=True
        ).astype(jnp.float32),
        lax.psum_scatter(
            totals[11].astype(jnp.bfloat16), "fsdp", scatter_dimension=1, tiled=True
        ).astype(jnp.float32),
        lax.psum_scatter(
            totals[12].astype(jnp.bfloat16), "fsdp", scatter_dimension=0, tiled=True
        ).astype(jnp.float32),
    )
    summed = jax.tree.map(
        lambda part: part.astype(jnp.float32), lax.psum(as_sent(totals), ("rep", "seq"))
    )
    return (
        jnp.stack(outputs),
        jnp.stack(input_grads),
        summed[0],
        summed[1],
        summed[2],
        summed[3],
        summed[4],
        summed[5],
        summed[6],
        summed[7],
        summed[8],
        summed[9],
        summed[10],
        summed[11],
        summed[12],
    )


SUB = 128
PAD = 128
FWD_ROWS = 512
BWD_ROWS = 1024


def dot(a, b):
    return lax.dot_general(a, b, (((1,), (0,)), ((), ())), preferred_element_type=HIGH)


def dot_nt(a, b):
    return lax.dot_general(a, b, (((1,), (1,)), ((), ())), preferred_element_type=HIGH)


def biased_scores(qs, table, kcat, s_ref, first, span):
    count = qs.shape[0]
    rel = dot_nt(qs, table).astype(LOW).astype(HIGH)
    lane = lax.broadcasted_iota(jnp.int32, (count, 128), 1)
    block = first + lax.broadcasted_iota(jnp.int32, (count, 128), 0) // SUB
    far = jnp.where(lane < block - 1, rel[:, 384:512], jnp.where(lane > block + 1, rel[:, 128:256], 0.0))
    s_ref[:, PAD : PAD + span] = dot_nt(jnp.concatenate([qs, far.astype(LOW)], axis=1), kcat)
    for sub in range(count // SUB):
        rows = slice(sub * SUB, (sub + 1) * SUB)
        band = pltpu.roll(rel[rows], LEFT, 1, stride=1, stride_axis=0)
        at = pl.multiple_of((first + sub) * SUB, 128)
        s_ref[rows, pl.ds(at, 384)] += band[:, :384]


def blocks_onehot(span):
    row = lax.broadcasted_iota(jnp.int32, (span, 128), 0)
    lane = lax.broadcasted_iota(jnp.int32, (span, 128), 1)
    return (row // SUB == lane).astype(HIGH).astype(LOW)


def attn_fwd_kernel(q_ref, k_ref, v_ref, table_ref, o_ref, lse_ref, kcat, vcat, s_ref):
    span = k_ref.shape[0]
    kcat[:, :128] = k_ref[...]
    kcat[:, 128:] = blocks_onehot(span)
    vcat[:, :128] = v_ref[...]
    vcat[:, 128:] = jnp.ones((span, 128), LOW)
    lane = lax.broadcasted_iota(jnp.int32, (FWD_ROWS, 128), 1)

    def body(qb, carry):
        rows = pl.ds(pl.multiple_of(qb * FWD_ROWS, FWD_ROWS), FWD_ROWS)
        q = q_ref[rows, :].astype(HIGH) * (HD**-0.5)
        outs, logs = [], []
        for h in range(2):
            mine = (lane < HD) if h == 0 else (lane >= HD)
            qs = jnp.where(mine, q, 0.0).astype(LOW)
            sr = s_ref.at[h]
            biased_scores(qs, table_ref[...], kcat[...], sr, qb * (FWD_ROWS // SUB), span)
        for h in range(2):
            s = s_ref[h, :, PAD : PAD + span]
            top = jnp.max(s, axis=-1, keepdims=True)
            p = jnp.exp(s - top).astype(LOW)
            mixed = dot(p, vcat[...])
            total = mixed[:, 128:]
            outs.append(mixed[:, :128] / total)
            logs.append(top + jnp.log(total))
        o_ref[rows, :] = jnp.where(lane < HD, outs[0], outs[1]).astype(o_ref.dtype)
        lse_ref[rows, :] = jnp.where(lane < HD, logs[0], logs[1])
        return carry

    lax.fori_loop(0, q_ref.shape[0] // FWD_ROWS, body, 0)


def attn_forward_call(proj, table, width):
    rows = proj.shape[0]
    pairs = width // 128
    col = lambda off: pl.BlockSpec((rows, 128), lambda h: (0, off * pairs + h))
    return pl.pallas_call(
        attn_fwd_kernel,
        grid=(pairs,),
        in_specs=[col(0), col(1), col(2), pl.BlockSpec((512, 128), lambda h: (0, 0))],
        out_specs=[pl.BlockSpec((rows, 128), lambda h: (0, h))] * 2,
        out_shape=[jax.ShapeDtypeStruct((rows, width), LOW), jax.ShapeDtypeStruct((rows, width), HIGH)],
        scratch_shapes=[
            pltpu.VMEM((rows, 256), LOW),
            pltpu.VMEM((rows, 256), LOW),
            pltpu.VMEM((2, FWD_ROWS, rows + 2 * PAD), HIGH),
        ],
        compiler_params=pltpu.CompilerParams(vmem_limit_bytes=40 * 1024 * 1024),
        cost_estimate=pl.CostEstimate(
            flops=16 * rows * rows * width, bytes_accessed=12 * rows * width, transcendentals=rows * rows * 16
        ),
    )(proj, proj, proj, table)


def attn_bwd_kernel(q_ref, k_ref, v_ref, o_ref, lse_ref, do_ref, table_ref, embed_ref,
                    g_ref, dembed_ref, bias_ref, kcat, qt, dot_t, dkt, dvt, s_ref):
    span = k_ref.shape[0]
    count = BWD_ROWS
    kcat[:, :128] = k_ref[...]
    kcat[:, 128:] = blocks_onehot(span)
    qt[...] = (q_ref[...].astype(HIGH) * (HD**-0.5)).T.astype(LOW)
    dot_t[...] = do_ref[...].astype(HIGH).T.astype(LOW)
    dkt[...] = jnp.zeros_like(dkt)
    dvt[...] = jnp.zeros_like(dvt)
    lane = lax.broadcasted_iota(jnp.int32, (count, 128), 1)
    block_of = lax.broadcasted_iota(jnp.int32, (count, 128), 0) // SUB
    column = lax.broadcasted_iota(jnp.int32, (SUB, 384), 1)
    last = q_ref.shape[0] // SUB - 1
    turn = lax.broadcasted_iota(jnp.int32, (SUB, SUB), 0) + lax.broadcasted_iota(jnp.int32, (SUB, SUB), 1)
    flip = (turn == SUB - 1).astype(HIGH).astype(LOW)
    lane_sub = lax.broadcasted_iota(jnp.int32, (SUB, 128), 1)
    edge = LEFT + RIGHT

    def body(qb, carry):
        dembed, dbias = carry
        first = qb * (count // SUB)
        rows = pl.ds(pl.multiple_of(qb * count, count), count)
        q = q_ref[rows, :].astype(HIGH) * (HD**-0.5)
        grad = do_ref[rows, :].astype(HIGH)
        lse2 = lse_ref[rows, :]
        weighted = grad * o_ref[rows, :].astype(HIGH)
        block = first + block_of
        dqs, news = [], []
        for h in range(2):
            mine = (lane < HD) if h == 0 else (lane >= HD)
            qs = jnp.where(mine, q, 0.0).astype(LOW)
            biased_scores(qs, table_ref[...], kcat[...], s_ref.at[h], first, span)
        for h in range(2):
            mine = (lane < HD) if h == 0 else (lane >= HD)
            part = slice(h * HD, (h + 1) * HD)
            sr = s_ref.at[h]
            lse = lse2[:, h * HD : h * HD + 1]
            p = jnp.exp(sr[:, PAD : PAD + span] - lse)
            delta = jnp.sum(jnp.where(mine, weighted, 0.0), axis=-1, keepdims=True)
            gs = jnp.where(mine, grad, 0.0).astype(LOW)
            ds = p * (dot_nt(gs, v_ref[...]) - delta)
            sr[:, PAD : PAD + span] = ds
            ds_low = ds.astype(LOW)
            dq = dot(ds_low, kcat[...])
            dvt[part, :] += dot(dot_t[part, rows], p.astype(LOW))
            dkt[part, :] += dot(qt[part, rows], ds_low)
            tables = []
            for sub in range(count // SUB):
                band = sr[sub * SUB : (sub + 1) * SUB, pl.ds(pl.multiple_of((first + sub) * SUB, 128), 384)]
                if sub == 0:
                    band = jnp.where((column < 128) & (first == 0), 0.0, band)
                if sub == count // SUB - 1:
                    band = jnp.where((column >= 256) & (first + sub == last), 0.0, band)
                turned = dot(flip, band.astype(LOW))
                turned = jnp.concatenate([turned, jnp.zeros((SUB, 128), HIGH)], axis=1)
                drel = pltpu.roll(turned, 512 - LEFT - SUB + 1, 1, stride=1, stride_axis=0)
                near, middle = drel[:, :128], drel[:, 256:384]
                left = jnp.sum(drel[:, 384:512] + jnp.where(lane_sub >= 64, middle, 0.0), axis=-1, keepdims=True)
                right = jnp.sum(
                    drel[:, 128:256] + jnp.where(lane_sub < 64, middle, 0.0) + jnp.where(lane_sub >= edge, near, 0.0),
                    axis=-1,
                    keepdims=True,
                )
                left_top, right_top = left.astype(LOW).astype(HIGH), right.astype(LOW).astype(HIGH)
                packed = jnp.where(lane_sub < edge, near, 0.0)
                for at, value in ((80, left_top), (81, left - left_top), (82, right_top), (83, right - right_top)):
                    packed = jnp.where(lane_sub == at, value, packed)
                tables.append(dot(flip, packed.astype(LOW)))
            table = jnp.concatenate(tables, axis=0)
            sums = dq[:, 128:]
            left = jnp.sum(jnp.where(lane < block - 1, sums, 0.0) + jnp.where((lane == 80) | (lane == 81), table, 0.0), axis=-1, keepdims=True)
            right = jnp.sum(jnp.where(lane > block + 1, sums, 0.0) + jnp.where((lane == 82) | (lane == 83), table, 0.0), axis=-1, keepdims=True)
            drl = jnp.where(lane < edge, table, 0.0) + jnp.where(lane == 0, left, 0.0) + jnp.where(lane == edge, right, 0.0)
            drl = drl.astype(LOW)
            dqs.append((dq[:, :128] + dot(drl, embed_ref[...])) * (HD**-0.5))
            news.append(dembed[part] + dot(qt[part, rows], drl))
        dq = jnp.where(lane < HD, dqs[0], dqs[1])
        g_ref[0, rows, :] = dq.astype(LOW)
        return (jnp.concatenate(news, axis=0), dbias + jnp.sum(dq, axis=0, keepdims=True))

    start = (jnp.zeros((128, 128), HIGH), jnp.zeros((1, 128), HIGH))
    dembed, dbias = lax.fori_loop(0, q_ref.shape[0] // count, body, start)
    dembed_ref[...] = dembed
    g_ref[1, :, :] = dkt[...].T.astype(LOW)
    dv = dvt[...].T
    g_ref[2, :, :] = dv.astype(LOW)
    row8 = lax.broadcasted_iota(jnp.int32, (8, 128), 0)
    bias_ref[...] = jnp.where(row8 == 0, dbias, jnp.where(row8 == 1, jnp.sum(dv, axis=0, keepdims=True), 0.0))


def attn_backward_call(proj, mixed, lse, grad_mixed, table, embed2, width):
    rows = proj.shape[0]
    pairs = width // 128
    col = lambda off: pl.BlockSpec((rows, 128), lambda h: (0, off * pairs + h))
    return pl.pallas_call(
        attn_bwd_kernel,
        grid=(pairs,),
        in_specs=[
            col(0), col(1), col(2), col(0), col(0), col(0),
            pl.BlockSpec((512, 128), lambda h: (0, 0)),
            pl.BlockSpec((128, 128), lambda h: (0, 0)),
        ],
        out_specs=[
            pl.BlockSpec((3, rows, 128), lambda h: (0, 0, h)),
            pl.BlockSpec((128, 128), lambda h: (0, h)),
            pl.BlockSpec((8, 128), lambda h: (0, h)),
        ],
        out_shape=[
            jax.ShapeDtypeStruct((3, rows, width), LOW),
            jax.ShapeDtypeStruct((128, width), HIGH),
            jax.ShapeDtypeStruct((8, width), HIGH),
        ],
        scratch_shapes=[
            pltpu.VMEM((rows, 256), LOW),
            pltpu.VMEM((128, rows), LOW),
            pltpu.VMEM((128, rows), LOW),
            pltpu.VMEM((128, rows), HIGH),
            pltpu.VMEM((128, rows), HIGH),
            pltpu.VMEM((2, BWD_ROWS, rows + 2 * PAD), HIGH),
        ],
        compiler_params=pltpu.CompilerParams(vmem_limit_bytes=48 * 1024 * 1024),
        cost_estimate=pl.CostEstimate(
            flops=40 * rows * rows * width, bytes_accessed=24 * rows * width, transcendentals=rows * rows * 16
        ),
    )(proj, proj, proj, mixed, lse, grad_mixed, table, embed2)


def bias_tables(embed):
    last = LEFT + RIGHT
    tail = jnp.broadcast_to(embed[last:], (320 - last - 1, HD))
    head = jnp.broadcast_to(embed[:1], (192, HD))
    table = jnp.concatenate([embed, tail, head], axis=0)
    pair = jnp.concatenate([table, table], axis=1)
    return pair, pair[:128]


CONV_ROWS = 64
EDGE = 32


def conv_fwd_kernel(u_ref, w_ref, m_ref, padded):
    rows = u_ref.shape[0]
    padded[:EDGE, :] = jnp.zeros((EDGE, 128), HIGH)
    padded[EDGE:, :] = u_ref[...].astype(HIGH)

    def chunk(i, carry):
        start = pl.multiple_of(i * CONV_ROWS, CONV_ROWS)
        total = jnp.zeros((CONV_ROWS, 128), HIGH)
        for tap in range(KERNEL):
            total += w_ref[tap : tap + 1, :] * padded[pl.ds(start + (EDGE - KERNEL + 1 + tap), CONV_ROWS), :]
        m_ref[pl.ds(start, CONV_ROWS), :] = total
        return carry

    lax.fori_loop(0, rows // CONV_ROWS, chunk, 0)


def conv_fwd_call(u, kernel):
    rows, width = u.shape
    return pl.pallas_call(
        conv_fwd_kernel,
        grid=(width // 128,),
        in_specs=[pl.BlockSpec((rows, 128), lambda c: (0, c)), pl.BlockSpec((KERNEL, 128), lambda c: (0, c))],
        out_specs=pl.BlockSpec((rows, 128), lambda c: (0, c)),
        out_shape=jax.ShapeDtypeStruct((rows, width), HIGH),
        scratch_shapes=[pltpu.VMEM((rows + EDGE, 128), HIGH)],
        cost_estimate=pl.CostEstimate(flops=62 * rows * width, bytes_accessed=6 * rows * width, transcendentals=0),
    )(u, kernel)


def conv_bwd_kernel(dm_ref, u_ref, pre_a_ref, pre_b_ref, w_ref, g_ref, dw_ref, padded, acc):
    rows = u_ref.shape[0]
    padded[:rows, :] = dm_ref[...]
    padded[rows:, :] = jnp.zeros((EDGE, 128), HIGH)
    acc[...] = jnp.zeros_like(acc)

    def chunk(i, carry):
        start = pl.multiple_of(i * CONV_ROWS, CONV_ROWS)
        at = pl.ds(start, CONV_ROWS)
        u = u_ref[at, :].astype(HIGH)
        total = jnp.zeros((CONV_ROWS, 128), HIGH)
        for tap in range(KERNEL):
            later = padded[pl.ds(start + (KERNEL - 1 - tap), CONV_ROWS), :]
            total += w_ref[tap : tap + 1, :] * later
            acc[tap] += jnp.sum((u * later).reshape(CONV_ROWS // 8, 8, 128), axis=0)
        gate = jax.nn.sigmoid(pre_b_ref[at, :].astype(HIGH))
        through = total * gate
        g_ref[0, at, :] = through.astype(LOW)
        g_ref[1, at, :] = (through * pre_a_ref[at, :].astype(HIGH) * (1.0 - gate)).astype(LOW)
        return carry

    lax.fori_loop(0, rows // CONV_ROWS, chunk, 0)
    dw_ref[...] = jnp.sum(acc[...], axis=1)


def conv_bwd_call(dm, u, pre, kernel):
    rows, width = u.shape
    cols = width // 128
    block = pl.BlockSpec((rows, 128), lambda c: (0, c))
    taps = pl.BlockSpec((KERNEL, 128), lambda c: (0, c))
    return pl.pallas_call(
        conv_bwd_kernel,
        grid=(cols,),
        in_specs=[block, block, block, pl.BlockSpec((rows, 128), lambda c: (0, cols + c)), taps],
        out_specs=[pl.BlockSpec((2, rows, 128), lambda c: (0, 0, c)), taps],
        out_shape=[jax.ShapeDtypeStruct((2, rows, width), LOW), jax.ShapeDtypeStruct((KERNEL, width), HIGH)],
        scratch_shapes=[pltpu.VMEM((rows + EDGE, 128), HIGH), pltpu.VMEM((KERNEL, 8, 128), HIGH)],
        cost_estimate=pl.CostEstimate(flops=124 * rows * width, bytes_accessed=14 * rows * width, transcendentals=rows * width),
    )(dm, u, pre, pre, kernel)


REPLICAS = ("rep", "seq")
X_FLIP, CORE_FLIP = 2, 1


def replica_index():
    return lax.axis_index("rep") * lax.axis_size("seq") + lax.axis_index("seq")


def hop(value, axis, flip):
    return lax.ppermute(value, axis, [(i, i ^ flip) for i in range(lax.axis_size(axis))])


def ring(value, axis, steps):
    count = lax.axis_size(axis)
    return lax.ppermute(value, axis, [(i, (i + steps) % count) for i in range(count)])


def place():
    rep = lax.axis_index("rep")
    return jnp.stack([rep // 2, rep % 2, lax.axis_index("seq"), lax.axis_index("fsdp")]).astype(jnp.int32)


def spread_blocks(x, core, y):
    for other in range(2):
        for half, moved, array in ((0, 0, 0), (0, 1, 1), (1, 0, 2), (1, 1, 3)):
            for entry in range(2):
                if half == 0:
                    flip_x, flip_y = entry, moved
                else:
                    flip_x, flip_y = moved, entry
                yield other * 4 + array, entry, half, x ^ flip_x, core ^ other, y ^ flip_y


def assemble_kernel(planes, at_ref, shard_ref, *refs):
    parts = refs[:8]
    out_ref, sems = refs[8:]
    x, core, y, z = (at_ref[i] for i in range(4))
    half_rows = parts[0].shape[-2]
    rows = 16 * half_rows
    copies = [(shard_ref, out_ref.at[pl.ds(pl.multiple_of(z * rows, rows), rows), :])]
    for array, entry, half, bx, bc, by in spread_blocks(x, core, y):
        for plane in range(planes):
            base = lax.rem(z + (planes - plane), planes + 1) * rows
            row = base + (((bx * 2 + bc) * 2 + by) * 2 + half) * half_rows
            copies.append((parts[array].at[entry, plane], out_ref.at[pl.ds(pl.multiple_of(row, half_rows), half_rows), :]))
    started = [pltpu.make_async_copy(source, target, sems.at[i]) for i, (source, target) in enumerate(copies)]
    for copy in started:
        copy.start()
    for copy in started:
        copy.wait()


def assemble(at, shard, parts):
    planes, half_rows, columns = parts[0].shape[1:]
    rows = 16 * half_rows * (planes + 1)
    return pl.pallas_call(
        functools.partial(assemble_kernel, planes),
        in_specs=[pl.BlockSpec(memory_space=pltpu.SMEM)] + [pl.BlockSpec(memory_space=pl.ANY)] * 9,
        out_specs=pl.BlockSpec(memory_space=pltpu.VMEM),
        out_shape=jax.ShapeDtypeStruct((rows, columns), LOW),
        scratch_shapes=[pltpu.SemaphoreType.DMA((16 * planes + 1,))],
        compiler_params=pltpu.CompilerParams(vmem_limit_bytes=12 * 1024 * 1024),
        cost_estimate=pl.CostEstimate(flops=0, bytes_accessed=4 * rows * columns, transcendentals=0),
    )(at, shard, *parts)


def own_piece(shard):
    count = shard.shape[0] // (lax.axis_size("rep") * lax.axis_size("seq"))
    return lax.dynamic_slice_in_dim(shard, replica_index() * count, count, 0)


def from_planes(piece):
    got = [ring(piece, "fsdp", steps) for steps in range(1, lax.axis_size("fsdp"))]
    half = piece.shape[0] // 2
    return jnp.stack([g[:half] for g in got]), jnp.stack([g[half:] for g in got])


def around(halves):
    first, second = halves
    first_x, second_y = hop(first, "rep", X_FLIP), hop(second, "seq", 1)
    first, second = jnp.stack([first, first_x]), jnp.stack([second, second_y])
    first_y, second_x = hop(first, "seq", 1), hop(second, "rep", X_FLIP)
    return [first, first_y, second, second_x]


def both_cores(near):
    return near + [hop(value, "rep", CORE_FLIP) for value in near]


def plus(a, b):
    return (a.astype(HIGH) + b.astype(HIGH)).astype(LOW)


def pick(value, index, axis):
    return lax.dynamic_index_in_dim(value, index, axis, keepdims=False)


X, Y, CORE = 4, 1, 2


def across(value, flip):
    pieces = lax.axis_size("rep") * lax.axis_size("seq")
    return lax.ppermute(value, REPLICAS, [(i, i ^ flip) for i in range(pieces)])


def reduce_cores(at, grad):
    groups = lax.axis_size("fsdp")
    rows, columns = grad.shape
    parts = grad.reshape(groups, 2, 2, 2, rows // (8 * groups), columns)
    return plus(pick(parts, at[1], 2), across(pick(parts, 1 - at[1], 2), CORE))


def reduce_first(at, total):
    x, y = at[0], at[2]
    half = total.shape[3] // 2
    first, second = total[:, :, :, :half], total[:, :, :, half:]
    first = plus(pick(first, x, 1), across(pick(first, 1 - x, 1), X))
    second = plus(pick(second, y, 2), across(pick(second, 1 - y, 2), Y))
    return first, second


def reduce_second(at, halves):
    x, y = at[0], at[2]
    first, second = halves
    first = plus(pick(first, y, 1), across(pick(first, 1 - y, 1), Y))
    second = plus(pick(second, x, 1), across(pick(second, 1 - x, 1), X))
    return jnp.concatenate([first, second], axis=1)


def reduce_along(at, part):
    groups, z = lax.axis_size("fsdp"), at[3]
    total = pick(part, z, 0).astype(HIGH)
    for steps in range(1, groups):
        total = total + ring(pick(part, (z + steps) % groups, 0), "fsdp", steps).astype(HIGH)
    return total.astype(LOW)


def spread_plane(part):
    return jnp.stack([part] + [across(part, flip) for flip in (X, Y, X + Y)])


def finish_kernel(at_ref, near_ref, far_ref, whole_ref, out_ref):
    step = pl.program_id(0)

    @pl.when(step < 4)
    def _():
        out_ref[...] = near_ref[...].astype(HIGH)

    @pl.when(step >= 4)
    def _():
        out_ref[...] = far_ref[...].astype(HIGH)


def finish_place(step, at):
    x, core, y = at[0], at[1], at[2]
    entry = step % 4
    return ((x ^ (entry % 2)) * 2 + (core ^ (step // 4))) * 2 + (y ^ (entry // 2))


def finish_first(at, near, far, whole):
    _, rows, columns = near.shape
    return pl.pallas_call(
        finish_kernel,
        grid_spec=pltpu.PrefetchScalarGridSpec(
            num_scalar_prefetch=1,
            grid=(8,),
            in_specs=[
                pl.BlockSpec((1, rows, columns), lambda i, at: (jnp.minimum(i, 3), 0, 0)),
                pl.BlockSpec((1, rows, columns), lambda i, at: (jnp.maximum(i - 4, 0), 0, 0)),
                pl.BlockSpec(memory_space=pl.ANY),
            ],
            out_specs=pl.BlockSpec((1, rows, columns), lambda i, at: (0, finish_place(i, at), 0)),
        ),
        out_shape=jax.ShapeDtypeStruct(whole.shape, HIGH),
        input_output_aliases={3: 0},
        cost_estimate=pl.CostEstimate(flops=0, bytes_accessed=48 * rows * columns, transcendentals=0),
    )(at, near, far, whole)


def turn_early_kernel(count, part_ref, out_ref, in_ref, conv_ref):
    shard, columns = part_ref.shape[2], out_ref.shape[2]
    for block in range(count):
        rows = slice(block * columns, (block + 1) * columns)
        out_ref[0, block * shard : (block + 1) * shard, :] = part_ref[0, rows, :].astype(HIGH).T
    edge = count * columns
    middle = edge + in_ref.shape[2]
    in_ref[0] = part_ref[0, edge:middle, :].astype(HIGH).T
    conv_ref[...] = part_ref[0, middle:, :].astype(HIGH).T


def turn_early(part, width, hidden):
    replicas, total, shard = part.shape
    count = hidden // width
    inner = total - (width + hidden) // replicas
    return pl.pallas_call(
        functools.partial(turn_early_kernel, count),
        grid=(replicas,),
        in_specs=[pl.BlockSpec((1, total, shard), lambda r: (r, 0, 0))],
        out_specs=[
            pl.BlockSpec((1, count * shard, width // replicas), lambda r: (1, 0, r)),
            pl.BlockSpec((1, shard, hidden // replicas), lambda r: (1, 0, r)),
            pl.BlockSpec((shard, 3 * width // replicas), lambda r: (0, r)),
        ],
        out_shape=[
            jax.ShapeDtypeStruct((2, count * shard, width), HIGH),
            jax.ShapeDtypeStruct((2, shard, hidden), HIGH),
            jax.ShapeDtypeStruct((shard, 3 * width), HIGH),
        ],
        cost_estimate=pl.CostEstimate(flops=0, bytes_accessed=6 * replicas * total * shard, transcendentals=0),
    )(part)


def turn_attn_kernel(edge, part_ref, qkv_ref, o_ref):
    turned = part_ref[0].astype(HIGH).T

    @pl.when(pl.program_id(0) < edge)
    def _():
        qkv_ref[...] = turned

    @pl.when(pl.program_id(0) >= edge)
    def _():
        o_ref[...] = turned


def turn_attn(part, width):
    replicas, total, shard = part.shape
    edge = 3 * width // total
    return pl.pallas_call(
        functools.partial(turn_attn_kernel, edge),
        grid=(replicas,),
        in_specs=[pl.BlockSpec((1, total, shard), lambda r: (r, 0, 0))],
        out_specs=[
            pl.BlockSpec((shard, total), lambda r: (0, jnp.minimum(r, edge - 1))),
            pl.BlockSpec((shard, total), lambda r: (0, jnp.maximum(r - edge, 0))),
        ],
        out_shape=[jax.ShapeDtypeStruct((shard, 3 * width), HIGH), jax.ShapeDtypeStruct((shard, width), HIGH)],
        cost_estimate=pl.CostEstimate(flops=0, bytes_accessed=6 * replicas * total * shard, transcendentals=0),
    )(part)


NORM_ROWS = 256


def normed_of(values, gain, shift):
    mean = jnp.mean(values, axis=-1, keepdims=True)
    centred = values - mean
    rstd = lax.rsqrt(jnp.mean(centred * centred, axis=-1, keepdims=True) + EPS)
    unit = centred * rstd
    return unit, rstd, unit * gain + shift


def norm_fwd_kernel(active, x_ref, gain_ref, shift_ref, out_ref):
    _, _, out = normed_of(x_ref[...].astype(HIGH), gain_ref[...], shift_ref[...])
    out_ref[...] = (jax.nn.silu(out) if active else out).astype(LOW)


def norm_fwd(values, gain, shift, active=False):
    rows, width = values.shape
    block = pl.BlockSpec((NORM_ROWS, width), lambda i: (i, 0))
    line = pl.BlockSpec((1, width), lambda i: (0, 0))
    return pl.pallas_call(
        functools.partial(norm_fwd_kernel, active),
        grid=(rows // NORM_ROWS,),
        in_specs=[block, line, line],
        out_specs=block,
        out_shape=jax.ShapeDtypeStruct((rows, width), LOW),
        cost_estimate=pl.CostEstimate(flops=10 * rows * width, bytes_accessed=6 * rows * width, transcendentals=0),
    )(values, gain[None], shift[None])


def norm_bwd_kernel(active, has_rest, scale, x_ref, grad_ref, gain_ref, shift_ref, *refs):
    rest_ref = refs[0] if has_rest else None
    out_ref, low_ref, sums_ref = refs[has_rest:]
    unit, rstd, out = normed_of(x_ref[...].astype(HIGH), gain_ref[...], shift_ref[...])
    grad = grad_ref[...].astype(HIGH)
    if active:
        gate = jax.nn.sigmoid(out)
        grad = grad * (gate * (1.0 + out * (1.0 - gate)))
    inner = grad * gain_ref[...]
    back = (inner - jnp.mean(inner, axis=-1, keepdims=True) - unit * jnp.mean(inner * unit, axis=-1, keepdims=True)) * rstd
    if has_rest:
        back = back + rest_ref[...]
    out_ref[...] = back
    scaled = back * scale
    low_ref[...] = scaled.astype(LOW)

    @pl.when(pl.program_id(0) == 0)
    def _():
        sums_ref[...] = jnp.zeros_like(sums_ref)

    sums_ref[0:1, :] += jnp.sum(grad * unit, axis=0, keepdims=True)
    sums_ref[1:2, :] += jnp.sum(grad, axis=0, keepdims=True)
    sums_ref[2:3, :] += jnp.sum(scaled, axis=0, keepdims=True)


def norm_bwd(values, grad, gain, shift, rest=None, scale=1.0, active=False):
    rows, width = values.shape
    block = pl.BlockSpec((NORM_ROWS, width), lambda i: (i, 0))
    line = pl.BlockSpec((1, width), lambda i: (0, 0))
    extra = [] if rest is None else [rest]
    return pl.pallas_call(
        functools.partial(norm_bwd_kernel, active, len(extra), scale),
        grid=(rows // NORM_ROWS,),
        in_specs=[block, block, line, line] + [block] * len(extra),
        out_specs=[block, block, pl.BlockSpec((8, width), lambda i: (0, 0))],
        out_shape=[
            jax.ShapeDtypeStruct((rows, width), HIGH),
            jax.ShapeDtypeStruct((rows, width), LOW),
            jax.ShapeDtypeStruct((8, width), HIGH),
        ],
        compiler_params=pltpu.CompilerParams(vmem_limit_bytes=32 * 1024 * 1024),
        cost_estimate=pl.CostEstimate(flops=30 * rows * width, bytes_accessed=18 * rows * width, transcendentals=0),
    )(values, grad, gain[None], shift[None], *extra)


def weight_grads_kernel(many, flipped, g_ref, last_ref, a_ref, b_ref, out_ref):
    step = pl.program_id(0)

    def product(grad, value):
        return (left_t(grad, value) if flipped else left_t(value, grad)).astype(LOW)

    @pl.when(step < many)
    def _():
        out_ref[...] = product(g_ref[...], a_ref[...])

    @pl.when(step == many)
    def _():
        out_ref[...] = product(last_ref[...], b_ref[...])


def weight_grads(grads, last, first_in, last_in, flipped):
    many, rows, width = grads.shape
    full = pl.BlockSpec((rows, width), lambda i: (0, 0))
    shape = ((many + 1) * width, width) if flipped else (width, (many + 1) * width)
    return pl.pallas_call(
        functools.partial(weight_grads_kernel, many, flipped),
        grid=(many + 1,),
        in_specs=[pl.BlockSpec((None, rows, width), lambda i: (jnp.minimum(i, many - 1), 0, 0)), full, full, full],
        out_specs=pl.BlockSpec((width, width), (lambda i: (i, 0)) if flipped else (lambda i: (0, i))),
        out_shape=jax.ShapeDtypeStruct(shape, LOW),
        compiler_params=pltpu.CompilerParams(vmem_limit_bytes=40 * 1024 * 1024),
        cost_estimate=pl.CostEstimate(
            flops=2 * (many + 1) * rows * width * width, bytes_accessed=4 * (many + 2) * rows * width, transcendentals=0
        ),
    )(grads, last, first_in, last_in)


def gather_weight(shard):
    pieces = lax.axis_size("rep") * lax.axis_size("seq")
    count = shard.shape[0] // pieces
    piece = lax.dynamic_slice_in_dim(shard, replica_index() * count, count, 0)
    return lax.all_gather(piece, ("fsdp",) + REPLICAS, axis=0, tiled=True)


def reduce_replicas(grad_t):
    return lax.psum_scatter(grad_t, REPLICAS, scatter_dimension=0, tiled=True)


def by_groups(part):
    groups = lax.axis_size("fsdp")
    columns, rows = part.shape
    return jnp.swapaxes(part.reshape(columns, groups, rows // groups), 0, 1)


def reduce_groups(part):
    return lax.psum_scatter(part, "fsdp", scatter_dimension=0, tiled=False)


def to_replicas(part):
    return lax.all_gather(part, REPLICAS, axis=0, tiled=False)


def swap_in(value):
    count = value.shape[0]
    rows = value.shape[1]
    me = lax.axis_index("seq")
    whole = jnp.zeros((count * rows,) + value.shape[2:], value.dtype)
    own = lax.dynamic_index_in_dim(value, me, 0, keepdims=False)
    whole = lax.dynamic_update_slice_in_dim(whole, own, me * rows, 0)
    for steps in range(1, count):
        sent = lax.dynamic_index_in_dim(value, (me + steps) % count, 0, keepdims=False)
        got = ring(sent, "seq", steps)
        whole = lax.dynamic_update_slice_in_dim(whole, got, ((me - steps) % count) * rows, 0)
    return whole


def swap_out(whole, count, kind, low=None):
    low = whole if low is None else low
    rows = whole.shape[0] // count
    me = lax.axis_index("seq")
    value = jnp.zeros((count, rows) + whole.shape[1:], kind)
    own = lax.dynamic_slice_in_dim(whole, me * rows, rows, 0)
    value = lax.dynamic_update_index_in_dim(value, own.astype(kind), me, 0)
    for steps in range(1, count):
        sent = lax.dynamic_slice_in_dim(low, ((me + steps) % count) * rows, rows, 0)
        got = ring(sent, "seq", steps)
        value = lax.dynamic_update_index_in_dim(value, got.astype(kind), (me - steps) % count, 0)
    return value


def pack_small(arrays, shard):
    gains, shifts, in_bias, out_bias, a_bias, embed, kernel = arrays
    flat = [x.reshape(-1) for x in (gains, shifts, in_bias, out_bias, a_bias, kernel, embed)]
    total = jnp.concatenate(flat)
    return jnp.pad(total, (0, -total.shape[0] % (16 * shard))).reshape(-1, shard)


def unpack_small(packed, shard):
    groups = packed.shape[0]
    wide = lambda lo, hi: jnp.swapaxes(packed[:, lo:hi], 0, 1).reshape(hi - lo, groups * shard)
    taken = 12
    gains, shifts = wide(0, 6), wide(6, 12)
    per = 4
    in_bias = jnp.swapaxes(packed[:, taken : taken + 2 * per].reshape(groups, 2, per * shard), 0, 1).reshape(2, -1)
    taken += 2 * per
    out_bias = wide(taken, taken + 2)
    a_bias = wide(taken + 2, taken + 5)
    kernel = wide(taken + 5, taken + 5 + KERNEL)
    taken += 5 + KERNEL
    buckets = LEFT + RIGHT + 1
    embed = packed[:, taken:].reshape(groups, -1)[:, : buckets * (HD // groups)].reshape(groups, buckets, HD // groups)
    return gains, shifts, in_bias, out_bias, a_bias, jnp.swapaxes(embed, 0, 1).reshape(buckets, HD), kernel


def split_small(whole, groups):
    gains, shifts, in_bias, out_bias, a_bias, embed, kernel = whole
    shard = gains.shape[1] // groups
    cut = lambda x: jnp.swapaxes(x.reshape(x.shape[0], groups, -1), 0, 1).reshape(groups, -1)
    flat = jnp.concatenate([cut(x) for x in (gains, shifts, in_bias, out_bias, a_bias, kernel, embed)], axis=1)
    flat = jnp.pad(flat, ((0, 0), (0, -flat.shape[1] % (16 * shard))))
    return flat.reshape(groups, -1, shard)


def unsplit_small(rows, shapes):
    flat = rows.reshape(-1)
    out, taken = [], 0
    for shape in shapes:
        size = shape[0] * shape[1]
        out.append(flat[taken : taken + size].reshape(shape))
        taken += size
    return out


def gather_small(value):
    groups, z = lax.axis_size("fsdp"), lax.axis_index("fsdp")
    parts = [value] + [ring(value, "fsdp", steps) for steps in range(1, groups)]
    turned = jnp.stack(parts[::-1] * 2)
    return lax.dynamic_slice_in_dim(turned, groups - 1 - z, groups, 0)


def reduce_planes(value):
    groups, z = lax.axis_size("fsdp"), lax.axis_index("fsdp")
    total = pick(value, z, 0)
    for steps in range(1, groups):
        total = total + ring(pick(value, (z + steps) % groups, 0), "fsdp", steps)
    return total


def sum_replicas(value):
    pieces = lax.axis_size("rep") * lax.axis_size("seq")
    terms = [value] + [across(value, flip) for flip in range(1, pieces)]
    while len(terms) > 1:
        terms = [a + b for a, b in zip(terms[::2], terms[1::2])]
    return terms[0]


def fast_body(inputs, cotangent, ln_gain, ln_bias, ffn_in, ffn_in_bias, ffn_out, ffn_out_bias, qkv_weight, attn_out, attn_bias, dist_embed, pw_in, depthwise, pw_out):
    micro, clips, rows, width = inputs.shape
    shard = ln_gain.shape[1]
    groups = lax.axis_size("fsdp")
    at = place()
    pieces = lax.axis_size("rep") * lax.axis_size("seq")
    small = pack_small((ln_gain, ln_bias, ffn_in_bias, ffn_out_bias, attn_bias, dist_embed, depthwise), shard)
    small = gather_small(small)
    start = swap_in(inputs.reshape(micro, rows, width))
    tie = lax.optimization_barrier
    piece, halves_in = tie((own_piece(ffn_out[0]), from_planes(own_piece(ffn_in[0]))))
    halves_out = from_planes(piece)
    near_in, halves_out, start, small = tie((around(halves_in), halves_out, start, small))
    f_in0 = assemble(at, ffn_in[0], both_cores(near_in))
    near_out = around(halves_out)
    w_attn = gather_weight(jnp.concatenate([qkv_weight, attn_out], axis=1))
    w_qkv, w_o = w_attn[:, : 3 * width], w_attn[:, 3 * width :]
    rest = gather_weight(jnp.concatenate([pw_in, pw_out, ffn_in[1]], axis=1))
    c_in, c_out, f_in1 = jnp.split(rest, [2 * width, 3 * width], axis=1)
    f_out1 = gather_weight(ffn_out[1])

    gains, shifts, f_in_b, f_out_b, a_bias, embed, kernel = unpack_small(small, shard)
    table, embed2 = bias_tables(embed)
    gains, shifts, f_in_b, f_out_b, a_bias, kernel = (x.astype(HIGH) for x in (gains, shifts, f_in_b, f_out_b, a_bias, kernel))

    def ffn_fwd(values, i, w_in, which, w_out):
        normed = norm_fwd(values, gains[which], shifts[which])
        linear = matmul(normed, w_in) + f_in_b[i]
        active, linear = tie((jax.nn.silu(linear).astype(LOW), linear.astype(LOW)))
        active, w_out = w_out(active)
        out = values.astype(HIGH) + 0.5 * (matmul(active, w_out) + f_out_b[i])
        return out, (values, normed, linear, active), w_out

    def late_weight(active):
        active_low, near = tie((active, near_out))
        return active_low, assemble(at, ffn_out[0], both_cores(near))

    def silu_bwd(grad, linear):
        gate = jax.nn.sigmoid(linear)
        return grad * (gate * (1.0 + linear * (1.0 - gate)))

    first, keep_one, f_out0 = ffn_fwd(start, 0, f_in0, 0, late_weight)
    n_two = norm_fwd(first, gains[1], shifts[1])
    proj_bias = jnp.concatenate([a_bias[0], jnp.zeros_like(a_bias[0]), a_bias[1]])
    proj = (matmul(n_two, w_qkv) + proj_bias).astype(LOW)
    mixed, lse = attn_forward_call(proj, table, width)
    second = first + matmul(mixed, w_o) + a_bias[2]
    n_three = norm_fwd(second, gains[2], shifts[2])
    pre = matmul(n_three, c_in)
    gated, pre = lax.optimization_barrier(((pre[:, :width] * jax.nn.sigmoid(pre[:, width:])).astype(LOW), pre.astype(LOW)))
    conv, cotangent = tie((conv_fwd_call(gated, kernel), cotangent))
    cot = swap_in(cotangent.reshape(micro, rows, width))
    z = norm_fwd(conv, gains[3], shifts[3], True)
    third = second + matmul(z, c_out)
    fourth, keep_four, _ = ffn_fwd(third, 1, f_in1, 4, lambda active: (active, f_out1))
    final = norm_fwd(fourth, gains[5], shifts[5])
    out_final = swap_out(final, micro, LOW)

    grad_fourth, grad_low, sums_five = norm_bwd(fourth, cot, gains[5], shifts[5], None, 0.5)
    tie = lax.optimization_barrier
    values, normed, linear, active = keep_four
    d_out1 = left_t(grad_low, active).astype(LOW)
    d_out1, grad_low = tie((d_out1, grad_low))
    p_out1 = reduce_replicas(d_out1)
    d_lin = silu_bwd(right_t(grad_low, f_out1), linear.astype(HIGH))
    d_in_b1 = jnp.sum(d_lin, axis=0)
    lin_low = tie(d_lin.astype(LOW))
    d_in1 = left_t(lin_low, normed).astype(LOW)
    lin_low, d_in1 = tie((lin_low, d_in1))
    p_in1 = reduce_replicas(d_in1)
    grad_third, grad_low, sums_four = norm_bwd(values, right_t(lin_low, f_in1), gains[4], shifts[4], grad_fourth)

    conv_low = grad_low
    grad_conv, _, sums_three = norm_bwd(conv, right_t(grad_low, c_out), gains[3], shifts[3], None, 1.0, True)
    g_pre, d_kernel = conv_bwd_call(grad_conv, gated, pre, kernel)
    d_conv = weight_grads(g_pre, conv_low, n_three, z, True)
    d_conv, g_pre, p_out1 = tie((d_conv, g_pre, p_out1))
    p_conv = reduce_replicas(d_conv)
    g_pre = jnp.concatenate([g_pre[0], g_pre[1]], axis=1)
    grad_second, grad_low, sums_two = norm_bwd(second, right_t(g_pre, c_in), gains[2], shifts[2], grad_third)

    attn_low = grad_low
    grad_mixed = right_t(grad_low, w_o).astype(LOW)
    g_proj, d_embed, d_bias = attn_backward_call(proj, mixed, lse, grad_mixed, table, embed2, width)
    d_embed = jnp.sum(d_embed.reshape(2, HD, width // 128, 128), axis=(0, 2)).T[: LEFT + RIGHT + 1]
    g_proj, p_out1, p_in1, p_conv = tie((g_proj, p_out1, p_in1, p_conv))
    strips = p_out1.reshape(p_out1.shape[0], groups, -1, width // groups).transpose(1, 2, 0, 3)
    early = jnp.concatenate([strips.reshape(groups, -1, width // groups), by_groups(p_in1), by_groups(p_conv)], axis=1)
    g_proj, early = tie((g_proj, early))
    early = reduce_groups(early)
    d_attn = weight_grads(g_proj, attn_low, n_two, mixed, True)
    d_attn, g_proj = tie((d_attn, g_proj))
    p_attn = reduce_replicas(d_attn)
    g_proj = jnp.concatenate([g_proj[0], g_proj[1], g_proj[2]], axis=1)
    grad_normed = right_t(g_proj, w_qkv)
    grad_first, grad_low, sums_one = norm_bwd(first, grad_normed, gains[1], shifts[1], grad_second, 0.5)

    values, normed, linear, active = keep_one
    d_out0 = left_t(active, grad_low).astype(LOW)
    d_out0, grad_low = tie((d_out0, grad_low))
    t_out0 = reduce_cores(at, d_out0)
    d_lin = silu_bwd(right_t(grad_low, f_out0), linear.astype(HIGH))
    d_in_b0 = jnp.sum(d_lin, axis=0)
    lin_low, t_out0, early, out_final = tie((d_lin.astype(LOW), t_out0, early, out_final))
    early = to_replicas(early)
    t_out0 = reduce_first(at, t_out0)
    d_in0 = left_t(normed, lin_low).astype(LOW)
    d_in0, lin_low, t_out0 = tie((d_in0, lin_low, t_out0))
    t_out0 = reduce_second(at, t_out0)
    t_in0 = reduce_cores(at, d_in0)
    grad_normed = right_t(lin_low, f_in0)
    grad_normed, t_out0, t_in0 = tie((grad_normed, t_out0, t_in0))
    t_out0 = reduce_along(at, t_out0)
    t_in0 = reduce_first(at, t_in0)
    grad_start, start_low, sums_zero = norm_bwd(values, grad_normed, gains[0], shifts[0], grad_first)
    start_low, t_out0, t_in0, p_attn = tie((start_low, t_out0, t_in0, p_attn))
    attn = to_replicas(reduce_groups(by_groups(p_attn)))

    sums = [sums_zero, sums_one, sums_two, sums_three, sums_four, sums_five]
    small = split_small(
        (
            jnp.stack([x[0] for x in sums]),
            jnp.stack([x[1] for x in sums]),
            jnp.stack([d_in_b0, d_in_b1]),
            jnp.stack([sums_one[2], sums_five[2]]),
            jnp.stack([d_bias[0], d_bias[1], sums_two[2]]),
            d_embed,
            d_kernel,
        ),
        groups,
    )
    near = spread_plane(t_out0)
    t_in0 = reduce_second(at, t_in0)
    near, t_in0, start_low, small = tie((near, t_in0, start_low, small))
    t_in0 = reduce_along(at, t_in0)
    small = reduce_planes(small)
    grad_start = swap_out(grad_start, micro, HIGH, start_low)
    far = across(near, CORE)
    near, far, t_in0, small = tie((near, far, t_in0, small))
    near_in = spread_plane(t_in0)
    small = sum_replicas(small)
    grad_out, grad_in, g_conv = turn_early(early, width, lin_low.shape[1])
    grad_out = finish_first(at, near, far, grad_out)
    grad_in = finish_first(at, near_in, across(near_in, CORE), grad_in)
    g_qkv, g_o = turn_attn(attn, width)
    shapes = [(6, shard), (6, shard), (2, 4 * shard), (2, shard), (3, shard), (KERNEL, shard), (LEFT + RIGHT + 1, HD // groups)]
    s_gain, s_shift, s_in_b, s_out_b, s_a, s_kernel, s_embed = unsplit_small(small, shapes)
    return (
        out_final.reshape(micro, clips, rows, width),
        grad_start.reshape(micro, clips, rows, width),
        s_gain,
        s_shift,
        grad_in,
        s_in_b,
        grad_out,
        s_out_b,
        g_qkv,
        g_o,
        s_a,
        s_embed,
        g_conv[:, : 2 * width],
        s_kernel,
        g_conv[:, 2 * width :],
    )


def body(inputs, *rest):
    micro, clips, _, width = inputs.shape
    if (lax.axis_size("seq"), lax.axis_size("rep"), micro, clips) == (2, 4, 2, 1):
        return fast_body(inputs, *rest)
    return general_body(inputs, *rest)


def solution(mesh):
    return jax.shard_map(
        body,
        mesh=mesh,
        in_specs=(
            P(None, ("rep", "fsdp"), "seq", None),
            P(None, ("rep", "fsdp"), "seq", None),
            P(None, "fsdp"),
            P(None, "fsdp"),
            P(None, "fsdp", None),
            P(None, "fsdp"),
            P(None, "fsdp", None),
            P(None, "fsdp"),
            P("fsdp", None),
            P("fsdp", None),
            P(None, "fsdp"),
            P(None, "fsdp"),
            P("fsdp", None),
            P(None, "fsdp"),
            P("fsdp", None),
        ),
        out_specs=(
            P(None, ("rep", "fsdp"), "seq", None),
            P(None, ("rep", "fsdp"), "seq", None),
            P(None, "fsdp"),
            P(None, "fsdp"),
            P(None, "fsdp", None),
            P(None, "fsdp"),
            P(None, "fsdp", None),
            P(None, "fsdp"),
            P("fsdp", None),
            P("fsdp", None),
            P(None, "fsdp"),
            P(None, "fsdp"),
            P("fsdp", None),
            P(None, "fsdp"),
            P("fsdp", None),
        ),
        check_vma=False,
    )
```
